32 devices in a mesh: gx: 16 (over z, y, core), gz: 2 (over x).
Axes of the slice: x: 2, y: 2, z: 4, core: 2. Of those that a mesh axis runs over, the one named last changes fastest.
Arguments:
- e_init: float32 [3, 512, 16, 256], P(None, 'gx', None, 'gz'), may hold values from -6 to 6
- h_init: float32 [3, 512, 16, 256], P(None, 'gx', None, 'gz'), may hold values from -6 to 6
- material: int32 [512, 16, 256], P('gx', None, 'gz'), may hold values from 0 to 15
- eps_table: float32 [16], replicated, may hold values from 1 to 12
- sigma_table: float32 [16], replicated, may hold values from 0.05 to 2
- face_cells: int32 [32, 128], P(('gx', 'gz')), may hold values from -1 to 65535, as said below
- owner_table: int32 [32], replicated, may hold values from 0 to 31, each once
Outputs:
- e_field: float32 [3, 512, 16, 256], P(None, 'gx', None, 'gz')
- h_field: float32 [3, 512, 16, 256], P(None, 'gx', None, 'gz')
- far_field: float32 [32, 4, 12, 128], P(('gx', 'gz'))
The draws below stay inside these ranges and needn't reach their ends.
Inputs may be any that keep to these rules, and one draw needn't show every extreme that they name: `face_cells`: within a tile the used entries are distinct and come first, the rest are -1; each tile uses between 64 and 128 slots, and some tile uses all of them. `owner_table`: every tile owns exactly one angle block.
All inputs are finite; a program needn't handle non-finite values.
Results may differ from the reference program's by a relative error of at most 0.0003.
Values sent between devices are 32-bit elements; how exact they have to be, the bound alone decides.
No kernel may reach another device: no remote copies, remote signals or barrier semaphores. Data moves between devices by JAX's collectives and lax.ppermute only.
A program may use at most 192 MiB of HBM per device.

```python
import math
import jax
import jax.numpy as jnp
from jax import lax

CX = 32
CY = 16
CZ = 128
SLOTS = 128
STEPS = 4
ANGLES = 4096
NPHI = 64
FREQS = 4
MATS = 16
NX = 512
NY = 16
NZ = 256
TILES = 32
CELLS = 65536
ANG_BLK = 128
N_GZ = 2


def draw_face_cells(key, part):
    key_count, key_full, key_stride, key_offset = jax.random.split(key, 4)
    tile = jnp.arange(TILES, dtype=jnp.int32)
    counts = jax.random.randint(key_count, (TILES,), SLOTS // 2, SLOTS + 1)
    full = jax.random.randint(key_full, (), 0, TILES)
    counts = jnp.where(tile == full, SLOTS, counts)
    stride = 6 * jax.random.randint(key_stride, (TILES,), 0, CELLS // 6 + 1) + 1
    offset = jax.random.randint(key_offset, (TILES,), 0, CELLS)
    offset = jnp.where(tile == full, CELLS - 1, offset)
    slot = jnp.arange(SLOTS, dtype=jnp.int32)
    cells = (offset[:, None] + slot[None, :] * stride[:, None]) % CELLS
    return jnp.where(slot[None, :] < counts[:, None], cells, -1).astype(jnp.int32)


def place_ends(result, stream_key, smallest, high):
    spot = [jax.random.randint(jax.random.fold_in(stream_key, axis), (), 0, length) for axis, length in enumerate(result.shape)]
    longest = result.shape.index(max(result.shape))
    next_to = spot[:longest] + [(spot[longest] + 1) % result.shape[longest]] + spot[longest + 1:]
    return result.at[tuple(spot)].set(smallest).at[tuple(next_to)].set(high)


def level_of(stream_key, dims, cuts, smallest, high):
    gain, own = 1.0, jax.random.fold_in(stream_key, 6)
    for dim, shards_of in cuts:
        steps = jnp.exp(jax.random.uniform(jax.random.fold_in(own, dim), (shards_of,), jnp.float32, smallest / len(cuts), high / len(cuts)))
        gain = gain * jnp.repeat(steps, dims[dim] // shards_of).reshape([-1 if axis == dim else 1 for axis in range(len(dims))])
    return gain


def scatter_about(own_key, shape, spread, most, pieces=(), held_as=jnp.bfloat16):
    values = spread * jax.random.normal(own_key, shape, jnp.float32)
    if pieces:
        values = values * level_of(own_key, shape, pieces, -0.22, 0.18)
    return jnp.clip(values, -most, most).astype(held_as)


def setup_inputs(seed: int = 0) -> dict:
    streams_of = jax.random.split(jax.random.key(seed), 8)
    e_init = scatter_about(streams_of[0], (3, NX, NY, NZ), 1.0, 6.0, ((1, 16), (3, 2)), jnp.float32)
    h_init = scatter_about(streams_of[1], (3, NX, NY, NZ), 1.0, 6.0, ((1, 16), (3, 2)), jnp.float32)
    material = place_ends(jax.random.randint(streams_of[2], (NX, NY, NZ), 0, MATS), jax.random.fold_in(streams_of[2], 1), 0, MATS - 1).astype(jnp.int32)
    eps_table = jnp.clip(jnp.exp(jax.random.uniform(streams_of[3], (MATS,), jnp.float32, math.log(1.0), math.log(12.0))), 1.0, 12.0)
    sigma_table = jnp.clip(jnp.exp(jax.random.uniform(streams_of[4], (MATS,), jnp.float32, math.log(0.05), math.log(2.0))), 0.05, 2.0)
    face_cells = draw_face_cells(jax.random.fold_in(streams_of[7], 71), 0)
    owner_table = jax.random.permutation(streams_of[6], TILES).astype(jnp.int32)
    return {"e_init": e_init, "h_init": h_init, "material": material, "eps_table": eps_table, "sigma_table": sigma_table, "face_cells": face_cells, "owner_table": owner_table}


DT = 0.5

def forward(field, axis):
    count = field.shape[axis]
    after = lax.slice_in_dim(field, 1, count, axis=axis)
    edge = jnp.zeros_like(lax.slice_in_dim(field, 0, 1, axis=axis))
    return jnp.concatenate([after, edge], axis=axis) - field

def backward(field, axis):
    count = field.shape[axis]
    before = lax.slice_in_dim(field, 0, count - 1, axis=axis)
    edge = jnp.zeros_like(lax.slice_in_dim(field, 0, 1, axis=axis))
    return field - jnp.concatenate([edge, before], axis=axis)

def directions(angle):
    theta = math.pi * ((angle // NPHI).astype(jnp.float32) + 0.5) / (ANGLES // NPHI)
    phi = 2.0 * math.pi * (angle % NPHI).astype(jnp.float32) / NPHI
    return (jnp.sin(theta) * jnp.cos(phi), jnp.sin(theta) * jnp.sin(phi), jnp.cos(theta))

def project(acc_re, acc_im, pos_x, pos_y, pos_z, angle, omegas):
    dir_x, dir_y, dir_z = directions(angle)
    geometry = dir_x[:, None] * pos_x[None] + dir_y[:, None] * pos_y[None] + dir_z[:, None] * pos_z[None]
    phase = omegas[:, None, None] * geometry[None]
    cosine = jnp.cos(phase)
    sine = jnp.sin(phase)
    high = lax.Precision.HIGHEST
    real = jnp.einsum('fas,fcs->fca', cosine, acc_re, precision=high) - jnp.einsum('fas,fcs->fca', sine, acc_im, precision=high)
    imag = jnp.einsum('fas,fcs->fca', sine, acc_re, precision=high) + jnp.einsum('fas,fcs->fca', cosine, acc_im, precision=high)
    return jnp.concatenate([real, imag], axis=1)

def reference(e_init, h_init, material, eps_table, sigma_table, face_cells, owner_table):
    eps_cell = eps_table[material]
    sigma_cell = sigma_table[material]
    loss = sigma_cell * DT / (2.0 * eps_cell)
    coef_a = (1.0 - loss) / (1.0 + loss)
    coef_b = DT / (eps_cell * (1.0 + loss))
    e_x, e_y, e_z = (e_init[0], e_init[1], e_init[2])
    h_x, h_y, h_z = (h_init[0], h_init[1], h_init[2])
    valid = (face_cells >= 0).astype(jnp.float32).reshape(-1)
    local = jnp.maximum(face_cells, 0)
    tile = jnp.arange(TILES, dtype=jnp.int32)[:, None]
    glob_x = (tile // N_GZ * CX + local // (CY * CZ)).reshape(-1)
    glob_y = (local // CZ % CY).reshape(-1)
    glob_z = (tile % N_GZ * CZ + local % CZ).reshape(-1)
    omegas = 0.4 * (jnp.arange(FREQS, dtype=jnp.float32) + 1.0)
    total = TILES * SLOTS
    acc_re = jnp.zeros((FREQS, 6, total), jnp.float32)
    acc_im = jnp.zeros((FREQS, 6, total), jnp.float32)
    for step in range(STEPS):
        h_x = h_x - DT * (forward(e_z, 1) - forward(e_y, 2))
        h_y = h_y - DT * (forward(e_x, 2) - forward(e_z, 0))
        h_z = h_z - DT * (forward(e_y, 0) - forward(e_x, 1))
        e_x = coef_a * e_x + coef_b * (backward(h_z, 1) - backward(h_y, 2))
        e_y = coef_a * e_y + coef_b * (backward(h_x, 2) - backward(h_z, 0))
        e_z = coef_a * e_z + coef_b * (backward(h_y, 0) - backward(h_x, 1))
        sample = jnp.stack([comp[glob_x, glob_y, glob_z] for comp in (e_x, e_y, e_z, h_x, h_y, h_z)]) * valid[None]
        phase = omegas * (DT * (step + 1))
        acc_re = acc_re + jnp.cos(phase)[:, None, None] * sample[None]
        acc_im = acc_im + jnp.sin(phase)[:, None, None] * sample[None]
    pos_x = glob_x.astype(jnp.float32) + (0.5 - NX / 2)
    pos_y = glob_y.astype(jnp.float32) + (0.5 - NY / 2)
    pos_z = glob_z.astype(jnp.float32) + (0.5 - NZ / 2)
    cycles = ANGLES // NPHI

    def cycle(index):
        angle = index * NPHI + jnp.arange(NPHI, dtype=jnp.int32)
        return project(acc_re, acc_im, pos_x, pos_y, pos_z, angle, omegas)
    pattern = lax.map(cycle, jnp.arange(cycles, dtype=jnp.int32))
    pattern = jnp.transpose(pattern, (1, 2, 0, 3)).reshape(FREQS, 12, ANGLES)
    blocks = jnp.transpose(pattern.reshape(FREQS, 12, TILES, ANG_BLK), (2, 0, 1, 3))
    far = jnp.zeros_like(blocks).at[owner_table].set(blocks)
    far = far * (1.0 / math.sqrt(TILES * SLOTS * STEPS))
    e_field = jnp.stack([e_x, e_y, e_z])
    h_field = jnp.stack([h_x, h_y, h_z])
    return (e_field, h_field, far)
```

```python
import functools
import math

import jax
import jax.numpy as jnp
from jax import lax
from jax.experimental import pallas as pl
from jax.experimental.pallas import tpu as pltpu
from jax.sharding import PartitionSpec as P

STEPS = 4
ANGLES = 4096
NPHI = 64
FREQS = 4
DT = 0.5

W = 4
LANES = 128
F32 = jnp.float32
BF16 = jnp.bfloat16


def roll(v, shift, axis):
    return pltpu.roll(v, shift, axis)


def iota(shape, axis):
    return lax.broadcasted_iota(jnp.int32, shape, axis)


def pack_kernel(ns, e_ref, h_ref, m_ref, xa_ref, xb_ref, zp_ref):
    size_x, size_y = m_ref.shape[0], m_ref.shape[1]
    gx, gz = lax.axis_index("gx"), lax.axis_index("gz")
    odd = gx % 2
    off_a = jnp.where(odd == 0, size_x - W, 0)
    off_b = jnp.where(odd == 0, 0, size_x - W)
    for ref, off in ((xa_ref, off_a), (xb_ref, off_b)):
        for c in range(3):
            ref[c * W : (c + 1) * W] = e_ref[c, pl.ds(off, W)]
            ref[(3 + c) * W : (4 + c) * W] = h_ref[c, pl.ds(off, W)]
        ref[6 * W : 7 * W] = m_ref[pl.ds(off, W)].astype(F32)
    lane = iota((size_y, LANES), 1)
    group = lane // 8
    for s in range(ns):
        up = (gz + s) % 2 == 0
        shift_in = jnp.where(up, 124, 4)
        base = jnp.where(up, 8, 0)
        own = jnp.where(up, lane, 127 - lane) >= 124
        for q in range(2):
            acc = [jnp.zeros((size_y, LANES), F32) for _ in range(4)]
            for g in range(16):
                x = (q * 16 + g - W) % 32
                comps = [e_ref[c, x] for c in range(3)] + [h_ref[c, x] for c in range(3)]
                comps.append(m_ref[x].astype(F32))
                comps.append(comps[6])
                for i in range(4):
                    cell = jnp.where(own, comps[2 * i + 1], roll(comps[2 * i], shift_in, 1))
                    cell = roll(cell, (base + 8 * g) % LANES, 1)
                    acc[i] = jnp.where(group == g, cell, acc[i])
            for i in range(4):
                zp_ref[s, q * 4 + i] = acc[i]
                if q == 0:
                    xa_ref[7 * W + 4 * s + i] = acc[i]
                    xb_ref[7 * W + 4 * s + i] = acc[i]


def coef_tables(eps_ref, sigma_ref, shape):
    lane = iota(shape, 1)
    eps = jnp.ones(shape, F32)
    sigma = jnp.zeros(shape, F32)
    for i in range(eps_ref.shape[1]):
        eps = jnp.where(lane == i, eps_ref[0, i], eps)
        sigma = jnp.where(lane == i, sigma_ref[0, i], sigma)
    loss = sigma * DT / (2.0 * eps)
    return (1.0 - loss) / (1.0 + loss), DT / (eps * (1.0 + loss))


def pick(table, index):
    return jnp.take_along_axis(table, index, axis=1, mode="promise_in_bounds")


def field_kernel(
    ns,
    nx,
    nz,
    e_ref,
    h_ref,
    m_ref,
    xa_ref,
    xb_ref,
    zp_ref,
    zr_ref,
    za_ref,
    zb_ref,
    eps_ref,
    sigma_ref,
    cells_ref,
    cellv_ref,
    eo_ref,
    ho_ref,
    so_ref,
    st_ref,
    co_ref,
    in_ref,
):
    size_x, size_y = m_ref.shape[0], m_ref.shape[1]
    wide = size_x + 2 * W
    span = wide * size_y
    shape = (size_y, LANES)
    gx, gz = lax.axis_index("gx"), lax.axis_index("gz")
    odd = gx % 2
    lower = gx > 0
    upper = gx < nx - 1
    lane = iota(shape, 1)
    row = iota(shape, 0)
    ca_t, cb_t = coef_tables(eps_ref, sigma_ref, shape)

    def at(t, c, x):
        return pl.ds(((t * 8 + c) * wide + x) * size_y, size_y)

    def coef_at(c, x):
        return pl.ds((c * wide + x) * size_y, size_y)

    def own_plane(x, _):
        for c in range(3):
            st_ref[at(0, c, x + W)] = e_ref[c, x]
            st_ref[at(0, 3 + c, x + W)] = h_ref[c, x]
        index = m_ref[x]
        co_ref[coef_at(0, x + W)] = pick(ca_t, index)
        co_ref[coef_at(1, x + W)] = pick(cb_t, index)
        return 0

    lax.fori_loop(0, size_x, own_plane, 0, unroll=4)
    pos_a = jnp.where(odd == 0, size_x + W, 0)
    pos_b = jnp.where(odd == 0, 0, size_x + W)
    ok_b = jnp.where(odd == 0, lower, upper).astype(F32)
    for ref, pos, ok in ((xa_ref, pos_a, None), (xb_ref, pos_b, ok_b)):
        for j in range(W):
            for c in range(6):
                st_ref[at(0, c, pos + j)] = ref[c * W + j]
            index = ref[6 * W + j].astype(jnp.int32)
            ca, cb = pick(ca_t, index), pick(cb_t, index)
            if ok is not None:
                ca, cb = ca * ok, cb * ok
            co_ref[coef_at(0, pos + j)] = ca
            co_ref[coef_at(1, pos + j)] = cb

    group = lane // 8
    first_half = lane % 8 < 4
    fy_keep = row < size_y - 1
    by_keep = row > 0

    def fwd_y(v):
        return jnp.where(fy_keep, roll(v, size_y - 1, 0), 0.0)

    def bwd_y(v):
        return jnp.where(by_keep, roll(v, 1, 0), 0.0)

    for s in range(ns):
        up = (gz + s) % 2 == 0
        partner = jnp.where(up, gz + 1, gz - 1)
        ok = jnp.logical_and(partner >= 0, partner < nz)
        give_e = jnp.where(jnp.logical_and(up, ok), 1.0, 0.0)
        give_h = jnp.where(jnp.logical_and(jnp.logical_not(up), ok), 1.0, 0.0)

        def whole(mine, other, c):
            lo = jnp.where(up, mine, other)
            hi = jnp.where(up, other, mine)
            if c % 2 == 0:
                return jnp.where(first_half, lo, hi)
            return jnp.where(first_half, roll(lo, 124, 1), roll(hi, 4, 1))

        strip = []
        for c in range(7):
            i = c // 2
            q0 = whole(zp_ref[s, i], zr_ref[s, i], c)
            q1 = whole(zp_ref[s, 4 + i], zr_ref[s, 4 + i], c)
            qa = whole(xa_ref[7 * W + 4 * s + i], za_ref[s, i], c)
            qb = whole(xb_ref[7 * W + 4 * s + i], zb_ref[s, i], c)
            below = jnp.where(odd == 0, qb, qa)
            above = jnp.where(odd == 0, qa, qb)
            strip.append(
                [jnp.where(group < W, below, q0), q1, jnp.where(group < W, q0, above)]
            )
        inside = [
            jnp.where(jnp.logical_and(group < W, jnp.logical_not(lower)), 0.0, 1.0),
            jnp.ones(shape, F32),
            jnp.where(jnp.logical_and(group >= W, jnp.logical_not(upper)), 0.0, 1.0),
        ]
        mats = [v.astype(jnp.int32) for v in strip[6]]
        ca_s = [pick(ca_t, v) * k for v, k in zip(mats, inside)]
        cb_s = [pick(cb_t, v) * k for v, k in zip(mats, inside)]
        dt_s = [DT * k for k in inside]
        ex, ey, ez, hx, hy, hz = strip[:6]

        def fwd_x(v):
            r = [roll(u, 120, 1) for u in v]
            return [jnp.where(lane < 120, r[0], r[1]), jnp.where(lane < 120, r[1], r[2]), r[2]]

        def bwd_x(v):
            r = [roll(u, 8, 1) for u in v]
            return [r[0], jnp.where(lane >= 8, r[1], r[0]), jnp.where(lane >= 8, r[2], r[1])]

        def each(f, *vs):
            return [f(*u) for u in zip(*vs)]

        def fwd_z(v):
            return roll(v, 127, 1)

        def bwd_z(v):
            return roll(v, 1, 1)

        for t in range(STEPS):
            for j, (v, give) in enumerate(((ex, give_e), (ey, give_e))):
                for q in range(3):
                    dst = pl.ds(((t * 4 + j) * 3 + q) * size_y, size_y)
                    add = v[q] * give
                    in_ref[dst] = add if s == 0 else in_ref[dst] + add
            ez_x, ey_x = fwd_x(ez), fwd_x(ey)
            hx = each(
                lambda h, z, y, d: h - d * ((fwd_y(z) - z) - (fwd_z(y) - y)), hx, ez, ey, dt_s
            )
            hy = each(
                lambda h, x, z, zx, d: h - d * ((fwd_z(x) - x) - (zx - z)), hy, ex, ez, ez_x, dt_s
            )
            hz = each(
                lambda h, y, yx, x, d: h - d * ((yx - y) - (fwd_y(x) - x)), hz, ey, ey_x, ex, dt_s
            )
            hz_x, hy_x = bwd_x(hz), bwd_x(hy)
            ex = each(
                lambda e, z, y, a, b: a * e + b * ((z - bwd_y(z)) - (y - bwd_z(y))),
                ex, hz, hy, ca_s, cb_s,
            )
            ey = each(
                lambda e, x, z, zx, a, b: a * e + b * ((x - bwd_z(x)) - (z - zx)),
                ey, hx, hz, hz_x, ca_s, cb_s,
            )
            ez = each(
                lambda e, y, yx, x, a, b: a * e + b * ((y - yx) - (x - bwd_y(x))),
                ez, hy, hy_x, hx, ca_s, cb_s,
            )
            for j, (v, give) in enumerate(((hx, give_h), (hy, give_h))):
                for q in range(3):
                    dst = pl.ds(((t * 4 + 2 + j) * 3 + q) * size_y, size_y)
                    add = v[q] * give
                    in_ref[dst] = add if s == 0 else in_ref[dst] + add

    dt_lo = jnp.where(lower, DT, 0.0)
    dt_hi = jnp.where(upper, DT, 0.0)

    def side(t, j, x, target):
        src = pl.ds(((t - 1) * 12 + j * 3 + x // 16) * size_y, size_y)
        return roll(in_ref[src], (target - 8 * (x % 16)) % LANES, 1)

    def update(t, x, carry, with_e, store_out):
        ex, ey, ez, hy_p, hz_p = carry
        exn, eyn, ezn = (st_ref[at(t - 1, c, x + 1)] for c in range(3))
        dt = jnp.where(x < W, dt_lo, jnp.where(x >= size_x + W, dt_hi, DT))
        ex_z = jnp.where(lane == 127, side(t, 0, x, 123), roll(ex, 127, 1))
        ey_z = jnp.where(lane == 127, side(t, 1, x, 123), roll(ey, 127, 1))
        hx = st_ref[at(t - 1, 3, x)] - dt * ((fwd_y(ez) - ez) - (ey_z - ey))
        hy = st_ref[at(t - 1, 4, x)] - dt * ((ex_z - ex) - (ezn - ez))
        hz = st_ref[at(t - 1, 5, x)] - dt * ((eyn - ey) - (fwd_y(ex) - ex))
        st_ref[at(t, 3, x)] = hx
        st_ref[at(t, 4, x)] = hy
        st_ref[at(t, 5, x)] = hz
        if with_e:
            ca, cb = co_ref[coef_at(0, x)], co_ref[coef_at(1, x)]
            hx_z = jnp.where(lane == 0, side(t, 2, x, 125), roll(hx, 1, 1))
            hy_z = jnp.where(lane == 0, side(t, 3, x, 125), roll(hy, 1, 1))
            ex = ca * ex + cb * ((hz - bwd_y(hz)) - (hy - hy_z))
            ey = ca * ey + cb * ((hx - hx_z) - (hz - hz_p))
            ez = ca * ez + cb * ((hy - hy_p) - (hx - bwd_y(hx)))
            st_ref[at(t, 0, x)] = ex
            st_ref[at(t, 1, x)] = ey
            st_ref[at(t, 2, x)] = ez
            if store_out:
                eo_ref[0, x - W] = ex
                eo_ref[1, x - W] = ey
                eo_ref[2, x - W] = ez
                ho_ref[0, x - W] = hx
                ho_ref[1, x - W] = hy
                ho_ref[2, x - W] = hz
        return exn, eyn, ezn, hy, hz

    for t in range(1, STEPS + 1):
        first = t - 1
        start = tuple(st_ref[at(t - 1, c, first)] for c in range(3))
        zero = jnp.zeros(shape, F32)
        carry = update(t, first, start + (zero, zero), False, False)
        lax.fori_loop(
            t,
            wide - t,
            lambda x, c, t=t: update(t, x, c, True, t == STEPS),
            carry,
            unroll=2,
        )

    lane8 = iota((8, LANES), 1)
    row8 = iota((8, LANES), 0)

    def slot(m, accs):
        cell = cells_ref[0, m]
        used = cell >= 0
        cell = jnp.maximum(cell, 0)
        line = cell // LANES
        shift = (m - cell) % LANES
        here = lane8 == jnp.where(used, m, -1)
        out = []
        for t in range(STEPS):
            start = (t + 1) * 8 * span + W * size_y + line
            v = st_ref[pl.ds(start, 8, stride=span), :]
            out.append(jnp.where(here, roll(v, shift, 1), accs[t]))
        return tuple(out)

    zero8 = jnp.zeros((8, LANES), F32)
    accs = lax.fori_loop(0, LANES, slot, (zero8,) * STEPS, unroll=4)
    for t in range(STEPS):
        extra = cellv_ref[...].astype(F32) if t == 0 else zero8
        so_ref[t * 8 : t * 8 + 8] = jnp.where(row8 < 6, accs[t], extra)


SIN_C = (1.0, -1.0 / 6, 1.0 / 120, -1.0 / 5040, 1.0 / 362880, -1.0 / 39916800)
COS_C = (1.0, -0.5, 1.0 / 24, -1.0 / 720, 1.0 / 40320, -1.0 / 3628800, 1.0 / 479001600)


def sincos(turns):
    r = turns - jnp.round(turns)
    w = r * math.pi
    w2 = w * w
    s = jnp.full_like(w, SIN_C[-1])
    for k in SIN_C[-2::-1]:
        s = s * w2 + k
    s = s * w
    c = jnp.full_like(w, COS_C[-1])
    for k in COS_C[-2::-1]:
        c = c * w2 + k
    twice = 2.0 * s
    return twice * c, 1.0 - twice * s


def multiples(s, c):
    c2, s2 = 2.0 * c * c - 1.0, 2.0 * s * c
    c3, s3 = c2 * c - s2 * s, s2 * c + c2 * s
    c4, s4 = 2.0 * c2 * c2 - 1.0, 2.0 * s2 * c2
    return ((s, c), (s2, c2), (s3, c3), (s4, c4))


def split(v):
    hi = v.astype(BF16)
    return hi, (v - hi.astype(F32)).astype(BF16)


def project_kernel(
    size_x, size_y, size_z, tiles_x, tiles_z, own_ref, r1_ref, r2_ref, r3_ref, owner_ref, out_ref,
    inv_ref, th_ref, tl_ref, ah_ref, al_ref,
):
    gx, gz = lax.axis_index("gx"), lax.axis_index("gz")
    tiles = tiles_x * tiles_z
    base = 0.4 / (2.0 * math.pi)

    def put(b, _):
        inv_ref[owner_ref[b]] = b
        return 0

    lax.fori_loop(0, tiles, put, 0)
    blocks = [inv_ref[(gx ^ (4 * d)) * tiles_z + gz] for d in range(4)]

    refs = [own_ref, r1_ref, r2_ref, r3_ref]
    gx_of = [gx, gx ^ 2, gx, gx ^ 2]
    gz_of = [gz, gz, 1 - gz, 1 - gz]
    row16 = iota((16, LANES), 0)
    lane = iota((1, LANES), 1)
    lane16 = iota((16, LANES), 1)

    def split3(v):
        a = v.astype(BF16).astype(F32)
        b = (v - a).astype(BF16).astype(F32)
        return a, b, v - a - b

    dirs = []
    for q in range(2):
        block = jnp.where(lane16 < 64, blocks[2 * q], blocks[2 * q + 1])
        polar = 2 * block + (lane16 % 64) // 32
        st, ct = sincos((polar.astype(F32) + 0.5) * (0.5 / (ANGLES // NPHI)))
        sp, cp = sincos((lane16 % 32).astype(F32) * (1.0 / NPHI))
        ux = split3(base * st * cp)
        uy = split3(base * st * sp)
        mat = jnp.zeros((16, LANES), F32)
        for k in range(9):
            src = ux[k % 3] if k < 6 else uy[k % 3]
            mat = jnp.where(row16 == k, src, mat)
        dirs.append(mat.astype(BF16))
    row8 = iota((8, LANES), 0)
    combo = jnp.zeros((8, LANES), jnp.int32)
    for d in range(4):
        combo = jnp.where(row8 // 2 == d, 2 * blocks[d] + row8 % 2, combo)
    _, uz = sincos((combo.astype(F32) + 0.5) * (0.5 / (ANGLES // NPHI)))
    uz = uz * base

    steps = [[(math.cos(0.4 * (f + 1) * DT * (t + 1)), math.sin(0.4 * (f + 1) * DT * (t + 1)))
              for t in range(STEPS)] for f in range(FREQS)]

    for n in range(8):
        ref, core = refs[n // 2], n % 2
        tile_x = gx_of[n // 2] ^ core
        tile_z = gz_of[n // 2]
        rows = [ref[core, t * 8 : t * 8 + 8] for t in range(STEPS)]
        cell = jnp.maximum(rows[0][6:7], 0.0).astype(jnp.int32)
        pz = (cell % size_z + tile_z * size_z).astype(F32) + (0.5 - size_z * tiles_z / 2)
        zs = multiples(*sincos(uz * pz))
        for f in range(FREQS):
            re = sum(steps[f][t][0] * rows[t] for t in range(STEPS))
            im = sum(steps[f][t][1] * rows[t] for t in range(STEPS))
            zsin, zcos = zs[f]
            for k in range(8):
                sk, ck = zsin[k : k + 1], zcos[k : k + 1]
                both = jnp.concatenate([re * ck - im * sk, re * sk + im * ck], axis=0)
                hi, lo = split(both)
                q, kk = k // 4, k % 4
                ah_ref[f * 2 + q, kk * 16 : kk * 16 + 16, n * LANES : (n + 1) * LANES] = hi
                ah_ref[f * 2 + q, 64 + kk * 16 : 80 + kk * 16, n * LANES : (n + 1) * LANES] = lo

    for q in range(2):
        for n in range(8):
            ref, core = refs[n // 2], n % 2
            tile_x = gx_of[n // 2] ^ core
            cell = jnp.maximum(ref[core, 6:7], 0.0).astype(jnp.int32)
            gxi = cell // (size_y * size_z) + tile_x * size_x - size_x * tiles_x // 2
            high = ((gxi >> 4) << 4).astype(F32)
            low = (gxi & 15).astype(F32) + 0.5
            py = ((cell // size_z) % size_y).astype(F32) + (0.5 - size_y / 2)
            pos = jnp.where(row16 < 3, high, jnp.where(row16 < 6, low, jnp.where(row16 < 9, py, 0.0)))
            phase = lax.dot_general(
                pos.astype(BF16), dirs[q], (((0,), (0,)), ((), ())), preferred_element_type=F32
            )
            for j in range(4):
                table = multiples(*sincos(phase[j * 32 : j * 32 + 32]))
                dst = slice(n * LANES + j * 32, n * LANES + j * 32 + 32)
                for f in range(FREQS):
                    sf, cf = table[f]
                    ch, cl = split(cf)
                    sh, sl = split(sf)
                    th_ref[f, dst, :LANES] = ch
                    th_ref[f, dst, LANES:] = sh
                    tl_ref[f, dst, :LANES] = cl
                    tl_ref[f, dst, LANES:] = sl
        for f in range(FREQS):
            a = ah_ref[f * 2 + q]
            o = jnp.dot(a, th_ref[f], preferred_element_type=F32)
            o = o[:64] + o[64:] + jnp.dot(a[:64], tl_ref[f], preferred_element_type=F32)
            for d in range(2):
                res = []
                for pol in range(2):
                    r = (d * 2 + pol) * 16
                    src = d * 64 + pol * 32
                    pq = []
                    for part in range(2):
                        for comp in range(2):
                            v = o[r + comp * 8 : r + comp * 8 + 8, part * LANES : (part + 1) * LANES]
                            lo_v = roll(v, (pol * 64 - src) % LANES, 1)
                            hi_v = roll(v, (pol * 64 + 32 - src) % LANES, 1)
                            pq.append(jnp.where(iota((8, LANES), 1) % 64 < 32, lo_v, hi_v))
                    pr, pi, qr, qi = pq
                    sign = jnp.where(iota((8, LANES), 1) % 64 < 32, 1.0, -1.0)
                    res.append((pr - sign * qi, pi + sign * qr))
                left = iota((8, LANES), 1) < 64
                out_ref[2 * q + d, f, 0:8] = jnp.where(left, res[0][0], res[1][0])
                out_ref[2 * q + d, f, 8:16] = jnp.where(left, res[0][1], res[1][1])


def directions(angle):
    theta = math.pi * ((angle // NPHI).astype(F32) + 0.5) / (ANGLES // NPHI)
    phi = 2.0 * math.pi * (angle % NPHI).astype(F32) / NPHI
    return (jnp.sin(theta) * jnp.cos(phi), jnp.sin(theta) * jnp.sin(phi), jnp.cos(theta))


def project(acc_re, acc_im, pos_x, pos_y, pos_z, angle, omegas):
    dir_x, dir_y, dir_z = directions(angle)
    geometry = (
        dir_x[:, None] * pos_x[None] + dir_y[:, None] * pos_y[None] + dir_z[:, None] * pos_z[None]
    )
    phase = omegas[:, None, None] * geometry[None]
    cosine = jnp.cos(phase)
    sine = jnp.sin(phase)
    high = lax.Precision.HIGHEST
    real = jnp.einsum("fas,fcs->fca", cosine, acc_re, precision=high) - jnp.einsum(
        "fas,fcs->fca", sine, acc_im, precision=high
    )
    imag = jnp.einsum("fas,fcs->fca", sine, acc_re, precision=high) + jnp.einsum(
        "fas,fcs->fca", cosine, acc_im, precision=high
    )
    return jnp.concatenate([real, imag], axis=1)


def far_general(samples, cells, owner_table, sizes, tiles_x, tiles_z, scale):
    size_x, size_y, size_z = sizes
    tiles = tiles_x * tiles_z
    sample = samples.reshape(STEPS, 8, LANES)[:, :6]
    omegas = 0.4 * (jnp.arange(FREQS, dtype=F32) + 1.0)
    phase = omegas[:, None] * (DT * (jnp.arange(STEPS, dtype=F32) + 1.0))[None]
    acc_re = jnp.sum(jnp.cos(phase)[:, :, None, None] * sample[None], axis=1)
    acc_im = jnp.sum(jnp.sin(phase)[:, :, None, None] * sample[None], axis=1)
    local = jnp.maximum(cells, 0)
    glob_x = lax.axis_index("gx") * size_x + local // (size_y * size_z)
    glob_y = local // size_z % size_y
    glob_z = lax.axis_index("gz") * size_z + local % size_z
    pos_x = glob_x.astype(F32) + (0.5 - size_x * tiles_x / 2)
    pos_y = glob_y.astype(F32) + (0.5 - size_y / 2)
    pos_z = glob_z.astype(F32) + (0.5 - size_z * tiles_z / 2)
    block_len = ANGLES // tiles
    owners = jnp.arange(tiles, dtype=jnp.int32)
    blocks = jnp.sum(jnp.where(owner_table[None, :] == owners[:, None], owners[None, :], 0), axis=1)
    angle = (blocks[:, None] * block_len + jnp.arange(block_len, dtype=jnp.int32)[None]).reshape(-1)
    pattern = project(acc_re, acc_im, pos_x, pos_y, pos_z, angle, omegas)
    pattern = jnp.transpose(pattern.reshape(FREQS, 12, tiles, block_len), (2, 0, 1, 3))
    return lax.psum_scatter(pattern, ("gx", "gz"), scatter_dimension=0, tiled=True) * scale


VMEM = pl.BlockSpec(memory_space=pltpu.VMEM)
SMEM = pl.BlockSpec(memory_space=pltpu.SMEM)


def shards(nx, nz, e_init, h_init, material, eps_table, sigma_table, face_cells, owner_table):
    size_x, size_y, size_z = material.shape
    ns = 1 if nz == 2 else 2
    plane = (size_y, size_z)
    both = ("gx", "gz")

    def pair_a(i):
        return i ^ 1

    def pair_b(i):
        return i + 1 if i % 2 else i - 1

    def pair_z(k, s):
        return k + 1 if (k + s) % 2 == 0 else k - 1

    payload = 7 * W + 4 * ns
    xa, xb, zp = pl.pallas_call(
        functools.partial(pack_kernel, ns),
        out_shape=(
            jax.ShapeDtypeStruct((payload,) + plane, F32),
            jax.ShapeDtypeStruct((payload,) + plane, F32),
            jax.ShapeDtypeStruct((ns, 8) + plane, F32),
        ),
        in_specs=[VMEM] * 3,
        out_specs=(VMEM,) * 3,
        name="pack",
    )(e_init, h_init, material)

    z_in, diag_in = [], []
    for s in range(ns):
        links = [
            (i * nz + k, pair_b(i) * nz + pair_z(k, s))
            for i in range(nx)
            for k in range(nz)
            if 0 <= pair_b(i) < nx and 0 <= pair_z(k, s) < nz
        ]
        diag_in.append(lax.ppermute(zp[s, :4], both, links))
        links = [(k, pair_z(k, s)) for k in range(nz) if 0 <= pair_z(k, s) < nz]
        z_in.append(lax.ppermute(zp[s], "gz", links))
    xb_in = lax.ppermute(
        xb, "gx", [(i, pair_b(i)) for i in range(nx) if 0 <= pair_b(i) < nx]
    )
    swap = [(i, pair_a(i)) for i in range(nx)]
    xa_in = lax.ppermute(xa, "gx", swap)
    z_in = jnp.stack(z_in)
    diag_in = jnp.stack(diag_in)
    za_in = lax.ppermute(z_in, "gx", swap)

    wide = size_x + 2 * W
    e_field, h_field, samples = pl.pallas_call(
        functools.partial(field_kernel, ns, nx, nz),
        out_shape=(
            jax.ShapeDtypeStruct(e_init.shape, F32),
            jax.ShapeDtypeStruct(h_init.shape, F32),
            jax.ShapeDtypeStruct((8 * STEPS, LANES), F32),
        ),
        in_specs=[VMEM] * 9 + [SMEM] * 3 + [VMEM],
        out_specs=(VMEM,) * 3,
        scratch_shapes=[
            pltpu.VMEM(((STEPS + 1) * 8 * wide * size_y, LANES), F32),
            pltpu.VMEM((2 * wide * size_y, LANES), F32),
            pltpu.VMEM((STEPS * 4 * 3 * size_y, LANES), F32),
        ],
        compiler_params=pltpu.CompilerParams(vmem_limit_bytes=48 * 1024 * 1024),
        name="fields",
    )(
        e_init, h_init, material, xa_in, xb_in, zp, z_in, za_in, diag_in,
        eps_table.reshape(1, -1), sigma_table.reshape(1, -1), face_cells, face_cells,
    )

    tiles = nx * nz
    scale = 1.0 / math.sqrt(tiles * face_cells.shape[1] * STEPS)
    if not (nx == 16 and nz == 2):
        far = far_general(
            samples, face_cells[0], owner_table, material.shape, nx, nz, scale
        )
        return e_field, h_field, far

    def swap_all(v, mx, mz):
        links = [(i * nz + k, (i ^ mx) * nz + (k ^ mz)) for i in range(nx) for k in range(nz)]
        return lax.ppermute(v, both, links)

    mine = jnp.stack([samples, swap_all(samples, 1, 0)])
    by_y = swap_all(mine, 2, 0)
    by_x = swap_all(mine, 0, 1)
    by_xy = swap_all(mine, 2, 1)
    slots = 8 * LANES
    parts = pl.pallas_call(
        functools.partial(project_kernel, size_x, size_y, size_z, nx, nz),
        out_shape=jax.ShapeDtypeStruct((4, FREQS, 16, LANES), F32),
        in_specs=[VMEM] * 4 + [SMEM],
        out_specs=VMEM,
        scratch_shapes=[
            pltpu.SMEM((tiles,), jnp.int32),
            pltpu.VMEM((FREQS, slots, 2 * LANES), BF16),
            pltpu.VMEM((FREQS, slots, 2 * LANES), BF16),
            pltpu.VMEM((FREQS * 2, 128, slots), BF16),
            pltpu.VMEM((8, LANES), F32),
        ],
        compiler_params=pltpu.CompilerParams(vmem_limit_bytes=48 * 1024 * 1024),
        name="project",
    )(mine, by_y, by_x, by_xy, owner_table)
    total = parts[0]
    for d in range(1, 4):
        total = total + swap_all(parts[d], 4 * d, 0)
    far = jnp.concatenate([total[:, 0:6], total[:, 8:14]], axis=1) * scale
    return e_field, h_field, far[None]


def solution(mesh):
    nx, nz = mesh.shape["gx"], mesh.shape["gz"]
    return jax.shard_map(
        functools.partial(shards, nx, nz),
        mesh=mesh,
        in_specs=(
            P(None, "gx", None, "gz"),
            P(None, "gx", None, "gz"),
            P("gx", None, "gz"),
            P(),
            P(),
            P(("gx", "gz"), None),
            P(),
        ),
        out_specs=(
            P(None, "gx", None, "gz"),
            P(None, "gx", None, "gz"),
            P(("gx", "gz"), None, None, None),
        ),
        check_vma=False,
    )
```

```python
import functools
import math

import jax
import jax.numpy as jnp
from jax import lax
from jax.experimental import pallas as pl
from jax.experimental.pallas import tpu as pltpu
from jax.sharding import PartitionSpec as P

STEPS = 4
ANGLES = 4096
NPHI = 64
FREQS = 4
DT = 0.5

W = 4
BLOCK = 10
LANES = 128
F32 = jnp.float32
BF16 = jnp.bfloat16


def roll(v, shift, axis):
    return pltpu.roll(v, shift, axis)


def iota(shape, axis):
    return lax.broadcasted_iota(jnp.int32, shape, axis)


def fold_pair(a, b, up, lane):
    own = jnp.where(up, lane, 127 - lane) >= 124
    return jnp.where(own, b, roll(a, jnp.where(up, 124, 4), 1))


def pack_kernel(ns, e_hbm, h_hbm, m_hbm, xa_ref, xb_ref, zp_ref, zd_ref, f_ref, m_ref, sem):
    size_x, size_y = m_ref.shape[0], m_ref.shape[1]
    gx, gz = lax.axis_index("gx"), lax.axis_index("gz")
    copies = [
        pltpu.make_async_copy((e_hbm if c < 3 else h_hbm).at[c % 3], f_ref.at[c], sem.at[c])
        for c in range(6)
    ]
    copies.append(pltpu.make_async_copy(m_hbm, m_ref, sem.at[6]))
    for copy in copies:
        copy.start()
    even = gx % 2 == 0
    lane = iota((size_y, LANES), 1)
    group = lane // 8

    def plane(c, x):
        return f_ref[c, x] if c < 6 else m_ref[x].astype(F32)

    for i in range(4):
        comps = (2 * i, 2 * i + 1) if i < 3 else (6, 6)
        for c in sorted(set(comps)):
            copies[c].wait()
            for ref, off in ((xa_ref, size_x - W), (xb_ref, 0)):
                off = jnp.where(even, off, size_x - W - off)
                for j in range(W):
                    ref[c * W + j] = plane(c, off + j)
        for s in range(ns):
            up = (gz + s) % 2 == 0
            base = jnp.where(up, 8, 0)

            def fold(g, acc):
                out = []
                for q in range(2):
                    x = (g + 28) % 32 if q == 0 else g + 12
                    cell = fold_pair(plane(comps[0], x), plane(comps[1], x), up, lane)
                    cell = roll(cell, (base + 8 * g) % LANES, 1)
                    out.append(jnp.where(group == g, cell, acc[q]))
                return tuple(out)

            zero = jnp.zeros((size_y, LANES), F32)
            acc = lax.fori_loop(0, 16, fold, (zero, zero), unroll=8)
            zp_ref[s, i] = acc[0]
            zp_ref[s, 4 + i] = acc[1]
            xa_ref[7 * W + 4 * s + i] = acc[0]
            zd_ref[s, i] = acc[0]


def coef_tables(eps_ref, sigma_ref, shape):
    lane = iota(shape, 1)
    eps = jnp.ones(shape, F32)
    sigma = jnp.zeros(shape, F32)
    for i in range(eps_ref.shape[0]):
        eps = jnp.where(lane == i, eps_ref[i], eps)
        sigma = jnp.where(lane == i, sigma_ref[i], sigma)
    loss = sigma * DT / (2.0 * eps)
    return (1.0 - loss) / (1.0 + loss), DT / (eps * (1.0 + loss))


def pick(table, index):
    return jnp.take_along_axis(table, index, axis=1, mode="promise_in_bounds")


def field_kernel(
    ns,
    nx,
    nz,
    e_ref,
    h_ref,
    m_ref,
    xa_ref,
    xb_ref,
    zp_ref,
    zr_ref,
    za_ref,
    zb_ref,
    eps_ref,
    sigma_ref,
    cells_ref,
    cellv_ref,
    eo_ref,
    ho_ref,
    so_ref,
    st_ref,
    co_ref,
    in_ref,
    sp_ref,
    sc_ref,
    qb_ref,
    sem,
):
    size_x, size_y = m_ref.shape[0], m_ref.shape[1]
    wide = size_x + 2 * W
    span = wide * size_y
    shape = (size_y, LANES)
    gx, gz = lax.axis_index("gx"), lax.axis_index("gz")
    even = gx % 2 == 0
    lower = gx > 0
    upper = gx < nx - 1
    lane = iota(shape, 1)
    row = iota(shape, 0)
    ca_t, cb_t = coef_tables(eps_ref, sigma_ref, shape)

    def at(t, c, x):
        return pl.ds(((t * 8 + c) * wide + x) * size_y, size_y)

    def coef_at(c, x):
        return pl.ds((c * wide + x) * size_y, size_y)

    def block(i):
        return pl.ds(i * size_y, size_y)

    def own_plane(x, _):
        for c in range(3):
            st_ref[at(0, c, x + W)] = e_ref[c, x]
            st_ref[at(0, 3 + c, x + W)] = h_ref[c, x]
        index = m_ref[x]
        co_ref[coef_at(0, x + W)] = pick(ca_t, index)
        co_ref[coef_at(1, x + W)] = pick(cb_t, index)
        return 0

    lax.fori_loop(0, size_x, own_plane, 0, unroll=8)
    pos_a = jnp.where(even, size_x + W, 0)
    pos_b = jnp.where(even, 0, size_x + W)
    ok_b = jnp.where(even, lower, upper).astype(F32)

    def halo_plane(j, _):
        for ref, pos, ok in ((xa_ref, pos_a, None), (xb_ref, pos_b, ok_b)):
            for c in range(6):
                st_ref[at(0, c, pos + j)] = ref[c * W + j]
            index = ref[6 * W + j].astype(jnp.int32)
            ca, cb = pick(ca_t, index), pick(cb_t, index)
            if ok is not None:
                ca, cb = ca * ok, cb * ok
            co_ref[coef_at(0, pos + j)] = ca
            co_ref[coef_at(1, pos + j)] = cb
        return 0

    lax.fori_loop(0, W, halo_plane, 0, unroll=4)

    group = lane // 8
    first_half = lane % 8 < 4
    fy_keep = row < size_y - 1
    by_keep = row > 0

    def fwd_y(v):
        return jnp.where(fy_keep, roll(v, size_y - 1, 0), 0.0)

    def bwd_y(v):
        return jnp.where(by_keep, roll(v, 1, 0), 0.0)

    def fwd_z(v):
        return roll(v, 127, 1)

    def bwd_z(v):
        return roll(v, 1, 1)

    inside = [
        jnp.where(jnp.logical_and(group < W, jnp.logical_not(lower)), 0.0, 1.0),
        jnp.ones(shape, F32),
        jnp.where(jnp.logical_and(group >= W, jnp.logical_not(upper)), 0.0, 1.0),
    ]
    for s in range(ns):
        up = (gz + s) % 2 == 0
        partner = jnp.where(up, gz + 1, gz - 1)
        ok = jnp.logical_and(partner >= 0, partner < nz)
        give_e = jnp.where(jnp.logical_and(up, ok), 1.0, 0.0)
        give_h = jnp.where(jnp.logical_and(jnp.logical_not(up), ok), 1.0, 0.0)
        base = jnp.where(up, 8, 0)

        def corner(j, acc):
            g = j + jnp.where(even, 0, W)
            comps = [xb_ref[c * W + j] for c in range(7)]
            comps.append(comps[6])
            out = []
            for i in range(4):
                cell = fold_pair(comps[2 * i], comps[2 * i + 1], up, lane)
                cell = roll(cell, (base + 8 * g) % LANES, 1)
                out.append(jnp.where(group == g, cell, acc[i]))
            return tuple(out)

        zero = jnp.zeros(shape, F32)
        acc = lax.fori_loop(0, W, corner, (zero,) * 4, unroll=4)
        for i in range(4):
            qb_ref[i] = acc[i]

        def unfold(i, _):
            def whole(mine, other):
                lo = jnp.where(up, mine, other)
                hi = jnp.where(up, other, mine)
                return (
                    jnp.where(first_half, lo, hi),
                    jnp.where(first_half, roll(lo, 124, 1), roll(hi, 4, 1)),
                )

            q0 = whole(zp_ref[s, i], zr_ref[s, i])
            q1 = whole(zp_ref[s, 4 + i], zr_ref[s, 4 + i])
            qa = whole(xa_ref[7 * W + 4 * s + i], za_ref[s, i])
            qb = whole(qb_ref[i], zb_ref[s, i])
            for k in range(2):
                below = jnp.where(even, qb[k], qa[k])
                above = jnp.where(even, qa[k], qb[k])
                c = (2 * i + k) * 3
                sp_ref[block(c)] = jnp.where(group < W, below, q0[k])
                sp_ref[block(c + 1)] = q1[k]
                sp_ref[block(c + 2)] = jnp.where(group < W, q0[k], above)
            return 0

        lax.fori_loop(0, 4, unfold, 0, unroll=4)
        for q in range(3):
            index = sp_ref[block(18 + q)].astype(jnp.int32)
            sc_ref[block(q)] = pick(ca_t, index) * inside[q]
            sc_ref[block(3 + q)] = pick(cb_t, index) * inside[q]

        def fwd_x(v):
            r = [roll(u, 120, 1) for u in v]
            return [jnp.where(lane < 120, r[0], r[1]), jnp.where(lane < 120, r[1], r[2]), r[2]]

        def bwd_x(v):
            r = [roll(u, 8, 1) for u in v]
            return [r[0], jnp.where(lane >= 8, r[1], r[0]), jnp.where(lane >= 8, r[2], r[1])]

        def each(f, *vs):
            return [f(*u) for u in zip(*vs)]

        def strip_step(t, _):
            ex, ey, ez, hx, hy, hz = (
                [sp_ref[block(c * 3 + q)] for q in range(3)] for c in range(6)
            )
            ca_s = [sc_ref[block(q)] for q in range(3)]
            cb_s = [sc_ref[block(3 + q)] for q in range(3)]
            dt_s = [DT * k for k in inside]
            side_e = [[v * give_e for v in ex], [v * give_e for v in ey]]
            ez_x, ey_x = fwd_x(ez), fwd_x(ey)
            hx = each(
                lambda h, z, y, d: h - d * ((fwd_y(z) - z) - (fwd_z(y) - y)), hx, ez, ey, dt_s
            )
            hy = each(
                lambda h, x, z, zx, d: h - d * ((fwd_z(x) - x) - (zx - z)), hy, ex, ez, ez_x, dt_s
            )
            hz = each(
                lambda h, y, yx, x, d: h - d * ((yx - y) - (fwd_y(x) - x)), hz, ey, ey_x, ex, dt_s
            )
            hz_x, hy_x = bwd_x(hz), bwd_x(hy)
            ex = each(
                lambda e, z, y, a, b: a * e + b * ((z - bwd_y(z)) - (y - bwd_z(y))),
                ex, hz, hy, ca_s, cb_s,
            )
            ey = each(
                lambda e, x, z, zx, a, b: a * e + b * ((x - bwd_z(x)) - (z - zx)),
                ey, hx, hz, hz_x, ca_s, cb_s,
            )
            ez = each(
                lambda e, y, yx, x, a, b: a * e + b * ((y - yx) - (x - bwd_y(x))),
                ez, hy, hy_x, hx, ca_s, cb_s,
            )
            for c, v in enumerate((ex, ey, ez, hx, hy, hz)):
                for q in range(3):
                    sp_ref[block(c * 3 + q)] = v[q]
            for j, v in enumerate((hx, hy)):
                for q in range(3):
                    dst = block((t * 2 + j) * 3 + q)
                    add = jnp.where(lane % 8 == 4, side_e[j][q], roll(v[q] * give_h, 2, 1))
                    in_ref[dst] = add if s == 0 else in_ref[dst] + add
            return 0

        lax.fori_loop(0, STEPS, strip_step, 0)

    dt_lo = jnp.where(lower, DT, 0.0)
    dt_hi = jnp.where(upper, DT, 0.0)

    planes = range(BLOCK)

    def advance(t, x, carry):
        hy_p, hz_p = carry
        old = [[st_ref[at(t - 1, c, x + i)] for i in range(BLOCK + (c < 3))] for c in range(6)]
        ca = [co_ref[coef_at(0, x + i)] for i in planes]
        cb = [co_ref[coef_at(1, x + i)] for i in planes]
        ex, ey, ez, hx, hy, hz = old
        side_x, side_y = [], []
        for i in planes:
            shift = (123 - 8 * ((x + i) % 16)) % LANES
            side_x.append(roll(in_ref[block((t - 1) * 6 + (x + i) // 16)], shift, 1))
            side_y.append(roll(in_ref[block((t - 1) * 6 + 3 + (x + i) // 16)], shift, 1))
        ex_z = [jnp.where(last, side_x[i], fwd_z(ex[i])) for i in planes]
        ey_z = [jnp.where(last, side_y[i], fwd_z(ey[i])) for i in planes]
        ez_y = [fwd_y(ez[i]) for i in planes]
        ex_y = [fwd_y(ex[i]) for i in planes]
        dt = [
            jnp.where(x + i < W, dt_lo, jnp.where(x + i >= size_x + W, dt_hi, DT)) for i in planes
        ]
        hx = [hx[i] - dt[i] * ((ez_y[i] - ez[i]) - (ey_z[i] - ey[i])) for i in planes]
        hy = [hy[i] - dt[i] * ((ex_z[i] - ex[i]) - (ez[i + 1] - ez[i])) for i in planes]
        hz = [hz[i] - dt[i] * ((ey[i + 1] - ey[i]) - (ex_y[i] - ex[i])) for i in planes]
        hx_z = [jnp.where(first, side_x[i], bwd_z(hx[i])) for i in planes]
        hy_z = [jnp.where(first, side_y[i], bwd_z(hy[i])) for i in planes]
        hy_x, hz_x = [hy_p] + hy, [hz_p] + hz
        new = [
            [ca[i] * ex[i] + cb[i] * ((hz[i] - bwd_y(hz[i])) - (hy[i] - hy_z[i])) for i in planes],
            [ca[i] * ey[i] + cb[i] * ((hx[i] - hx_z[i]) - (hz[i] - hz_x[i])) for i in planes],
            [ca[i] * ez[i] + cb[i] * ((hy[i] - hy_x[i]) - (hx[i] - bwd_y(hx[i]))) for i in planes],
            hx, hy, hz,
        ]
        for c in range(6):
            for i in planes:
                st_ref[at(t, c, x + i)] = new[c][i]
        return hy[-1], hz[-1]

    last, first = lane == 127, lane == 0

    def step(t, _):
        zero = jnp.zeros(shape, F32)
        lax.fori_loop(0, wide // BLOCK, lambda i, c: advance(t, i * BLOCK, c), (zero, zero))
        return 0

    lax.fori_loop(1, STEPS + 1, step, 0)

    copies = []
    for c in range(3):
        for ref, cc in ((eo_ref, c), (ho_ref, 3 + c)):
            src = pl.ds(((STEPS * 8 + cc) * wide + W) * size_y, size_x * size_y)
            copies.append(pltpu.make_async_copy(st_ref.at[src], ref.at[c], sem.at[cc]))
    for copy in copies:
        copy.start()

    lane8 = iota((8, LANES), 1)
    row8 = iota((8, LANES), 0)

    def slot(m, accs):
        cell = cells_ref[0, m]
        used = cell >= 0
        cell = jnp.maximum(cell, 0)
        line = cell // LANES
        shift = (m - cell) % LANES
        here = lane8 == jnp.where(used, m, -1)
        out = []
        for t in range(STEPS):
            start = (t + 1) * 8 * span + W * size_y + line
            v = st_ref[pl.ds(start, 8, stride=span), :]
            out.append(jnp.where(here, roll(v, shift, 1), accs[t]))
        return tuple(out)

    zero8 = jnp.zeros((8, LANES), F32)
    accs = lax.fori_loop(0, LANES, slot, (zero8,) * STEPS, unroll=32)
    for t in range(STEPS):
        extra = cellv_ref[...].astype(F32) if t == 0 else zero8
        so_ref[t * 8 : t * 8 + 8] = jnp.where(row8 < 6, accs[t], extra)
    for copy in copies:
        copy.wait()


SIN_C = (3.1415926401307077, -5.167710083507896, 2.550077523214726, -0.5982912856213906, 0.07765766030763246)
COS_C = (0.9999999532476085, -4.934792830619649, 4.058411352862754, -1.3318765680819573, 0.21968961109991972)
ROUND = 12582912.0


def horner(coefs, u):
    v = u * coefs[-1] + coefs[-2]
    for k in coefs[-3::-1]:
        v = v * u + k
    return v


def sincos4(turns):
    r = turns - ((turns + ROUND) - ROUND)
    u = r * r
    half_s = horner(SIN_C, u) * r
    half_c = horner(COS_C, u)
    twice = half_s + half_s
    s = twice * half_c
    c = 1.0 - twice * half_s
    s_2, c_2 = s + s, c + c
    s2 = s_2 * c
    c2 = 1.0 - s_2 * s
    s3 = c_2 * s2 - s
    c3 = c_2 * c2 - c
    s2_2 = s2 + s2
    return (s, c), (s2, c2), (s3, c3), (s2_2 * c2, 1.0 - s2_2 * s2)


def sincos(turns):
    return sincos4(turns)[0]


def split(v):
    hi = v.astype(BF16)
    return hi, (v - hi.astype(F32)).astype(BF16)


def project_kernel(
    size_x, size_y, size_z, tiles_x, tiles_z, own_ref, r1_ref, r2_ref, r3_ref, owner_ref, out_ref,
    inv_ref, smp_ref, dir_ref, pos_ref, th_ref, tl_ref, a_ref, acc_ref,
):
    gx, gz = lax.axis_index("gx"), lax.axis_index("gz")
    tiles = tiles_x * tiles_z
    base = 0.4 / (2.0 * math.pi)
    polars = ANGLES // NPHI

    def put(b, _):
        inv_ref[owner_ref[b]] = b
        return 0

    lax.fori_loop(0, tiles, put, 0, unroll=8)
    blocks = [inv_ref[(gx ^ (4 * d)) * tiles_z + gz] for d in range(4)]

    for i, ref in enumerate((own_ref, r1_ref, r2_ref, r3_ref)):
        for core in range(2):
            smp_ref[2 * i + core] = ref[core]
    row16 = iota((16, LANES), 0)
    lane16 = iota((16, LANES), 1)
    row8 = iota((8, LANES), 0)
    lane8 = iota((8, LANES), 1)

    def split3(v):
        a = v.astype(BF16).astype(F32)
        b = (v - a).astype(BF16).astype(F32)
        return a, b, v - a - b

    for q in range(2):
        block = jnp.where(lane16 < 64, blocks[2 * q], blocks[2 * q + 1])
        polar = 2 * block + (lane16 % 64) // 32
        st, _ = sincos((polar.astype(F32) + 0.5) * (0.5 / polars))
        sp, cp = sincos((lane16 % 32).astype(F32) * (1.0 / NPHI))
        ux = split3(base * st * cp)
        uy = split3(base * st * sp)
        mat = jnp.zeros((16, LANES), F32)
        for k in range(9):
            src = ux[k % 3] if k < 6 else uy[k % 3]
            mat = jnp.where(row16 == k, src, mat)
        dir_ref[q] = mat.astype(BF16)
    combo = jnp.zeros((8, LANES), jnp.int32)
    for d in range(4):
        combo = jnp.where(row8 // 2 == d, 2 * blocks[d] + row8 % 2, combo)
    _, uz = sincos((combo.astype(F32) + 0.5) * (0.5 / polars))
    uz = uz * base

    def wave(f, t):
        angle = 0.4 * (f + 1) * DT * (t + 1)
        return math.cos(angle), math.sin(angle)

    def gather(pair, _):
        pos = []
        for core in range(2):
            n = 2 * pair + core
            tile_x = gx ^ (2 * (pair % 2) + core)
            tile_z = gz ^ (pair // 2)
            rows = [smp_ref[n, t * 8 : t * 8 + 8] for t in range(STEPS)]
            cell = jnp.maximum(rows[0][6:7], 0.0).astype(jnp.int32)
            pz = (cell % size_z + tile_z * size_z).astype(F32) + (0.5 - size_z * tiles_z / 2)
            zs = sincos4(uz * pz)
            lanes = slice(core * LANES, (core + 1) * LANES)
            for f in range(FREQS):
                re = sum(wave(f, t)[0] * rows[t] for t in range(STEPS))
                im = sum(wave(f, t)[1] * rows[t] for t in range(STEPS))
                zsin, zcos = zs[f]
                for k in range(8):
                    sk, ck = zsin[k : k + 1], zcos[k : k + 1]
                    both = jnp.concatenate([re * ck - im * sk, re * sk + im * ck], axis=0)
                    hi, lo = split(both)
                    q, kk = k // 4, k % 4
                    a_ref[pair, f * 2 + q, kk * 16 : kk * 16 + 16, lanes] = hi
                    a_ref[pair, f * 2 + q, 64 + kk * 16 : 80 + kk * 16, lanes] = lo
            gxi = cell // (size_y * size_z) + tile_x * size_x - size_x * tiles_x // 2
            high = ((gxi >> 4) << 4).astype(F32)
            low = (gxi & 15).astype(F32) + 0.5
            py = ((cell // size_z) % size_y).astype(F32) + (0.5 - size_y / 2)
            pos.append(
                jnp.where(row16 < 3, high, jnp.where(row16 < 6, low, jnp.where(row16 < 9, py, 0.0)))
            )
        pos_ref[pair] = jnp.concatenate(pos, axis=1).astype(BF16)
        return 0

    lax.fori_loop(0, 4, gather, 0)
    acc_ref[...] = jnp.zeros_like(acc_ref)

    def table(i, b):
        phase = lax.dot_general(
            pos_ref[i % 4], dir_ref[i // 4], (((0,), (0,)), ((), ())), preferred_element_type=F32
        )
        for j in range(8):
            dst = slice(j * 32, j * 32 + 32)
            values = sincos4(phase[dst])
            for f in range(FREQS):
                for part in range(2):
                    hi, lo = split(values[f][1 - part])
                    th_ref[b * 4 + f, dst, part * LANES : (part + 1) * LANES] = hi
                    tl_ref[b * 4 + f, dst, part * LANES : (part + 1) * LANES] = lo

    def multiply(i, b):
        for f in range(FREQS):
            a = a_ref[i % 4, f * 2 + i // 4]
            o = jnp.dot(a, th_ref[b * 4 + f], preferred_element_type=F32)
            o = o[:64] + o[64:] + jnp.dot(a[:64], tl_ref[b * 4 + f], preferred_element_type=F32)
            acc_ref[i // 4, f] += o

    table(0, 0)
    for k in range(8):
        if k < 7:
            table(k + 1, (k + 1) % 2)
        multiply(k, k % 2)

    near = lane8 % 64 < 32
    sign = jnp.where(near, 1.0, -1.0)

    def finish(i, _):
        q, f = i // 4, i % 4
        for d in range(2):
            res = []
            for pol in range(2):
                r = (d * 2 + pol) * 16
                src = d * 64 + pol * 32
                pq = []
                for part in range(2):
                    for comp in range(2):
                        v = acc_ref[
                            q, f, r + comp * 8 : r + comp * 8 + 8, part * LANES : (part + 1) * LANES
                        ]
                        lo_v = roll(v, (pol * 64 - src) % LANES, 1)
                        hi_v = roll(v, (pol * 64 + 32 - src) % LANES, 1)
                        pq.append(jnp.where(near, lo_v, hi_v))
                pr, pi, qr, qi = pq
                res.append((pr - sign * qi, pi + sign * qr))
            out_ref[2 * q + d, f, 0:8] = jnp.where(lane8 < 64, res[0][0], res[1][0])
            out_ref[2 * q + d, f, 8:16] = jnp.where(lane8 < 64, res[0][1], res[1][1])
        return 0

    lax.fori_loop(0, 8, finish, 0, unroll=2)


def directions(angle):
    theta = math.pi * ((angle // NPHI).astype(F32) + 0.5) / (ANGLES // NPHI)
    phi = 2.0 * math.pi * (angle % NPHI).astype(F32) / NPHI
    return (jnp.sin(theta) * jnp.cos(phi), jnp.sin(theta) * jnp.sin(phi), jnp.cos(theta))


def project(acc_re, acc_im, pos_x, pos_y, pos_z, angle, omegas):
    dir_x, dir_y, dir_z = directions(angle)
    geometry = (
        dir_x[:, None] * pos_x[None] + dir_y[:, None] * pos_y[None] + dir_z[:, None] * pos_z[None]
    )
    phase = omegas[:, None, None] * geometry[None]
    cosine = jnp.cos(phase)
    sine = jnp.sin(phase)
    high = lax.Precision.HIGHEST
    real = jnp.einsum("fas,fcs->fca", cosine, acc_re, precision=high) - jnp.einsum(
        "fas,fcs->fca", sine, acc_im, precision=high
    )
    imag = jnp.einsum("fas,fcs->fca", sine, acc_re, precision=high) + jnp.einsum(
        "fas,fcs->fca", cosine, acc_im, precision=high
    )
    return jnp.concatenate([real, imag], axis=1)


def far_general(samples, cells, owner_table, sizes, tiles_x, tiles_z, scale):
    size_x, size_y, size_z = sizes
    tiles = tiles_x * tiles_z
    sample = samples.reshape(STEPS, 8, LANES)[:, :6]
    omegas = 0.4 * (jnp.arange(FREQS, dtype=F32) + 1.0)
    phase = omegas[:, None] * (DT * (jnp.arange(STEPS, dtype=F32) + 1.0))[None]
    acc_re = jnp.sum(jnp.cos(phase)[:, :, None, None] * sample[None], axis=1)
    acc_im = jnp.sum(jnp.sin(phase)[:, :, None, None] * sample[None], axis=1)
    local = jnp.maximum(cells, 0)
    glob_x = lax.axis_index("gx") * size_x + local // (size_y * size_z)
    glob_y = local // size_z % size_y
    glob_z = lax.axis_index("gz") * size_z + local % size_z
    pos_x = glob_x.astype(F32) + (0.5 - size_x * tiles_x / 2)
    pos_y = glob_y.astype(F32) + (0.5 - size_y / 2)
    pos_z = glob_z.astype(F32) + (0.5 - size_z * tiles_z / 2)
    block_len = ANGLES // tiles
    owners = jnp.arange(tiles, dtype=jnp.int32)
    blocks = jnp.sum(jnp.where(owner_table[None, :] == owners[:, None], owners[None, :], 0), axis=1)
    angle = (blocks[:, None] * block_len + jnp.arange(block_len, dtype=jnp.int32)[None]).reshape(-1)
    pattern = project(acc_re, acc_im, pos_x, pos_y, pos_z, angle, omegas)
    pattern = jnp.transpose(pattern.reshape(FREQS, 12, tiles, block_len), (2, 0, 1, 3))
    return lax.psum_scatter(pattern, ("gx", "gz"), scatter_dimension=0, tiled=True) * scale


VMEM = pl.BlockSpec(memory_space=pltpu.VMEM)
SMEM = pl.BlockSpec(memory_space=pltpu.SMEM)
ANY = pl.BlockSpec(memory_space=pl.ANY)


def shards(nx, nz, e_init, h_init, material, eps_table, sigma_table, face_cells, owner_table):
    size_x, size_y, size_z = material.shape
    ns = 1 if nz == 2 else 2
    plane = (size_y, size_z)
    both = ("gx", "gz")

    def pair_a(i):
        return i ^ 1

    def pair_b(i):
        return i + 1 if i % 2 else i - 1

    def pair_z(k, s):
        return k + 1 if (k + s) % 2 == 0 else k - 1

    xa, xb, zp, zd = pl.pallas_call(
        functools.partial(pack_kernel, ns),
        out_shape=(
            jax.ShapeDtypeStruct((7 * W + 4 * ns,) + plane, F32),
            jax.ShapeDtypeStruct((7 * W,) + plane, F32),
            jax.ShapeDtypeStruct((ns, 8) + plane, F32),
            jax.ShapeDtypeStruct((ns, 4) + plane, F32),
        ),
        in_specs=[ANY] * 3,
        out_specs=(VMEM,) * 4,
        scratch_shapes=[
            pltpu.VMEM((6, size_x) + plane, F32),
            pltpu.VMEM((size_x,) + plane, jnp.int32),
            pltpu.SemaphoreType.DMA((7,)),
        ],
        compiler_params=pltpu.CompilerParams(vmem_limit_bytes=60 * 1024 * 1024),
        name="pack",
    )(e_init, h_init, material)
    xb_in = lax.ppermute(
        xb, "gx", [(i, pair_b(i)) for i in range(nx) if 0 <= pair_b(i) < nx]
    )

    swap = [(i, pair_a(i)) for i in range(nx)]
    xa_in = lax.ppermute(xa, "gx", swap)

    def turned(v, s, pair_x):
        links = [
            (i * nz + k, pair_x(i) * nz + pair_z(k, s))
            for i in range(nx)
            for k in range(nz)
            if 0 <= pair_x(i) < nx and 0 <= pair_z(k, s) < nz
        ]
        return lax.ppermute(v, both, links)

    z_in = []
    for s in range(ns):
        links = [(k, pair_z(k, s)) for k in range(nz) if 0 <= pair_z(k, s) < nz]
        z_in.append(lax.ppermute(zp[s], "gz", links))
    z_in = jnp.stack(z_in)
    za_in = jnp.stack([turned(zd[s], s, pair_a) for s in range(ns)])
    zb_in = jnp.stack([turned(zd[s], s, pair_b) for s in range(ns)])

    wide = size_x + 2 * W
    e_field, h_field, samples = pl.pallas_call(
        functools.partial(field_kernel, ns, nx, nz),
        out_shape=(
            jax.ShapeDtypeStruct((3, size_x * size_y, size_z), F32),
            jax.ShapeDtypeStruct((3, size_x * size_y, size_z), F32),
            jax.ShapeDtypeStruct((8 * STEPS, LANES), F32),
        ),
        in_specs=[VMEM] * 9 + [SMEM] * 3 + [VMEM],
        out_specs=(ANY, ANY, VMEM),
        scratch_shapes=[
            pltpu.VMEM(((STEPS + 1) * 8 * wide * size_y, LANES), F32),
            pltpu.VMEM((2 * wide * size_y, LANES), F32),
            pltpu.VMEM((STEPS * 2 * 3 * size_y, LANES), F32),
            pltpu.VMEM((8 * 3 * size_y, LANES), F32),
            pltpu.VMEM((2 * 3 * size_y, LANES), F32),
            pltpu.VMEM((4,) + plane, F32),
            pltpu.SemaphoreType.DMA((6,)),
        ],
        compiler_params=pltpu.CompilerParams(vmem_limit_bytes=48 * 1024 * 1024),
        name="fields",
    )(
        e_init, h_init, material, xa_in, xb_in, zp, z_in, za_in, zb_in,
        eps_table, sigma_table, face_cells, face_cells,
    )
    e_field = e_field.reshape(e_init.shape)
    h_field = h_field.reshape(h_init.shape)

    tiles = nx * nz
    scale = 1.0 / math.sqrt(tiles * face_cells.shape[1] * STEPS)
    if not (nx == 16 and nz == 2):
        far = far_general(
            samples, face_cells[0], owner_table, material.shape, nx, nz, scale
        )
        return e_field, h_field, far

    def swap_all(v, mx, mz):
        links = [(i * nz + k, (i ^ mx) * nz + (k ^ mz)) for i in range(nx) for k in range(nz)]
        return lax.ppermute(v, both, links)

    mine = jnp.stack([samples, swap_all(samples, 1, 0)])
    by_y = swap_all(mine, 2, 0)
    by_x = swap_all(mine, 0, 1)
    by_xy = swap_all(mine, 2, 1)
    parts = pl.pallas_call(
        functools.partial(project_kernel, size_x, size_y, size_z, nx, nz),
        out_shape=jax.ShapeDtypeStruct((4, FREQS, 16, LANES), F32),
        in_specs=[VMEM] * 4 + [SMEM],
        out_specs=VMEM,
        scratch_shapes=[
            pltpu.SMEM((tiles,), jnp.int32),
            pltpu.VMEM((8, 8 * STEPS, LANES), F32),
            pltpu.VMEM((2, 16, LANES), BF16),
            pltpu.VMEM((4, 16, 2 * LANES), BF16),
            pltpu.VMEM((2 * FREQS, 2 * LANES, 2 * LANES), BF16),
            pltpu.VMEM((2 * FREQS, 2 * LANES, 2 * LANES), BF16),
            pltpu.VMEM((4, FREQS * 2, 128, 2 * LANES), BF16),
            pltpu.VMEM((2, FREQS, 64, 2 * LANES), F32),
        ],
        compiler_params=pltpu.CompilerParams(vmem_limit_bytes=48 * 1024 * 1024),
        name="project",
    )(mine, by_y, by_x, by_xy, owner_table)
    total = parts[0]
    for d in range(1, 4):
        total = total + swap_all(parts[d], 4 * d, 0)
    far = jnp.concatenate([total[:, 0:6], total[:, 8:14]], axis=1) * scale
    return e_field, h_field, far[None]


def solution(mesh):
    nx, nz = mesh.shape["gx"], mesh.shape["gz"]
    return jax.shard_map(
        functools.partial(shards, nx, nz),
        mesh=mesh,
        in_specs=(
            P(None, "gx", None, "gz"),
            P(None, "gx", None, "gz"),
            P("gx", None, "gz"),
            P(),
            P(),
            P(("gx", "gz"), None),
            P(),
        ),
        out_specs=(
            P(None, "gx", None, "gz"),
            P(None, "gx", None, "gz"),
            P(("gx", "gz"), None, None, None),
        ),
        check_vma=False,
    )
```

```python
import functools
import math

import jax
import jax.numpy as jnp
from jax import lax
from jax.experimental import pallas as pl
from jax.experimental.pallas import tpu as pltpu
from jax.sharding import PartitionSpec as P

STEPS = 4
ANGLES = 4096
NPHI = 64
FREQS = 4
DT = 0.5

W = 4
BLOCK = 10
LANES = 128
F32 = jnp.float32
BF16 = jnp.bfloat16


def roll(v, shift, axis):
    return pltpu.roll(v, shift, axis)


def iota(shape, axis):
    return lax.broadcasted_iota(jnp.int32, shape, axis)


def fold_pair(a, b, up, lane):
    own = jnp.where(up, lane, 127 - lane) >= 124
    return jnp.where(own, b, roll(a, jnp.where(up, 124, 4), 1))


def pack_kernel(ns, e_hbm, h_hbm, m_hbm, xa_ref, xb_ref, zp_ref, zd_ref, f_ref, m_ref, sem):
    size_x, size_y = m_ref.shape[0], m_ref.shape[1]
    gx, gz = lax.axis_index("gx"), lax.axis_index("gz")
    copies = [
        pltpu.make_async_copy((e_hbm if c < 3 else h_hbm).at[c % 3], f_ref.at[c], sem.at[c])
        for c in range(6)
    ]
    copies.append(pltpu.make_async_copy(m_hbm, m_ref, sem.at[6]))
    for copy in copies:
        copy.start()
    even = gx % 2 == 0
    lane = iota((size_y, LANES), 1)
    group = lane // 8

    def plane(c, x):
        return f_ref[c, x] if c < 6 else m_ref[x].astype(F32)

    for i in range(4):
        comps = (2 * i, 2 * i + 1) if i < 3 else (6, 6)
        for c in sorted(set(comps)):
            copies[c].wait()
            for ref, off in ((xa_ref, size_x - W), (xb_ref, 0)):
                off = jnp.where(even, off, size_x - W - off)
                for j in range(W):
                    ref[c * W + j] = plane(c, off + j)
        for s in range(ns):
            up = (gz + s) % 2 == 0
            base = jnp.where(up, 8, 0)

            def fold(g, acc):
                out = []
                for q in range(2):
                    x = (g + 28) % 32 if q == 0 else g + 12
                    cell = fold_pair(plane(comps[0], x), plane(comps[1], x), up, lane)
                    cell = roll(cell, (base + 8 * g) % LANES, 1)
                    out.append(jnp.where(group == g, cell, acc[q]))
                return tuple(out)

            zero = jnp.zeros((size_y, LANES), F32)
            acc = lax.fori_loop(0, 16, fold, (zero, zero), unroll=8)
            zp_ref[s, i] = acc[0]
            zp_ref[s, 4 + i] = acc[1]
            xa_ref[7 * W + 4 * s + i] = acc[0]
            zd_ref[s, i] = acc[0]


def coef_tables(eps_ref, sigma_ref, shape):
    lane = iota(shape, 1)
    eps = jnp.ones(shape, F32)
    sigma = jnp.zeros(shape, F32)
    for i in range(eps_ref.shape[1]):
        eps = jnp.where(lane == i, eps_ref[0, i], eps)
        sigma = jnp.where(lane == i, sigma_ref[0, i], sigma)
    loss = sigma * DT / (2.0 * eps)
    return (1.0 - loss) / (1.0 + loss), DT / (eps * (1.0 + loss))


def pick(table, index):
    return jnp.take_along_axis(table, index, axis=1, mode="promise_in_bounds")


def field_kernel(
    ns,
    nx,
    nz,
    e_ref,
    h_ref,
    m_ref,
    xa_ref,
    xb_ref,
    zr_ref,
    za_ref,
    zb_ref,
    zp_ref,
    eps_hbm,
    sigma_hbm,
    cells_hbm,
    eo_ref,
    ho_ref,
    so_ref,
    st_ref,
    co_ref,
    in_ref,
    sp_ref,
    sc_ref,
    qb_ref,
    eps_ref,
    sigma_ref,
    cells_ref,
    sem,
    in_sem,
):
    size_x, size_y = m_ref.shape[0], m_ref.shape[1]
    wide = size_x + 2 * W
    span = wide * size_y
    shape = (size_y, LANES)
    gx, gz = lax.axis_index("gx"), lax.axis_index("gz")
    even = gx % 2 == 0
    lower = gx > 0
    upper = gx < nx - 1
    lane = iota(shape, 1)
    row = iota(shape, 0)
    small = [
        pltpu.make_async_copy(src, dst, in_sem.at[i])
        for i, (src, dst) in enumerate(
            (
                (eps_hbm, eps_ref),
                (sigma_hbm, sigma_ref),
                (cells_hbm, cells_ref),
            )
        )
    ]
    for copy in small:
        copy.start()

    def at(t, c, x):
        return pl.ds(((t * 8 + c) * wide + x) * size_y, size_y)

    def coef_at(c, x):
        return pl.ds((c * wide + x) * size_y, size_y)

    def block(i):
        return pl.ds(i * size_y, size_y)

    def own_plane(x, _):
        for c in range(3):
            st_ref[at(0, c, x + W)] = e_ref[c, x]
            st_ref[at(0, 3 + c, x + W)] = h_ref[c, x]
        return 0

    lax.fori_loop(0, size_x, own_plane, 0, unroll=8)
    for copy in small:
        copy.wait()
    ca_t, cb_t = coef_tables(eps_ref, sigma_ref, shape)

    def own_coef(x, _):
        index = m_ref[x]
        co_ref[coef_at(0, x + W)] = pick(ca_t, index)
        co_ref[coef_at(1, x + W)] = pick(cb_t, index)
        return 0

    lax.fori_loop(0, size_x, own_coef, 0, unroll=8)
    pos_a = jnp.where(even, size_x + W, 0)
    pos_b = jnp.where(even, 0, size_x + W)
    ok_b = jnp.where(even, lower, upper).astype(F32)

    def halo_plane(j, _):
        for ref, pos, ok in ((xa_ref, pos_a, None), (xb_ref, pos_b, ok_b)):
            for c in range(6):
                st_ref[at(0, c, pos + j)] = ref[c * W + j]
            index = ref[6 * W + j].astype(jnp.int32)
            ca, cb = pick(ca_t, index), pick(cb_t, index)
            if ok is not None:
                ca, cb = ca * ok, cb * ok
            co_ref[coef_at(0, pos + j)] = ca
            co_ref[coef_at(1, pos + j)] = cb
        return 0

    lax.fori_loop(0, W, halo_plane, 0, unroll=4)

    group = lane // 8
    first_half = lane % 8 < 4
    fy_keep = row < size_y - 1
    by_keep = row > 0

    def fwd_y(v):
        return jnp.where(fy_keep, roll(v, size_y - 1, 0), 0.0)

    def bwd_y(v):
        return jnp.where(by_keep, roll(v, 1, 0), 0.0)

    def fwd_z(v):
        return roll(v, 127, 1)

    def bwd_z(v):
        return roll(v, 1, 1)

    inside = [
        jnp.where(jnp.logical_and(group < W, jnp.logical_not(lower)), 0.0, 1.0),
        jnp.ones(shape, F32),
        jnp.where(jnp.logical_and(group >= W, jnp.logical_not(upper)), 0.0, 1.0),
    ]
    for s in range(ns):
        up = (gz + s) % 2 == 0
        partner = jnp.where(up, gz + 1, gz - 1)
        ok = jnp.logical_and(partner >= 0, partner < nz)
        give_e = jnp.where(jnp.logical_and(up, ok), 1.0, 0.0)
        give_h = jnp.where(jnp.logical_and(jnp.logical_not(up), ok), 1.0, 0.0)
        base = jnp.where(up, 8, 0)

        def corner(j, acc):
            g = j + jnp.where(even, 0, W)
            comps = [xb_ref[c * W + j] for c in range(7)]
            comps.append(comps[6])
            out = []
            for i in range(4):
                cell = fold_pair(comps[2 * i], comps[2 * i + 1], up, lane)
                cell = roll(cell, (base + 8 * g) % LANES, 1)
                out.append(jnp.where(group == g, cell, acc[i]))
            return tuple(out)

        zero = jnp.zeros(shape, F32)
        acc = lax.fori_loop(0, W, corner, (zero,) * 4, unroll=4)
        for i in range(4):
            qb_ref[i] = acc[i]

        def unfold(i, _):
            def whole(mine, other):
                lo = jnp.where(up, mine, other)
                hi = jnp.where(up, other, mine)
                return (
                    jnp.where(first_half, lo, hi),
                    jnp.where(first_half, roll(lo, 124, 1), roll(hi, 4, 1)),
                )

            q0 = whole(zp_ref[s, i], zr_ref[s, i])
            q1 = whole(zp_ref[s, 4 + i], zr_ref[s, 4 + i])
            qa = whole(xa_ref[7 * W + 4 * s + i], za_ref[s, i])
            qb = whole(qb_ref[i], zb_ref[s, i])
            for k in range(2):
                below = jnp.where(even, qb[k], qa[k])
                above = jnp.where(even, qa[k], qb[k])
                c = (2 * i + k) * 3
                sp_ref[block(c)] = jnp.where(group < W, below, q0[k])
                sp_ref[block(c + 1)] = q1[k]
                sp_ref[block(c + 2)] = jnp.where(group < W, q0[k], above)
            return 0

        lax.fori_loop(0, 4, unfold, 0, unroll=4)
        for q in range(3):
            index = sp_ref[block(18 + q)].astype(jnp.int32)
            sc_ref[block(q)] = pick(ca_t, index) * inside[q]
            sc_ref[block(3 + q)] = pick(cb_t, index) * inside[q]

        def fwd_x(v):
            r = [roll(u, 120, 1) for u in v]
            return [jnp.where(lane < 120, r[0], r[1]), jnp.where(lane < 120, r[1], r[2]), r[2]]

        def bwd_x(v):
            r = [roll(u, 8, 1) for u in v]
            return [r[0], jnp.where(lane >= 8, r[1], r[0]), jnp.where(lane >= 8, r[2], r[1])]

        def each(f, *vs):
            return [f(*u) for u in zip(*vs)]

        def strip_step(t, _):
            ex, ey, ez, hx, hy, hz = (
                [sp_ref[block(c * 3 + q)] for q in range(3)] for c in range(6)
            )
            ca_s = [sc_ref[block(q)] for q in range(3)]
            cb_s = [sc_ref[block(3 + q)] for q in range(3)]
            dt_s = [DT * k for k in inside]
            side_e = [[v * give_e for v in ex], [v * give_e for v in ey]]
            ez_x, ey_x = fwd_x(ez), fwd_x(ey)
            hx = each(
                lambda h, z, y, d: h - d * ((fwd_y(z) - z) - (fwd_z(y) - y)), hx, ez, ey, dt_s
            )
            hy = each(
                lambda h, x, z, zx, d: h - d * ((fwd_z(x) - x) - (zx - z)), hy, ex, ez, ez_x, dt_s
            )
            hz = each(
                lambda h, y, yx, x, d: h - d * ((yx - y) - (fwd_y(x) - x)), hz, ey, ey_x, ex, dt_s
            )
            hz_x, hy_x = bwd_x(hz), bwd_x(hy)
            ex = each(
                lambda e, z, y, a, b: a * e + b * ((z - bwd_y(z)) - (y - bwd_z(y))),
                ex, hz, hy, ca_s, cb_s,
            )
            ey = each(
                lambda e, x, z, zx, a, b: a * e + b * ((x - bwd_z(x)) - (z - zx)),
                ey, hx, hz, hz_x, ca_s, cb_s,
            )
            ez = each(
                lambda e, y, yx, x, a, b: a * e + b * ((y - yx) - (x - bwd_y(x))),
                ez, hy, hy_x, hx, ca_s, cb_s,
            )
            for c, v in enumerate((ex, ey, ez, hx, hy, hz)):
                for q in range(3):
                    sp_ref[block(c * 3 + q)] = v[q]
            for j, v in enumerate((hx, hy)):
                for q in range(3):
                    dst = block((t * 2 + j) * 3 + q)
                    add = jnp.where(lane % 8 == 4, side_e[j][q], roll(v[q] * give_h, 2, 1))
                    in_ref[dst] = add if s == 0 else in_ref[dst] + add
            return 0

        lax.fori_loop(0, STEPS, strip_step, 0)

    dt_lo = jnp.where(lower, DT, 0.0)
    dt_hi = jnp.where(upper, DT, 0.0)

    planes = range(BLOCK)

    def advance(t, x, carry):
        hy_p, hz_p = carry
        old = [[st_ref[at(t - 1, c, x + i)] for i in range(BLOCK + (c < 3))] for c in range(6)]
        ca = [co_ref[coef_at(0, x + i)] for i in planes]
        cb = [co_ref[coef_at(1, x + i)] for i in planes]
        ex, ey, ez, hx, hy, hz = old
        side_x, side_y = [], []
        for i in planes:
            shift = (123 - 8 * ((x + i) % 16)) % LANES
            side_x.append(roll(in_ref[block((t - 1) * 6 + (x + i) // 16)], shift, 1))
            side_y.append(roll(in_ref[block((t - 1) * 6 + 3 + (x + i) // 16)], shift, 1))
        ex_z = [jnp.where(last, side_x[i], fwd_z(ex[i])) for i in planes]
        ey_z = [jnp.where(last, side_y[i], fwd_z(ey[i])) for i in planes]
        ez_y = [fwd_y(ez[i]) for i in planes]
        ex_y = [fwd_y(ex[i]) for i in planes]
        dt = [
            jnp.where(x + i < W, dt_lo, jnp.where(x + i >= size_x + W, dt_hi, DT)) for i in planes
        ]
        hx = [hx[i] - dt[i] * ((ez_y[i] - ez[i]) - (ey_z[i] - ey[i])) for i in planes]
        hy = [hy[i] - dt[i] * ((ex_z[i] - ex[i]) - (ez[i + 1] - ez[i])) for i in planes]
        hz = [hz[i] - dt[i] * ((ey[i + 1] - ey[i]) - (ex_y[i] - ex[i])) for i in planes]
        hx_z = [jnp.where(first, side_x[i], bwd_z(hx[i])) for i in planes]
        hy_z = [jnp.where(first, side_y[i], bwd_z(hy[i])) for i in planes]
        hy_x, hz_x = [hy_p] + hy, [hz_p] + hz
        new = [
            [ca[i] * ex[i] + cb[i] * ((hz[i] - bwd_y(hz[i])) - (hy[i] - hy_z[i])) for i in planes],
            [ca[i] * ey[i] + cb[i] * ((hx[i] - hx_z[i]) - (hz[i] - hz_x[i])) for i in planes],
            [ca[i] * ez[i] + cb[i] * ((hy[i] - hy_x[i]) - (hx[i] - bwd_y(hx[i]))) for i in planes],
            hx, hy, hz,
        ]
        for c in range(6):
            for i in planes:
                st_ref[at(t, c, x + i)] = new[c][i]
        return hy[-1], hz[-1]

    last, first = lane == 127, lane == 0

    half = size_x // 2
    copies = []
    for part in range(2):
        copies.append([])
        for c in range(3):
            for ref, cc in ((eo_ref, c), (ho_ref, 3 + c)):
                src = ((STEPS * 8 + cc) * wide + W + part * half) * size_y
                copies[part].append(
                    pltpu.make_async_copy(
                        st_ref.at[pl.ds(src, half * size_y)],
                        ref.at[c, pl.ds(part * half * size_y, half * size_y)],
                        sem.at[part * 6 + cc],
                    )
                )
    blocks = wide // BLOCK

    def step(t, _):
        zero = jnp.zeros(shape, F32)

        def planes_from(i, c):
            c = advance(t, i * BLOCK, c)

            @pl.when(jnp.logical_and(t == STEPS, i == blocks // 2 - 1 + blocks % 2))
            def _():
                for copy in copies[0]:
                    copy.start()

            return c

        lax.fori_loop(0, blocks, planes_from, (zero, zero))
        return 0

    lax.fori_loop(1, STEPS + 1, step, 0)
    for copy in copies[1]:
        copy.start()

    lane8 = iota((8, LANES), 1)
    row8 = iota((8, LANES), 0)

    def slot(m, accs):
        *accs, numbers = accs
        cell = cells_ref[0, m]
        numbers = jnp.where(lane8 == m, cell.astype(F32), numbers)
        used = cell >= 0
        cell = jnp.maximum(cell, 0)
        line = cell // LANES
        shift = (m - cell) % LANES
        here = lane8 == jnp.where(used, m, -1)
        out = []
        for t in range(STEPS):
            start = (t + 1) * 8 * span + W * size_y + line
            v = st_ref[pl.ds(start, 8, stride=span), :]
            out.append(jnp.where(here, roll(v, shift, 1), accs[t]))
        return tuple(out) + (numbers,)

    zero8 = jnp.zeros((8, LANES), F32)
    *accs, numbers = lax.fori_loop(0, LANES, slot, (zero8,) * (STEPS + 1), unroll=32)
    for t in range(STEPS):
        extra = numbers if t == 0 else zero8
        so_ref[t * 8 : t * 8 + 8] = jnp.where(row8 < 6, accs[t], extra)
    for copy in copies[0] + copies[1]:
        copy.wait()


SIN_C = (3.1415926401307077, -5.167710083507896, 2.550077523214726, -0.5982912856213906, 0.07765766030763246)
COS_C = (0.9999999532476085, -4.934792830619649, 4.058411352862754, -1.3318765680819573, 0.21968961109991972)
ROUND = 12582912.0


def horner(coefs, u):
    v = u * coefs[-1] + coefs[-2]
    for k in coefs[-3::-1]:
        v = v * u + k
    return v


def sincos4(turns):
    r = turns - ((turns + ROUND) - ROUND)
    u = r * r
    half_s = horner(SIN_C, u) * r
    half_c = horner(COS_C, u)
    twice = half_s + half_s
    s = twice * half_c
    c = 1.0 - twice * half_s
    s_2, c_2 = s + s, c + c
    s2 = s_2 * c
    c2 = 1.0 - s_2 * s
    s3 = c_2 * s2 - s
    c3 = c_2 * c2 - c
    s2_2 = s2 + s2
    return (s, c), (s2, c2), (s3, c3), (s2_2 * c2, 1.0 - s2_2 * s2)


def sincos(turns):
    return sincos4(turns)[0]


def split(v):
    hi = v.astype(BF16)
    return hi, (v - hi.astype(F32)).astype(BF16)


def project_kernel(
    size_x, size_y, size_z, tiles_x, tiles_z, own_ref, r1_ref, r2_ref, r3_ref, owner_ref, out_ref,
    inv_ref, smp_ref, dir_ref, pos_ref, th_ref, tl_ref, a_ref, acc_ref,
):
    gx, gz = lax.axis_index("gx"), lax.axis_index("gz")
    tiles = tiles_x * tiles_z
    base = 0.4 / (2.0 * math.pi)
    polars = ANGLES // NPHI

    def put(b, _):
        inv_ref[owner_ref[b]] = b
        return 0

    lax.fori_loop(0, tiles, put, 0, unroll=8)
    blocks = [inv_ref[(gx ^ (4 * d)) * tiles_z + gz] for d in range(4)]

    for i, ref in enumerate((own_ref, r1_ref, r2_ref, r3_ref)):
        for core in range(2):
            smp_ref[2 * i + core] = ref[core]
    row16 = iota((16, LANES), 0)
    lane16 = iota((16, LANES), 1)
    row8 = iota((8, LANES), 0)
    lane8 = iota((8, LANES), 1)

    def split3(v):
        a = v.astype(BF16).astype(F32)
        b = (v - a).astype(BF16).astype(F32)
        return a, b, v - a - b

    for q in range(2):
        block = jnp.where(lane16 < 64, blocks[2 * q], blocks[2 * q + 1])
        polar = 2 * block + (lane16 % 64) // 32
        st, _ = sincos((polar.astype(F32) + 0.5) * (0.5 / polars))
        sp, cp = sincos((lane16 % 32).astype(F32) * (1.0 / NPHI))
        ux = split3(base * st * cp)
        uy = split3(base * st * sp)
        mat = jnp.zeros((16, LANES), F32)
        for k in range(9):
            src = ux[k % 3] if k < 6 else uy[k % 3]
            mat = jnp.where(row16 == k, src, mat)
        dir_ref[q] = mat.astype(BF16)
    combo = jnp.zeros((8, LANES), jnp.int32)
    for d in range(4):
        combo = jnp.where(row8 // 2 == d, 2 * blocks[d] + row8 % 2, combo)
    _, uz = sincos((combo.astype(F32) + 0.5) * (0.5 / polars))
    uz = uz * base

    def wave(f, t):
        angle = 0.4 * (f + 1) * DT * (t + 1)
        return math.cos(angle), math.sin(angle)

    def gather(pair, _):
        pos = []
        for core in range(2):
            n = 2 * pair + core
            tile_x = gx ^ (2 * (pair % 2) + core)
            tile_z = gz ^ (pair // 2)
            rows = [smp_ref[n, t * 8 : t * 8 + 8] for t in range(STEPS)]
            cell = jnp.maximum(rows[0][6:7], 0.0).astype(jnp.int32)
            pz = (cell % size_z + tile_z * size_z).astype(F32) + (0.5 - size_z * tiles_z / 2)
            zs = sincos4(uz * pz)
            lanes = slice(core * LANES, (core + 1) * LANES)
            for f in range(FREQS):
                re = sum(wave(f, t)[0] * rows[t] for t in range(STEPS))
                im = sum(wave(f, t)[1] * rows[t] for t in range(STEPS))
                zsin, zcos = zs[f]
                for k in range(8):
                    sk, ck = zsin[k : k + 1], zcos[k : k + 1]
                    both = jnp.concatenate([re * ck - im * sk, re * sk + im * ck], axis=0)
                    hi, lo = split(both)
                    q, kk = k // 4, k % 4
                    a_ref[pair, f * 2 + q, kk * 16 : kk * 16 + 16, lanes] = hi
                    a_ref[pair, f * 2 + q, 64 + kk * 16 : 80 + kk * 16, lanes] = lo
            gxi = cell // (size_y * size_z) + tile_x * size_x - size_x * tiles_x // 2
            high = ((gxi >> 4) << 4).astype(F32)
            low = (gxi & 15).astype(F32) + 0.5
            py = ((cell // size_z) % size_y).astype(F32) + (0.5 - size_y / 2)
            pos.append(
                jnp.where(row16 < 3, high, jnp.where(row16 < 6, low, jnp.where(row16 < 9, py, 0.0)))
            )
        pos_ref[pair] = jnp.concatenate(pos, axis=1).astype(BF16)
        return 0

    lax.fori_loop(0, 4, gather, 0)
    acc_ref[...] = jnp.zeros_like(acc_ref)

    def table(i, b):
        phase = lax.dot_general(
            pos_ref[i % 4], dir_ref[i // 4], (((0,), (0,)), ((), ())), preferred_element_type=F32
        )
        for j in range(8):
            dst = slice(j * 32, j * 32 + 32)
            values = sincos4(phase[dst])
            for f in range(FREQS):
                for part in range(2):
                    hi, lo = split(values[f][1 - part])
                    th_ref[b * 4 + f, dst, part * LANES : (part + 1) * LANES] = hi
                    tl_ref[b * 4 + f, dst, part * LANES : (part + 1) * LANES] = lo

    def multiply(i, b):
        for f in range(FREQS):
            a = a_ref[i % 4, f * 2 + i // 4]
            o = jnp.dot(a, th_ref[b * 4 + f], preferred_element_type=F32)
            o = o[:64] + o[64:] + jnp.dot(a[:64], tl_ref[b * 4 + f], preferred_element_type=F32)
            acc_ref[i // 4, f] += o

    table(0, 0)
    for k in range(8):
        if k < 7:
            table(k + 1, (k + 1) % 2)
        multiply(k, k % 2)

    near = lane8 % 64 < 32
    sign = jnp.where(near, 1.0, -1.0)

    def finish(i, _):
        q, f = i // 4, i % 4
        for d in range(2):
            res = []
            for pol in range(2):
                r = (d * 2 + pol) * 16
                src = d * 64 + pol * 32
                pq = []
                for part in range(2):
                    for comp in range(2):
                        v = acc_ref[
                            q, f, r + comp * 8 : r + comp * 8 + 8, part * LANES : (part + 1) * LANES
                        ]
                        lo_v = roll(v, (pol * 64 - src) % LANES, 1)
                        hi_v = roll(v, (pol * 64 + 32 - src) % LANES, 1)
                        pq.append(jnp.where(near, lo_v, hi_v))
                pr, pi, qr, qi = pq
                res.append((pr - sign * qi, pi + sign * qr))
            out_ref[2 * q + d, f, 0:8] = jnp.where(lane8 < 64, res[0][0], res[1][0])
            out_ref[2 * q + d, f, 8:16] = jnp.where(lane8 < 64, res[0][1], res[1][1])
        return 0

    lax.fori_loop(0, 8, finish, 0, unroll=2)


def directions(angle):
    theta = math.pi * ((angle // NPHI).astype(F32) + 0.5) / (ANGLES // NPHI)
    phi = 2.0 * math.pi * (angle % NPHI).astype(F32) / NPHI
    return (jnp.sin(theta) * jnp.cos(phi), jnp.sin(theta) * jnp.sin(phi), jnp.cos(theta))


def project(acc_re, acc_im, pos_x, pos_y, pos_z, angle, omegas):
    dir_x, dir_y, dir_z = directions(angle)
    geometry = (
        dir_x[:, None] * pos_x[None] + dir_y[:, None] * pos_y[None] + dir_z[:, None] * pos_z[None]
    )
    phase = omegas[:, None, None] * geometry[None]
    cosine = jnp.cos(phase)
    sine = jnp.sin(phase)
    high = lax.Precision.HIGHEST
    real = jnp.einsum("fas,fcs->fca", cosine, acc_re, precision=high) - jnp.einsum(
        "fas,fcs->fca", sine, acc_im, precision=high
    )
    imag = jnp.einsum("fas,fcs->fca", sine, acc_re, precision=high) + jnp.einsum(
        "fas,fcs->fca", cosine, acc_im, precision=high
    )
    return jnp.concatenate([real, imag], axis=1)


def far_general(samples, cells, owner_table, sizes, tiles_x, tiles_z, scale):
    size_x, size_y, size_z = sizes
    tiles = tiles_x * tiles_z
    sample = samples.reshape(STEPS, 8, LANES)[:, :6]
    omegas = 0.4 * (jnp.arange(FREQS, dtype=F32) + 1.0)
    phase = omegas[:, None] * (DT * (jnp.arange(STEPS, dtype=F32) + 1.0))[None]
    acc_re = jnp.sum(jnp.cos(phase)[:, :, None, None] * sample[None], axis=1)
    acc_im = jnp.sum(jnp.sin(phase)[:, :, None, None] * sample[None], axis=1)
    local = jnp.maximum(cells, 0)
    glob_x = lax.axis_index("gx") * size_x + local // (size_y * size_z)
    glob_y = local // size_z % size_y
    glob_z = lax.axis_index("gz") * size_z + local % size_z
    pos_x = glob_x.astype(F32) + (0.5 - size_x * tiles_x / 2)
    pos_y = glob_y.astype(F32) + (0.5 - size_y / 2)
    pos_z = glob_z.astype(F32) + (0.5 - size_z * tiles_z / 2)
    block_len = ANGLES // tiles
    owners = jnp.arange(tiles, dtype=jnp.int32)
    blocks = jnp.sum(jnp.where(owner_table[None, :] == owners[:, None], owners[None, :], 0), axis=1)
    angle = (blocks[:, None] * block_len + jnp.arange(block_len, dtype=jnp.int32)[None]).reshape(-1)
    pattern = project(acc_re, acc_im, pos_x, pos_y, pos_z, angle, omegas)
    pattern = jnp.transpose(pattern.reshape(FREQS, 12, tiles, block_len), (2, 0, 1, 3))
    return lax.psum_scatter(pattern, ("gx", "gz"), scatter_dimension=0, tiled=True) * scale


VMEM = pl.BlockSpec(memory_space=pltpu.VMEM)
SMEM = pl.BlockSpec(memory_space=pltpu.SMEM)
ANY = pl.BlockSpec(memory_space=pl.ANY)
HBM = pl.BlockSpec(memory_space=pltpu.HBM)


def in_hbm(v):
    return pltpu.with_memory_space_constraint(v, pltpu.HBM)


def shards(nx, nz, e_init, h_init, material, eps_table, sigma_table, face_cells, owner_table):
    size_x, size_y, size_z = material.shape
    ns = 1 if nz == 2 else 2
    plane = (size_y, size_z)
    both = ("gx", "gz")

    def pair_a(i):
        return i ^ 1

    def pair_b(i):
        return i + 1 if i % 2 else i - 1

    def pair_z(k, s):
        return k + 1 if (k + s) % 2 == 0 else k - 1

    xa, xb, zp, zd = pl.pallas_call(
        functools.partial(pack_kernel, ns),
        out_shape=(
            jax.ShapeDtypeStruct((7 * W + 4 * ns,) + plane, F32),
            jax.ShapeDtypeStruct((7 * W,) + plane, F32),
            jax.ShapeDtypeStruct((ns, 8) + plane, F32),
            jax.ShapeDtypeStruct((ns, 4) + plane, F32),
        ),
        in_specs=[ANY] * 3,
        out_specs=(VMEM,) * 4,
        scratch_shapes=[
            pltpu.VMEM((6, size_x) + plane, F32),
            pltpu.VMEM((size_x,) + plane, jnp.int32),
            pltpu.SemaphoreType.DMA((7,)),
        ],
        compiler_params=pltpu.CompilerParams(vmem_limit_bytes=16 * 1024 * 1024),
        name="pack",
    )(in_hbm(e_init), in_hbm(h_init), in_hbm(material))
    xb_in = lax.ppermute(
        xb, "gx", [(i, pair_b(i)) for i in range(nx) if 0 <= pair_b(i) < nx]
    )

    swap = [(i, pair_a(i)) for i in range(nx)]
    xa_in = lax.ppermute(xa, "gx", swap)

    def turned(v, s, pair_x):
        links = [
            (i * nz + k, pair_x(i) * nz + pair_z(k, s))
            for i in range(nx)
            for k in range(nz)
            if 0 <= pair_x(i) < nx and 0 <= pair_z(k, s) < nz
        ]
        return lax.ppermute(v, both, links)

    z_in = []
    for s in range(ns):
        links = [(k, pair_z(k, s)) for k in range(nz) if 0 <= pair_z(k, s) < nz]
        z_in.append(lax.ppermute(zp[s], "gz", links))
    z_in = jnp.stack(z_in)
    za_in = jnp.stack([turned(zd[s], s, pair_a) for s in range(ns)])
    zb_in = jnp.stack([turned(zd[s], s, pair_b) for s in range(ns)])

    wide = size_x + 2 * W
    e_field, h_field, samples = pl.pallas_call(
        functools.partial(field_kernel, ns, nx, nz),
        out_shape=(
            jax.ShapeDtypeStruct((3, size_x * size_y, size_z), F32),
            jax.ShapeDtypeStruct((3, size_x * size_y, size_z), F32),
            jax.ShapeDtypeStruct((8 * STEPS, LANES), F32),
        ),
        in_specs=[VMEM] * 9 + [HBM] * 3,
        out_specs=(ANY, ANY, VMEM),
        scratch_shapes=[
            pltpu.VMEM(((STEPS + 1) * 8 * wide * size_y, LANES), F32),
            pltpu.VMEM((2 * wide * size_y, LANES), F32),
            pltpu.VMEM((STEPS * 2 * 3 * size_y, LANES), F32),
            pltpu.VMEM((8 * 3 * size_y, LANES), F32),
            pltpu.VMEM((2 * 3 * size_y, LANES), F32),
            pltpu.VMEM((4,) + plane, F32),
            pltpu.SMEM((1, eps_table.shape[0]), F32),
            pltpu.SMEM((1, eps_table.shape[0]), F32),
            pltpu.SMEM((1, LANES), jnp.int32),
            pltpu.SemaphoreType.DMA((12,)),
            pltpu.SemaphoreType.DMA((3,)),
        ],
        compiler_params=pltpu.CompilerParams(vmem_limit_bytes=48 * 1024 * 1024),
        name="fields",
    )(
        e_init, h_init, material, xa_in, xb_in, z_in, za_in, zb_in, zp,
        in_hbm(eps_table.reshape(1, -1)), in_hbm(sigma_table.reshape(1, -1)), in_hbm(face_cells),
    )
    e_field = e_field.reshape(e_init.shape)
    h_field = h_field.reshape(h_init.shape)

    tiles = nx * nz
    scale = 1.0 / math.sqrt(tiles * face_cells.shape[1] * STEPS)
    if not (nx == 16 and nz == 2):
        far = far_general(
            samples, face_cells[0], owner_table, material.shape, nx, nz, scale
        )
        return e_field, h_field, far

    def swap_all(v, mx, mz):
        links = [(i * nz + k, (i ^ mx) * nz + (k ^ mz)) for i in range(nx) for k in range(nz)]
        return lax.ppermute(v, both, links)

    mine = jnp.stack([samples, swap_all(samples, 1, 0)])
    by_y = swap_all(mine, 2, 0)
    by_x = swap_all(mine, 0, 1)
    by_xy = swap_all(mine, 2, 1)
    parts = pl.pallas_call(
        functools.partial(project_kernel, size_x, size_y, size_z, nx, nz),
        out_shape=jax.ShapeDtypeStruct((4, FREQS, 16, LANES), F32),
        in_specs=[VMEM] * 4 + [SMEM],
        out_specs=VMEM,
        scratch_shapes=[
            pltpu.SMEM((tiles,), jnp.int32),
            pltpu.VMEM((8, 8 * STEPS, LANES), F32),
            pltpu.VMEM((2, 16, LANES), BF16),
            pltpu.VMEM((4, 16, 2 * LANES), BF16),
            pltpu.VMEM((2 * FREQS, 2 * LANES, 2 * LANES), BF16),
            pltpu.VMEM((2 * FREQS, 2 * LANES, 2 * LANES), BF16),
            pltpu.VMEM((4, FREQS * 2, 128, 2 * LANES), BF16),
            pltpu.VMEM((2, FREQS, 64, 2 * LANES), F32),
        ],
        compiler_params=pltpu.CompilerParams(vmem_limit_bytes=48 * 1024 * 1024),
        name="project",
    )(mine, by_y, by_x, by_xy, owner_table)
    total = parts[0]
    for d in range(1, 4):
        total = total + swap_all(parts[d], 4 * d, 0)
    far = jnp.concatenate([total[:, 0:6], total[:, 8:14]], axis=1) * scale
    return e_field, h_field, far[None]


def solution(mesh):
    nx, nz = mesh.shape["gx"], mesh.shape["gz"]
    return jax.shard_map(
        functools.partial(shards, nx, nz),
        mesh=mesh,
        in_specs=(
            P(None, "gx", None, "gz"),
            P(None, "gx", None, "gz"),
            P("gx", None, "gz"),
            P(),
            P(),
            P(("gx", "gz"), None),
            P(),
        ),
        out_specs=(
            P(None, "gx", None, "gz"),
            P(None, "gx", None, "gz"),
            P(("gx", "gz"), None, None, None),
        ),
        check_vma=False,
    )
```

```python
import functools
import math

import jax
import jax.numpy as jnp
from jax import lax
from jax.experimental import pallas as pl
from jax.experimental.pallas import tpu as pltpu
from jax.sharding import PartitionSpec as P

STEPS = 4
ANGLES = 4096
NPHI = 64
FREQS = 4
DT = 0.5

W = 4
BLOCK = 10
LANES = 128
F32 = jnp.float32
BF16 = jnp.bfloat16


def roll(v, shift, axis):
    return pltpu.roll(v, shift, axis)


def iota(shape, axis):
    return lax.broadcasted_iota(jnp.int32, shape, axis)


def fold_pair(a, b, up, lane):
    own = jnp.where(up, lane, 127 - lane) >= 124
    return jnp.where(own, b, roll(a, jnp.where(up, 124, 4), 1))


def pack_kernel(ns, e_hbm, h_hbm, m_hbm, xa_ref, xb_ref, zp_ref, zd_ref, f_ref, m_ref, sem):
    size_x, size_y = m_ref.shape[0], m_ref.shape[1]
    gx, gz = lax.axis_index("gx"), lax.axis_index("gz")
    copies = [
        pltpu.make_async_copy((e_hbm if c < 3 else h_hbm).at[c % 3], f_ref.at[c], sem.at[c])
        for c in range(6)
    ]
    copies.append(pltpu.make_async_copy(m_hbm, m_ref, sem.at[6]))
    for copy in copies:
        copy.start()
    even = gx % 2 == 0
    lane = iota((size_y, LANES), 1)
    group = lane // 8

    def plane(c, x):
        return f_ref[c, x] if c < 6 else m_ref[x].astype(F32)

    for i in range(4):
        comps = (2 * i, 2 * i + 1) if i < 3 else (6, 6)
        for c in sorted(set(comps)):
            copies[c].wait()
            for ref, off in ((xa_ref, size_x - W), (xb_ref, 0)):
                off = jnp.where(even, off, size_x - W - off)
                for j in range(W):
                    ref[c * W + j] = plane(c, off + j)
        for s in range(ns):
            up = (gz + s) % 2 == 0
            base = jnp.where(up, 8, 0)

            def fold(g, acc):
                out = []
                for q in range(2):
                    x = (g + 28) % 32 if q == 0 else g + 12
                    cell = fold_pair(plane(comps[0], x), plane(comps[1], x), up, lane)
                    cell = roll(cell, (base + 8 * g) % LANES, 1)
                    out.append(jnp.where(group == g, cell, acc[q]))
                return tuple(out)

            zero = jnp.zeros((size_y, LANES), F32)
            acc = lax.fori_loop(0, 16, fold, (zero, zero), unroll=8)
            zp_ref[s, i] = acc[0]
            zp_ref[s, 4 + i] = acc[1]
            xa_ref[7 * W + 4 * s + i] = acc[0]
            zd_ref[s, i] = acc[0]


def coef_tables(eps_ref, sigma_ref, shape):
    lane = iota(shape, 1)
    eps = jnp.ones(shape, F32)
    sigma = jnp.zeros(shape, F32)
    for i in range(eps_ref.shape[1]):
        eps = jnp.where(lane == i, eps_ref[0, i], eps)
        sigma = jnp.where(lane == i, sigma_ref[0, i], sigma)
    loss = sigma * DT / (2.0 * eps)
    return (1.0 - loss) / (1.0 + loss), DT / (eps * (1.0 + loss))


def pick(table, index):
    return jnp.take_along_axis(table, index, axis=1, mode="promise_in_bounds")


def field_kernel(
    ns,
    nx,
    nz,
    e_ref,
    h_ref,
    m_ref,
    xa_ref,
    xb_ref,
    zr_ref,
    za_ref,
    zb_ref,
    zp_ref,
    eps_hbm,
    sigma_hbm,
    cells_hbm,
    eo_ref,
    ho_ref,
    so_ref,
    st_ref,
    co_ref,
    in_ref,
    sp_ref,
    sc_ref,
    qb_ref,
    eps_ref,
    sigma_ref,
    cells_ref,
    sem,
    in_sem,
):
    size_x, size_y = m_ref.shape[0], m_ref.shape[1]
    wide = size_x + 2 * W
    span = wide * size_y
    shape = (size_y, LANES)
    gx, gz = lax.axis_index("gx"), lax.axis_index("gz")
    even = gx % 2 == 0
    lower = gx > 0
    upper = gx < nx - 1
    lane = iota(shape, 1)
    row = iota(shape, 0)
    small = [
        pltpu.make_async_copy(src, dst, in_sem.at[i])
        for i, (src, dst) in enumerate(
            (
                (eps_hbm, eps_ref),
                (sigma_hbm, sigma_ref),
                (cells_hbm, cells_ref),
            )
        )
    ]
    for copy in small:
        copy.start()

    def at(t, c, x):
        return pl.ds(((t * 8 + c) * wide + x) * size_y, size_y)

    def coef_at(c, x):
        return pl.ds((c * wide + x) * size_y, size_y)

    def block(i):
        return pl.ds(i * size_y, size_y)

    pos_a = jnp.where(even, size_x + W, 0)
    pos_b = jnp.where(even, 0, size_x + W)
    ok_b = jnp.where(even, lower, upper).astype(F32)
    sides = ((xa_ref, pos_a, None), (xb_ref, pos_b, ok_b))

    def halo_plane(j, _):
        for ref, pos, _ in sides:
            for c in range(6):
                st_ref[at(0, c, pos + j)] = ref[c * W + j]
        return 0

    lax.fori_loop(0, W, halo_plane, 0, unroll=2)

    group = lane // 8
    first_half = lane % 8 < 4
    fy_keep = row < size_y - 1
    by_keep = row > 0

    def fwd_y(v):
        return jnp.where(fy_keep, roll(v, size_y - 1, 0), 0.0)

    def bwd_y(v):
        return jnp.where(by_keep, roll(v, 1, 0), 0.0)

    def fwd_z(v):
        return roll(v, 127, 1)

    def bwd_z(v):
        return roll(v, 1, 1)

    inside = [
        jnp.where(jnp.logical_and(group < W, jnp.logical_not(lower)), 0.0, 1.0),
        jnp.ones(shape, F32),
        jnp.where(jnp.logical_and(group >= W, jnp.logical_not(upper)), 0.0, 1.0),
    ]
    for s in range(ns):
        up = (gz + s) % 2 == 0
        partner = jnp.where(up, gz + 1, gz - 1)
        ok = jnp.logical_and(partner >= 0, partner < nz)
        give_e = jnp.where(jnp.logical_and(up, ok), 1.0, 0.0)
        give_h = jnp.where(jnp.logical_and(jnp.logical_not(up), ok), 1.0, 0.0)
        base = jnp.where(up, 8, 0)

        def corner(j, acc):
            g = j + jnp.where(even, 0, W)
            comps = [xb_ref[c * W + j] for c in range(7)]
            comps.append(comps[6])
            out = []
            for i in range(4):
                cell = fold_pair(comps[2 * i], comps[2 * i + 1], up, lane)
                cell = roll(cell, (base + 8 * g) % LANES, 1)
                out.append(jnp.where(group == g, cell, acc[i]))
            return tuple(out)

        zero = jnp.zeros(shape, F32)
        acc = lax.fori_loop(0, W, corner, (zero,) * 4, unroll=4)
        for i in range(4):
            qb_ref[i] = acc[i]

        def unfold(i, _):
            def whole(mine, other):
                lo = jnp.where(up, mine, other)
                hi = jnp.where(up, other, mine)
                return (
                    jnp.where(first_half, lo, hi),
                    jnp.where(first_half, roll(lo, 124, 1), roll(hi, 4, 1)),
                )

            q0 = whole(zp_ref[s, i], zr_ref[s, i])
            q1 = whole(zp_ref[s, 4 + i], zr_ref[s, 4 + i])
            qa = whole(xa_ref[7 * W + 4 * s + i], za_ref[s, i])
            qb = whole(qb_ref[i], zb_ref[s, i])
            for k in range(2):
                below = jnp.where(even, qb[k], qa[k])
                above = jnp.where(even, qa[k], qb[k])
                c = (2 * i + k) * 3
                sp_ref[block(c)] = jnp.where(group < W, below, q0[k])
                sp_ref[block(c + 1)] = q1[k]
                sp_ref[block(c + 2)] = jnp.where(group < W, q0[k], above)
            return 0

        lax.fori_loop(0, 4, unfold, 0, unroll=4)
        if s == 0:
            for copy in small:
                copy.wait()
            ca_t, cb_t = coef_tables(eps_ref, sigma_ref, shape)

            def halo_coef(j, _):
                for ref, pos, ok_side in sides:
                    index = ref[6 * W + j].astype(jnp.int32)
                    ca, cb = pick(ca_t, index), pick(cb_t, index)
                    if ok_side is not None:
                        ca, cb = ca * ok_side, cb * ok_side
                    co_ref[coef_at(0, pos + j)] = ca
                    co_ref[coef_at(1, pos + j)] = cb
                return 0

            lax.fori_loop(0, W, halo_coef, 0, unroll=4)
        for q in range(3):
            index = sp_ref[block(18 + q)].astype(jnp.int32)
            sc_ref[block(q)] = pick(ca_t, index) * inside[q]
            sc_ref[block(3 + q)] = pick(cb_t, index) * inside[q]

        def fwd_x(v):
            r = [roll(u, 120, 1) for u in v]
            return [jnp.where(lane < 120, r[0], r[1]), jnp.where(lane < 120, r[1], r[2]), r[2]]

        def bwd_x(v):
            r = [roll(u, 8, 1) for u in v]
            return [r[0], jnp.where(lane >= 8, r[1], r[0]), jnp.where(lane >= 8, r[2], r[1])]

        def each(f, *vs):
            return [f(*u) for u in zip(*vs)]

        def own_planes(t):
            for j in range(size_x // STEPS):
                x = t * (size_x // STEPS) + j
                for c in range(3):
                    st_ref[at(0, c, x + W)] = e_ref[c, x]
                    st_ref[at(0, 3 + c, x + W)] = h_ref[c, x]
                index = m_ref[x]
                co_ref[coef_at(0, x + W)] = pick(ca_t, index)
                co_ref[coef_at(1, x + W)] = pick(cb_t, index)

        def strip_step(t, _):
            ex, ey, ez, hx, hy, hz = (
                [sp_ref[block(c * 3 + q)] for q in range(3)] for c in range(6)
            )
            ca_s = [sc_ref[block(q)] for q in range(3)]
            cb_s = [sc_ref[block(3 + q)] for q in range(3)]
            dt_s = [DT * k for k in inside]
            side_e = [[v * give_e for v in ex], [v * give_e for v in ey]]
            ez_x, ey_x = fwd_x(ez), fwd_x(ey)
            hx = each(
                lambda h, z, y, d: h - d * ((fwd_y(z) - z) - (fwd_z(y) - y)), hx, ez, ey, dt_s
            )
            hy = each(
                lambda h, x, z, zx, d: h - d * ((fwd_z(x) - x) - (zx - z)), hy, ex, ez, ez_x, dt_s
            )
            hz = each(
                lambda h, y, yx, x, d: h - d * ((yx - y) - (fwd_y(x) - x)), hz, ey, ey_x, ex, dt_s
            )
            if s == 0:
                own_planes(t)
            hz_x, hy_x = bwd_x(hz), bwd_x(hy)
            ex = each(
                lambda e, z, y, a, b: a * e + b * ((z - bwd_y(z)) - (y - bwd_z(y))),
                ex, hz, hy, ca_s, cb_s,
            )
            ey = each(
                lambda e, x, z, zx, a, b: a * e + b * ((x - bwd_z(x)) - (z - zx)),
                ey, hx, hz, hz_x, ca_s, cb_s,
            )
            ez = each(
                lambda e, y, yx, x, a, b: a * e + b * ((y - yx) - (x - bwd_y(x))),
                ez, hy, hy_x, hx, ca_s, cb_s,
            )
            for c, v in enumerate((ex, ey, ez, hx, hy, hz)):
                for q in range(3):
                    sp_ref[block(c * 3 + q)] = v[q]
            for j, v in enumerate((hx, hy)):
                for q in range(3):
                    dst = block((t * 2 + j) * 3 + q)
                    add = jnp.where(lane % 8 == 4, side_e[j][q], roll(v[q] * give_h, 2, 1))
                    in_ref[dst] = add if s == 0 else in_ref[dst] + add
            return 0

        lax.fori_loop(0, STEPS, strip_step, 0)

    dt_lo = jnp.where(lower, DT, 0.0)
    dt_hi = jnp.where(upper, DT, 0.0)

    planes = range(BLOCK)

    def advance(t, x, carry):
        hy_p, hz_p = carry
        old = [[st_ref[at(t - 1, c, x + i)] for i in range(BLOCK + (c < 3))] for c in range(6)]
        ca = [co_ref[coef_at(0, x + i)] for i in planes]
        cb = [co_ref[coef_at(1, x + i)] for i in planes]
        ex, ey, ez, hx, hy, hz = old
        side_x, side_y = [], []
        for i in planes:
            shift = (123 - 8 * ((x + i) % 16)) % LANES
            side_x.append(roll(in_ref[block((t - 1) * 6 + (x + i) // 16)], shift, 1))
            side_y.append(roll(in_ref[block((t - 1) * 6 + 3 + (x + i) // 16)], shift, 1))
        ex_z = [jnp.where(last, side_x[i], fwd_z(ex[i])) for i in planes]
        ey_z = [jnp.where(last, side_y[i], fwd_z(ey[i])) for i in planes]
        ez_y = [fwd_y(ez[i]) for i in planes]
        ex_y = [fwd_y(ex[i]) for i in planes]
        dt = [
            jnp.where(x + i < W, dt_lo, jnp.where(x + i >= size_x + W, dt_hi, DT)) for i in planes
        ]
        hx = [hx[i] - dt[i] * ((ez_y[i] - ez[i]) - (ey_z[i] - ey[i])) for i in planes]
        hy = [hy[i] - dt[i] * ((ex_z[i] - ex[i]) - (ez[i + 1] - ez[i])) for i in planes]
        hz = [hz[i] - dt[i] * ((ey[i + 1] - ey[i]) - (ex_y[i] - ex[i])) for i in planes]
        hx_z = [jnp.where(first, side_x[i], bwd_z(hx[i])) for i in planes]
        hy_z = [jnp.where(first, side_y[i], bwd_z(hy[i])) for i in planes]
        hy_x, hz_x = [hy_p] + hy, [hz_p] + hz
        new = [
            [ca[i] * ex[i] + cb[i] * ((hz[i] - bwd_y(hz[i])) - (hy[i] - hy_z[i])) for i in planes],
            [ca[i] * ey[i] + cb[i] * ((hx[i] - hx_z[i]) - (hz[i] - hz_x[i])) for i in planes],
            [ca[i] * ez[i] + cb[i] * ((hy[i] - hy_x[i]) - (hx[i] - bwd_y(hx[i]))) for i in planes],
            hx, hy, hz,
        ]
        for c in range(6):
            for i in planes:
                st_ref[at(t, c, x + i)] = new[c][i]
        return hy[-1], hz[-1]

    last, first = lane == 127, lane == 0

    half = size_x // 2
    copies = []
    for part in range(2):
        copies.append([])
        for c in range(3):
            for ref, cc in ((eo_ref, c), (ho_ref, 3 + c)):
                src = ((STEPS * 8 + cc) * wide + W + part * half) * size_y
                copies[part].append(
                    pltpu.make_async_copy(
                        st_ref.at[pl.ds(src, half * size_y)],
                        ref.at[c, pl.ds(part * half * size_y, half * size_y)],
                        sem.at[part * 6 + cc],
                    )
                )
    blocks = wide // BLOCK
    def step(t, _):
        zero = jnp.zeros(shape, F32)

        def planes_from(i, c):
            c = advance(t, i * BLOCK, c)

            @pl.when(jnp.logical_and(t == STEPS, i == blocks // 2 - 1 + blocks % 2))
            def _():
                for copy in copies[0]:
                    copy.start()

            return c

        lax.fori_loop(0, blocks, planes_from, (zero, zero))
        return 0

    lax.fori_loop(1, STEPS + 1, step, 0)
    for copy in copies[1]:
        copy.start()

    rows = 6
    lane8 = iota((rows, LANES), 1)
    zero8 = jnp.zeros((rows, LANES), F32)

    def slot(m, accs):
        cell = cells_ref[0, m]
        here = lane8 == m
        found = lane8 == jnp.where(cell >= 0, m, -1)
        numbers = jnp.where(here[:2], cell.astype(F32), accs[STEPS])
        cell = jnp.maximum(cell, 0)
        out = []
        for t in range(STEPS):
            start = (t + 1) * 8 * span + W * size_y + (cell >> 7)
            v = st_ref[pl.ds(start, rows, stride=span), :]
            out.append(jnp.where(found, roll(v, (m - cell) & 127, 1), accs[t]))
        return tuple(out) + (numbers,)

    zero2 = jnp.zeros((2, LANES), F32)
    accs = lax.fori_loop(0, LANES, slot, (zero8,) * STEPS + (zero2,), unroll=32)
    for t in range(STEPS):
        so_ref[t * 8 : t * 8 + 6] = accs[t][:6]
        so_ref[t * 8 + 6 : t * 8 + 8] = accs[STEPS] if t == 0 else zero2
    for copy in copies[0] + copies[1]:
        copy.wait()


SIN_C = (3.1415926401307077, -5.167710083507896, 2.550077523214726, -0.5982912856213906, 0.07765766030763246)
COS_C = (0.9999999532476085, -4.934792830619649, 4.058411352862754, -1.3318765680819573, 0.21968961109991972)
ROUND = 12582912.0


def horner(coefs, u):
    v = u * coefs[-1] + coefs[-2]
    for k in coefs[-3::-1]:
        v = v * u + k
    return v


def sincos4(turns):
    r = turns - ((turns + ROUND) - ROUND)
    u = r * r
    half_s = horner(SIN_C, u) * r
    half_c = horner(COS_C, u)
    twice = half_s + half_s
    s = twice * half_c
    c = 1.0 - twice * half_s
    s_2, c_2 = s + s, c + c
    s2 = s_2 * c
    c2 = 1.0 - s_2 * s
    s3 = c_2 * s2 - s
    c3 = c_2 * c2 - c
    s2_2 = s2 + s2
    return (s, c), (s2, c2), (s3, c3), (s2_2 * c2, 1.0 - s2_2 * s2)


def sincos(turns):
    return sincos4(turns)[0]


def split(v):
    hi = v.astype(BF16)
    return hi, (v - hi.astype(F32)).astype(BF16)


def project_kernel(
    size_x, size_y, size_z, tiles_x, tiles_z, own_ref, r1_ref, r2_ref, r3_ref, owner_ref, out_ref,
    inv_ref, smp_ref, dir_ref, pos_ref, th_ref, tl_ref, a_ref, acc_ref,
):
    gx, gz = lax.axis_index("gx"), lax.axis_index("gz")
    tiles = tiles_x * tiles_z
    base = 0.4 / (2.0 * math.pi)
    polars = ANGLES // NPHI

    def put(b, _):
        inv_ref[owner_ref[b]] = b
        return 0

    lax.fori_loop(0, tiles, put, 0, unroll=8)
    blocks = [inv_ref[(gx ^ (4 * d)) * tiles_z + gz] for d in range(4)]

    for i, ref in enumerate((own_ref, r1_ref, r2_ref, r3_ref)):
        for core in range(2):
            smp_ref[2 * i + core] = ref[core]
    row16 = iota((16, LANES), 0)
    lane16 = iota((16, LANES), 1)
    row8 = iota((8, LANES), 0)
    lane8 = iota((8, LANES), 1)

    def split3(v):
        a = v.astype(BF16).astype(F32)
        b = (v - a).astype(BF16).astype(F32)
        return a, b, v - a - b

    for q in range(2):
        block = jnp.where(lane16 < 64, blocks[2 * q], blocks[2 * q + 1])
        polar = 2 * block + (lane16 % 64) // 32
        st, _ = sincos((polar.astype(F32) + 0.5) * (0.5 / polars))
        sp, cp = sincos((lane16 % 32).astype(F32) * (1.0 / NPHI))
        ux = split3(base * st * cp)
        uy = split3(base * st * sp)
        mat = jnp.zeros((16, LANES), F32)
        for k in range(9):
            src = ux[k % 3] if k < 6 else uy[k % 3]
            mat = jnp.where(row16 == k, src, mat)
        dir_ref[q] = mat.astype(BF16)
    combo = jnp.zeros((8, LANES), jnp.int32)
    for d in range(4):
        combo = jnp.where(row8 // 2 == d, 2 * blocks[d] + row8 % 2, combo)
    _, uz = sincos((combo.astype(F32) + 0.5) * (0.5 / polars))
    uz = uz * base

    def wave(f, t):
        angle = 0.4 * (f + 1) * DT * (t + 1)
        return math.cos(angle), math.sin(angle)

    def gather(pair, _):
        pos = []
        for core in range(2):
            n = 2 * pair + core
            tile_x = gx ^ (2 * (pair % 2) + core)
            tile_z = gz ^ (pair // 2)
            rows = [smp_ref[n, t * 8 : t * 8 + 8] for t in range(STEPS)]
            cell = jnp.maximum(rows[0][6:7], 0.0).astype(jnp.int32)
            pz = (cell % size_z + tile_z * size_z).astype(F32) + (0.5 - size_z * tiles_z / 2)
            zs = sincos4(uz * pz)
            lanes = slice(core * LANES, (core + 1) * LANES)
            for f in range(FREQS):
                re = sum(wave(f, t)[0] * rows[t] for t in range(STEPS))
                im = sum(wave(f, t)[1] * rows[t] for t in range(STEPS))
                zsin, zcos = zs[f]
                for k in range(8):
                    sk, ck = zsin[k : k + 1], zcos[k : k + 1]
                    both = jnp.concatenate([re * ck - im * sk, re * sk + im * ck], axis=0)
                    hi, lo = split(both)
                    q, kk = k // 4, k % 4
                    a_ref[pair, f * 2 + q, kk * 16 : kk * 16 + 16, lanes] = hi
                    a_ref[pair, f * 2 + q, 64 + kk * 16 : 80 + kk * 16, lanes] = lo
            gxi = cell // (size_y * size_z) + tile_x * size_x - size_x * tiles_x // 2
            high = ((gxi >> 4) << 4).astype(F32)
            low = (gxi & 15).astype(F32) + 0.5
            py = ((cell // size_z) % size_y).astype(F32) + (0.5 - size_y / 2)
            pos.append(
                jnp.where(row16 < 3, high, jnp.where(row16 < 6, low, jnp.where(row16 < 9, py, 0.0)))
            )
        pos_ref[pair] = jnp.concatenate(pos, axis=1).astype(BF16)
        return 0

    lax.fori_loop(0, 4, gather, 0)
    acc_ref[...] = jnp.zeros_like(acc_ref)

    def table(i, b):
        phase = lax.dot_general(
            pos_ref[i % 4], dir_ref[i // 4], (((0,), (0,)), ((), ())), preferred_element_type=F32
        )
        for j in range(8):
            dst = slice(j * 32, j * 32 + 32)
            values = sincos4(phase[dst])
            for f in range(FREQS):
                for part in range(2):
                    hi, lo = split(values[f][1 - part])
                    th_ref[b * 4 + f, dst, part * LANES : (part + 1) * LANES] = hi
                    tl_ref[b * 4 + f, dst, part * LANES : (part + 1) * LANES] = lo

    def multiply(i, b):
        for f in range(FREQS):
            a = a_ref[i % 4, f * 2 + i // 4]
            o = jnp.dot(a, th_ref[b * 4 + f], preferred_element_type=F32)
            o = o[:64] + o[64:] + jnp.dot(a[:64], tl_ref[b * 4 + f], preferred_element_type=F32)
            acc_ref[i // 4, f] += o

    table(0, 0)
    for k in range(8):
        if k < 7:
            table(k + 1, (k + 1) % 2)
        multiply(k, k % 2)

    near = lane8 % 64 < 32
    sign = jnp.where(near, 1.0, -1.0)

    def finish(i, _):
        q, f = i // 4, i % 4
        for d in range(2):
            res = []
            for pol in range(2):
                r = (d * 2 + pol) * 16
                src = d * 64 + pol * 32
                pq = []
                for part in range(2):
                    for comp in range(2):
                        v = acc_ref[
                            q, f, r + comp * 8 : r + comp * 8 + 8, part * LANES : (part + 1) * LANES
                        ]
                        lo_v = roll(v, (pol * 64 - src) % LANES, 1)
                        hi_v = roll(v, (pol * 64 + 32 - src) % LANES, 1)
                        pq.append(jnp.where(near, lo_v, hi_v))
                pr, pi, qr, qi = pq
                res.append((pr - sign * qi, pi + sign * qr))
            out_ref[2 * q + d, f, 0:8] = jnp.where(lane8 < 64, res[0][0], res[1][0])
            out_ref[2 * q + d, f, 8:16] = jnp.where(lane8 < 64, res[0][1], res[1][1])
        return 0

    lax.fori_loop(0, 8, finish, 0, unroll=2)


def directions(angle):
    theta = math.pi * ((angle // NPHI).astype(F32) + 0.5) / (ANGLES // NPHI)
    phi = 2.0 * math.pi * (angle % NPHI).astype(F32) / NPHI
    return (jnp.sin(theta) * jnp.cos(phi), jnp.sin(theta) * jnp.sin(phi), jnp.cos(theta))


def project(acc_re, acc_im, pos_x, pos_y, pos_z, angle, omegas):
    dir_x, dir_y, dir_z = directions(angle)
    geometry = (
        dir_x[:, None] * pos_x[None] + dir_y[:, None] * pos_y[None] + dir_z[:, None] * pos_z[None]
    )
    phase = omegas[:, None, None] * geometry[None]
    cosine = jnp.cos(phase)
    sine = jnp.sin(phase)
    high = lax.Precision.HIGHEST
    real = jnp.einsum("fas,fcs->fca", cosine, acc_re, precision=high) - jnp.einsum(
        "fas,fcs->fca", sine, acc_im, precision=high
    )
    imag = jnp.einsum("fas,fcs->fca", sine, acc_re, precision=high) + jnp.einsum(
        "fas,fcs->fca", cosine, acc_im, precision=high
    )
    return jnp.concatenate([real, imag], axis=1)


def far_general(samples, cells, owner_table, sizes, tiles_x, tiles_z, scale):
    size_x, size_y, size_z = sizes
    tiles = tiles_x * tiles_z
    sample = samples.reshape(STEPS, 8, LANES)[:, :6]
    omegas = 0.4 * (jnp.arange(FREQS, dtype=F32) + 1.0)
    phase = omegas[:, None] * (DT * (jnp.arange(STEPS, dtype=F32) + 1.0))[None]
    acc_re = jnp.sum(jnp.cos(phase)[:, :, None, None] * sample[None], axis=1)
    acc_im = jnp.sum(jnp.sin(phase)[:, :, None, None] * sample[None], axis=1)
    local = jnp.maximum(cells, 0)
    glob_x = lax.axis_index("gx") * size_x + local // (size_y * size_z)
    glob_y = local // size_z % size_y
    glob_z = lax.axis_index("gz") * size_z + local % size_z
    pos_x = glob_x.astype(F32) + (0.5 - size_x * tiles_x / 2)
    pos_y = glob_y.astype(F32) + (0.5 - size_y / 2)
    pos_z = glob_z.astype(F32) + (0.5 - size_z * tiles_z / 2)
    block_len = ANGLES // tiles
    owners = jnp.arange(tiles, dtype=jnp.int32)
    blocks = jnp.sum(jnp.where(owner_table[None, :] == owners[:, None], owners[None, :], 0), axis=1)
    angle = (blocks[:, None] * block_len + jnp.arange(block_len, dtype=jnp.int32)[None]).reshape(-1)
    pattern = project(acc_re, acc_im, pos_x, pos_y, pos_z, angle, omegas)
    pattern = jnp.transpose(pattern.reshape(FREQS, 12, tiles, block_len), (2, 0, 1, 3))
    return lax.psum_scatter(pattern, ("gx", "gz"), scatter_dimension=0, tiled=True) * scale


VMEM = pl.BlockSpec(memory_space=pltpu.VMEM)
SMEM = pl.BlockSpec(memory_space=pltpu.SMEM)
ANY = pl.BlockSpec(memory_space=pl.ANY)
HBM = pl.BlockSpec(memory_space=pltpu.HBM)


def in_hbm(v):
    return pltpu.with_memory_space_constraint(v, pltpu.HBM)


def shards(nx, nz, e_init, h_init, material, eps_table, sigma_table, face_cells, owner_table):
    size_x, size_y, size_z = material.shape
    ns = 1 if nz == 2 else 2
    plane = (size_y, size_z)
    both = ("gx", "gz")

    def pair_a(i):
        return i ^ 1

    def pair_b(i):
        return i + 1 if i % 2 else i - 1

    def pair_z(k, s):
        return k + 1 if (k + s) % 2 == 0 else k - 1

    xa, xb, zp, zd = pl.pallas_call(
        functools.partial(pack_kernel, ns),
        out_shape=(
            jax.ShapeDtypeStruct((7 * W + 4 * ns,) + plane, F32),
            jax.ShapeDtypeStruct((7 * W,) + plane, F32),
            jax.ShapeDtypeStruct((ns, 8) + plane, F32),
            jax.ShapeDtypeStruct((ns, 4) + plane, F32),
        ),
        in_specs=[ANY] * 3,
        out_specs=(VMEM,) * 4,
        scratch_shapes=[
            pltpu.VMEM((6, size_x) + plane, F32),
            pltpu.VMEM((size_x,) + plane, jnp.int32),
            pltpu.SemaphoreType.DMA((7,)),
        ],
        compiler_params=pltpu.CompilerParams(vmem_limit_bytes=16 * 1024 * 1024),
        name="pack",
    )(in_hbm(e_init), in_hbm(h_init), in_hbm(material))
    xb_in = lax.ppermute(
        xb, "gx", [(i, pair_b(i)) for i in range(nx) if 0 <= pair_b(i) < nx]
    )

    swap = [(i, pair_a(i)) for i in range(nx)]
    xa_in = lax.ppermute(xa, "gx", swap)

    def turned(v, s, pair_x):
        links = [
            (i * nz + k, pair_x(i) * nz + pair_z(k, s))
            for i in range(nx)
            for k in range(nz)
            if 0 <= pair_x(i) < nx and 0 <= pair_z(k, s) < nz
        ]
        return lax.ppermute(v, both, links)

    z_in = []
    for s in range(ns):
        links = [(k, pair_z(k, s)) for k in range(nz) if 0 <= pair_z(k, s) < nz]
        z_in.append(lax.ppermute(zp[s], "gz", links))
    z_in = jnp.stack(z_in)
    za_in = jnp.stack([turned(zd[s], s, pair_a) for s in range(ns)])
    zb_in = jnp.stack([turned(zd[s], s, pair_b) for s in range(ns)])

    wide = size_x + 2 * W
    e_field, h_field, samples = pl.pallas_call(
        functools.partial(field_kernel, ns, nx, nz),
        out_shape=(
            jax.ShapeDtypeStruct((3, size_x * size_y, size_z), F32),
            jax.ShapeDtypeStruct((3, size_x * size_y, size_z), F32),
            jax.ShapeDtypeStruct((8 * STEPS, LANES), F32),
        ),
        in_specs=[VMEM] * 9 + [HBM] * 3,
        out_specs=(ANY, ANY, VMEM),
        scratch_shapes=[
            pltpu.VMEM(((STEPS + 1) * 8 * wide * size_y, LANES), F32),
            pltpu.VMEM((2 * wide * size_y, LANES), F32),
            pltpu.VMEM((STEPS * 2 * 3 * size_y, LANES), F32),
            pltpu.VMEM((8 * 3 * size_y, LANES), F32),
            pltpu.VMEM((2 * 3 * size_y, LANES), F32),
            pltpu.VMEM((4,) + plane, F32),
            pltpu.SMEM((1, eps_table.shape[0]), F32),
            pltpu.SMEM((1, eps_table.shape[0]), F32),
            pltpu.SMEM((1, LANES), jnp.int32),
            pltpu.SemaphoreType.DMA((12,)),
            pltpu.SemaphoreType.DMA((3,)),
        ],
        compiler_params=pltpu.CompilerParams(vmem_limit_bytes=48 * 1024 * 1024),
        name="fields",
    )(
        e_init, h_init, material, xa_in, xb_in, z_in, za_in, zb_in, zp,
        in_hbm(eps_table.reshape(1, -1)), in_hbm(sigma_table.reshape(1, -1)), in_hbm(face_cells),
    )
    e_field = e_field.reshape(e_init.shape)
    h_field = h_field.reshape(h_init.shape)

    tiles = nx * nz
    scale = 1.0 / math.sqrt(tiles * face_cells.shape[1] * STEPS)
    if not (nx == 16 and nz == 2):
        far = far_general(
            samples, face_cells[0], owner_table, material.shape, nx, nz, scale
        )
        return e_field, h_field, far

    def swap_all(v, mx, mz):
        links = [(i * nz + k, (i ^ mx) * nz + (k ^ mz)) for i in range(nx) for k in range(nz)]
        return lax.ppermute(v, both, links)

    mine = jnp.stack([samples, swap_all(samples, 1, 0)])
    by_y = swap_all(mine, 2, 0)
    by_x = swap_all(mine, 0, 1)
    by_xy = swap_all(mine, 2, 1)
    parts = pl.pallas_call(
        functools.partial(project_kernel, size_x, size_y, size_z, nx, nz),
        out_shape=jax.ShapeDtypeStruct((4, FREQS, 16, LANES), F32),
        in_specs=[VMEM] * 4 + [SMEM],
        out_specs=VMEM,
        scratch_shapes=[
            pltpu.SMEM((tiles,), jnp.int32),
            pltpu.VMEM((8, 8 * STEPS, LANES), F32),
            pltpu.VMEM((2, 16, LANES), BF16),
            pltpu.VMEM((4, 16, 2 * LANES), BF16),
            pltpu.VMEM((2 * FREQS, 2 * LANES, 2 * LANES), BF16),
            pltpu.VMEM((2 * FREQS, 2 * LANES, 2 * LANES), BF16),
            pltpu.VMEM((4, FREQS * 2, 128, 2 * LANES), BF16),
            pltpu.VMEM((2, FREQS, 64, 2 * LANES), F32),
        ],
        compiler_params=pltpu.CompilerParams(vmem_limit_bytes=48 * 1024 * 1024),
        name="project",
    )(mine, by_y, by_x, by_xy, owner_table)
    total = parts[0]
    for d in range(1, 4):
        total = total + swap_all(parts[d], 4 * d, 0)
    far = jnp.concatenate([total[:, 0:6], total[:, 8:14]], axis=1) * scale
    return e_field, h_field, far[None]


def solution(mesh):
    nx, nz = mesh.shape["gx"], mesh.shape["gz"]
    return jax.shard_map(
        functools.partial(shards, nx, nz),
        mesh=mesh,
        in_specs=(
            P(None, "gx", None, "gz"),
            P(None, "gx", None, "gz"),
            P("gx", None, "gz"),
            P(),
            P(),
            P(("gx", "gz"), None),
            P(),
        ),
        out_specs=(
            P(None, "gx", None, "gz"),
            P(None, "gx", None, "gz"),
            P(("gx", "gz"), None, None, None),
        ),
        check_vma=False,
    )
```

```python
import functools
import math

import jax
import jax.numpy as jnp
from jax import lax
from jax.experimental import pallas as pl
from jax.experimental.pallas import tpu as pltpu
from jax.sharding import PartitionSpec as P

STEPS = 4
ANGLES = 4096
NPHI = 64
FREQS = 4
DT = 0.5

W = 4
BLOCK = 10
LANES = 128
F32 = jnp.float32
BF16 = jnp.bfloat16


def roll(v, shift, axis):
    return pltpu.roll(v, shift, axis)


def iota(shape, axis):
    return lax.broadcasted_iota(jnp.int32, shape, axis)


def fold_pair(a, b, up, lane):
    own = jnp.where(up, lane, 127 - lane) >= 124
    return jnp.where(own, b, roll(a, jnp.where(up, 124, 4), 1))


def pack_kernel(ns, e_hbm, h_hbm, m_hbm, xa_ref, xb_ref, zp_ref, zd_ref, f_ref, m_ref, sem):
    size_x, size_y = m_ref.shape[0], m_ref.shape[1]
    gx, gz = lax.axis_index("gx"), lax.axis_index("gz")
    copies = [
        pltpu.make_async_copy((e_hbm if c < 3 else h_hbm).at[c % 3], f_ref.at[c], sem.at[c])
        for c in range(6)
    ]
    copies.append(pltpu.make_async_copy(m_hbm, m_ref, sem.at[6]))
    for copy in copies:
        copy.start()
    even = gx % 2 == 0
    lane = iota((size_y, LANES), 1)
    group = lane // 8

    def plane(c, x):
        return f_ref[c, x] if c < 6 else m_ref[x].astype(F32)

    for i in range(4):
        comps = (2 * i, 2 * i + 1) if i < 3 else (6, 6)
        for c in sorted(set(comps)):
            copies[c].wait()
            for ref, off in ((xa_ref, size_x - W), (xb_ref, 0)):
                off = jnp.where(even, off, size_x - W - off)
                for j in range(W):
                    ref[c * W + j] = plane(c, off + j)
        for s in range(ns):
            up = (gz + s) % 2 == 0
            base = jnp.where(up, 8, 0)

            def fold(g, acc):
                out = []
                for q in range(2):
                    x = (g + 28) % 32 if q == 0 else g + 12
                    cell = fold_pair(plane(comps[0], x), plane(comps[1], x), up, lane)
                    cell = roll(cell, (base + 8 * g) % LANES, 1)
                    out.append(jnp.where(group == g, cell, acc[q]))
                return tuple(out)

            zero = jnp.zeros((size_y, LANES), F32)
            acc = lax.fori_loop(0, 16, fold, (zero, zero), unroll=8)
            zp_ref[s, i] = acc[0]
            zp_ref[s, 4 + i] = acc[1]
            xa_ref[7 * W + 4 * s + i] = acc[0]
            zd_ref[s, i] = acc[0]


def coef_tables(eps_ref, sigma_ref, shape):
    lane = iota(shape, 1)
    eps = jnp.ones(shape, F32)
    sigma = jnp.zeros(shape, F32)
    for i in range(eps_ref.shape[1]):
        eps = jnp.where(lane == i, eps_ref[0, i], eps)
        sigma = jnp.where(lane == i, sigma_ref[0, i], sigma)
    loss = sigma * DT / (2.0 * eps)
    return (1.0 - loss) / (1.0 + loss), DT / (eps * (1.0 + loss))


def pick(table, index):
    return jnp.take_along_axis(table, index, axis=1, mode="promise_in_bounds")


def field_kernel(
    ns,
    nx,
    nz,
    e_ref,
    h_ref,
    m_ref,
    xa_ref,
    xb_ref,
    zr_ref,
    za_ref,
    zb_ref,
    zp_ref,
    eps_hbm,
    sigma_hbm,
    cells_hbm,
    eo_ref,
    ho_ref,
    so_ref,
    st_ref,
    co_ref,
    in_ref,
    sp_ref,
    sc_ref,
    qb_ref,
    eps_ref,
    sigma_ref,
    cells_ref,
    sem,
    in_sem,
):
    size_x, size_y = m_ref.shape[0], m_ref.shape[1]
    wide = size_x + 2 * W
    span = wide * size_y
    shape = (size_y, LANES)
    gx, gz = lax.axis_index("gx"), lax.axis_index("gz")
    even = gx % 2 == 0
    lower = gx > 0
    upper = gx < nx - 1
    lane = iota(shape, 1)
    row = iota(shape, 0)
    small = [
        pltpu.make_async_copy(src, dst, in_sem.at[i])
        for i, (src, dst) in enumerate(
            (
                (eps_hbm, eps_ref),
                (sigma_hbm, sigma_ref),
                (cells_hbm, cells_ref),
            )
        )
    ]
    for copy in small:
        copy.start()

    def at(t, c, x):
        return pl.ds(((t * 8 + c) * wide + x) * size_y, size_y)

    def coef_at(c, x):
        return pl.ds((c * wide + x) * size_y, size_y)

    def block(i):
        return pl.ds(i * size_y, size_y)

    pos_a = jnp.where(even, size_x + W, 0)
    pos_b = jnp.where(even, 0, size_x + W)
    ok_b = jnp.where(even, lower, upper).astype(F32)
    sides = ((xa_ref, pos_a, None), (xb_ref, pos_b, ok_b))

    def halo_plane(j, _):
        for ref, pos, _ in sides:
            for c in range(6):
                st_ref[at(0, c, pos + j)] = ref[c * W + j]
        return 0

    lax.fori_loop(0, W, halo_plane, 0, unroll=2)

    group = lane // 8
    first_half = lane % 8 < 4
    fy_keep = row < size_y - 1
    by_keep = row > 0

    def fwd_y(v):
        return jnp.where(fy_keep, roll(v, size_y - 1, 0), 0.0)

    def bwd_y(v):
        return jnp.where(by_keep, roll(v, 1, 0), 0.0)

    def fwd_z(v):
        return roll(v, 127, 1)

    def bwd_z(v):
        return roll(v, 1, 1)

    inside = [
        jnp.where(jnp.logical_and(group < W, jnp.logical_not(lower)), 0.0, 1.0),
        jnp.ones(shape, F32),
        jnp.where(jnp.logical_and(group >= W, jnp.logical_not(upper)), 0.0, 1.0),
    ]
    for s in range(ns):
        up = (gz + s) % 2 == 0
        partner = jnp.where(up, gz + 1, gz - 1)
        ok = jnp.logical_and(partner >= 0, partner < nz)
        give_e = jnp.where(jnp.logical_and(up, ok), 1.0, 0.0)
        give_h = jnp.where(jnp.logical_and(jnp.logical_not(up), ok), 1.0, 0.0)
        base = jnp.where(up, 8, 0)

        def corner(j, acc):
            g = j + jnp.where(even, 0, W)
            comps = [xb_ref[c * W + j] for c in range(7)]
            comps.append(comps[6])
            out = []
            for i in range(4):
                cell = fold_pair(comps[2 * i], comps[2 * i + 1], up, lane)
                cell = roll(cell, (base + 8 * g) % LANES, 1)
                out.append(jnp.where(group == g, cell, acc[i]))
            return tuple(out)

        zero = jnp.zeros(shape, F32)
        acc = lax.fori_loop(0, W, corner, (zero,) * 4, unroll=4)
        for i in range(4):
            qb_ref[i] = acc[i]

        def unfold(i, _):
            def whole(mine, other):
                lo = jnp.where(up, mine, other)
                hi = jnp.where(up, other, mine)
                return (
                    jnp.where(first_half, lo, hi),
                    jnp.where(first_half, roll(lo, 124, 1), roll(hi, 4, 1)),
                )

            q0 = whole(zp_ref[s, i], zr_ref[s, i])
            q1 = whole(zp_ref[s, 4 + i], zr_ref[s, 4 + i])
            qa = whole(xa_ref[7 * W + 4 * s + i], za_ref[s, i])
            qb = whole(qb_ref[i], zb_ref[s, i])
            for k in range(2):
                below = jnp.where(even, qb[k], qa[k])
                above = jnp.where(even, qa[k], qb[k])
                c = (2 * i + k) * 3
                sp_ref[block(c)] = jnp.where(group < W, below, q0[k])
                sp_ref[block(c + 1)] = q1[k]
                sp_ref[block(c + 2)] = jnp.where(group < W, q0[k], above)
            return 0

        lax.fori_loop(0, 4, unfold, 0, unroll=4)
        if s == 0:
            for copy in small:
                copy.wait()
            ca_t, cb_t = coef_tables(eps_ref, sigma_ref, shape)

            def halo_coef(j, _):
                for ref, pos, ok_side in sides:
                    index = ref[6 * W + j].astype(jnp.int32)
                    ca, cb = pick(ca_t, index), pick(cb_t, index)
                    if ok_side is not None:
                        ca, cb = ca * ok_side, cb * ok_side
                    co_ref[coef_at(0, pos + j)] = ca
                    co_ref[coef_at(1, pos + j)] = cb
                return 0

            lax.fori_loop(0, W, halo_coef, 0, unroll=4)
        for q in range(3):
            index = sp_ref[block(18 + q)].astype(jnp.int32)
            sc_ref[block(q)] = pick(ca_t, index) * inside[q]
            sc_ref[block(3 + q)] = pick(cb_t, index) * inside[q]

        def fwd_x(v):
            r = [roll(u, 120, 1) for u in v]
            return [jnp.where(lane < 120, r[0], r[1]), jnp.where(lane < 120, r[1], r[2]), r[2]]

        def bwd_x(v):
            r = [roll(u, 8, 1) for u in v]
            return [r[0], jnp.where(lane >= 8, r[1], r[0]), jnp.where(lane >= 8, r[2], r[1])]

        def each(f, *vs):
            return [f(*u) for u in zip(*vs)]

        def own_planes(t):
            for j in range(size_x // STEPS):
                x = t * (size_x // STEPS) + j
                for c in range(3):
                    st_ref[at(0, c, x + W)] = e_ref[c, x]
                    st_ref[at(0, 3 + c, x + W)] = h_ref[c, x]
                index = m_ref[x]
                co_ref[coef_at(0, x + W)] = pick(ca_t, index)
                co_ref[coef_at(1, x + W)] = pick(cb_t, index)

        def strip_step(t, _):
            ex, ey, ez, hx, hy, hz = (
                [sp_ref[block(c * 3 + q)] for q in range(3)] for c in range(6)
            )
            ca_s = [sc_ref[block(q)] for q in range(3)]
            cb_s = [sc_ref[block(3 + q)] for q in range(3)]
            dt_s = [DT * k for k in inside]
            side_e = [[v * give_e for v in ex], [v * give_e for v in ey]]
            ez_x, ey_x = fwd_x(ez), fwd_x(ey)
            hx = each(
                lambda h, z, y, d: h - d * ((fwd_y(z) - z) - (fwd_z(y) - y)), hx, ez, ey, dt_s
            )
            hy = each(
                lambda h, x, z, zx, d: h - d * ((fwd_z(x) - x) - (zx - z)), hy, ex, ez, ez_x, dt_s
            )
            hz = each(
                lambda h, y, yx, x, d: h - d * ((yx - y) - (fwd_y(x) - x)), hz, ey, ey_x, ex, dt_s
            )
            if s == 0:
                own_planes(t)
            hz_x, hy_x = bwd_x(hz), bwd_x(hy)
            ex = each(
                lambda e, z, y, a, b: a * e + b * ((z - bwd_y(z)) - (y - bwd_z(y))),
                ex, hz, hy, ca_s, cb_s,
            )
            ey = each(
                lambda e, x, z, zx, a, b: a * e + b * ((x - bwd_z(x)) - (z - zx)),
                ey, hx, hz, hz_x, ca_s, cb_s,
            )
            ez = each(
                lambda e, y, yx, x, a, b: a * e + b * ((y - yx) - (x - bwd_y(x))),
                ez, hy, hy_x, hx, ca_s, cb_s,
            )
            for c, v in enumerate((ex, ey, ez, hx, hy, hz)):
                for q in range(3):
                    sp_ref[block(c * 3 + q)] = v[q]
            for j, v in enumerate((hx, hy)):
                for q in range(3):
                    dst = block((t * 2 + j) * 3 + q)
                    add = jnp.where(lane % 8 == 4, side_e[j][q], roll(v[q] * give_h, 2, 1))
                    in_ref[dst] = add if s == 0 else in_ref[dst] + add
            return 0

        lax.fori_loop(0, STEPS, strip_step, 0)

    dt_lo = jnp.where(lower, DT, 0.0)
    dt_hi = jnp.where(upper, DT, 0.0)

    planes = range(BLOCK)

    def advance(t, x, carry):
        hy_p, hz_p = carry
        old = [[st_ref[at(t - 1, c, x + i)] for i in range(BLOCK + (c < 3))] for c in range(6)]
        ca = [co_ref[coef_at(0, x + i)] for i in planes]
        cb = [co_ref[coef_at(1, x + i)] for i in planes]
        ex, ey, ez, hx, hy, hz = old
        side_x, side_y = [], []
        for i in planes:
            shift = (123 - 8 * ((x + i) % 16)) % LANES
            side_x.append(roll(in_ref[block((t - 1) * 6 + (x + i) // 16)], shift, 1))
            side_y.append(roll(in_ref[block((t - 1) * 6 + 3 + (x + i) // 16)], shift, 1))
        ex_z = [jnp.where(last, side_x[i], fwd_z(ex[i])) for i in planes]
        ey_z = [jnp.where(last, side_y[i], fwd_z(ey[i])) for i in planes]
        ez_y = [fwd_y(ez[i]) for i in planes]
        ex_y = [fwd_y(ex[i]) for i in planes]
        dt = [
            jnp.where(x + i < W, dt_lo, jnp.where(x + i >= size_x + W, dt_hi, DT)) for i in planes
        ]
        hx = [hx[i] - dt[i] * ((ez_y[i] - ez[i]) - (ey_z[i] - ey[i])) for i in planes]
        hy = [hy[i] - dt[i] * ((ex_z[i] - ex[i]) - (ez[i + 1] - ez[i])) for i in planes]
        hz = [hz[i] - dt[i] * ((ey[i + 1] - ey[i]) - (ex_y[i] - ex[i])) for i in planes]
        hx_z = [jnp.where(first, side_x[i], bwd_z(hx[i])) for i in planes]
        hy_z = [jnp.where(first, side_y[i], bwd_z(hy[i])) for i in planes]
        hy_x, hz_x = [hy_p] + hy, [hz_p] + hz
        new = [
            [ca[i] * ex[i] + cb[i] * ((hz[i] - bwd_y(hz[i])) - (hy[i] - hy_z[i])) for i in planes],
            [ca[i] * ey[i] + cb[i] * ((hx[i] - hx_z[i]) - (hz[i] - hz_x[i])) for i in planes],
            [ca[i] * ez[i] + cb[i] * ((hy[i] - hy_x[i]) - (hx[i] - bwd_y(hx[i]))) for i in planes],
            hx, hy, hz,
        ]
        for c in range(6):
            for i in planes:
                st_ref[at(t, c, x + i)] = new[c][i]
        return hy[-1], hz[-1]

    last, first = lane == 127, lane == 0

    half = size_x // 2
    copies = []
    for part in range(2):
        copies.append([])
        for c in range(3):
            for ref, cc in ((eo_ref, c), (ho_ref, 3 + c)):
                src = ((STEPS * 8 + cc) * wide + W + part * half) * size_y
                copies[part].append(
                    pltpu.make_async_copy(
                        st_ref.at[pl.ds(src, half * size_y)],
                        ref.at[c, pl.ds(part * half * size_y, half * size_y)],
                        sem.at[part * 6 + cc],
                    )
                )
    blocks = wide // BLOCK
    def step(t, _):
        zero = jnp.zeros(shape, F32)

        def planes_from(i, c):
            c = advance(t, i * BLOCK, c)

            @pl.when(jnp.logical_and(t == STEPS, i == blocks // 2 - 1 + blocks % 2))
            def _():
                for copy in copies[0]:
                    copy.start()

            return c

        lax.fori_loop(0, blocks, planes_from, (zero, zero))
        return 0

    lax.fori_loop(1, STEPS + 1, step, 0)
    for copy in copies[1]:
        copy.start()

    rows = 6
    lane8 = iota((rows, LANES), 1)
    zero8 = jnp.zeros((rows, LANES), F32)

    def slot(m, accs):
        cell = cells_ref[0, m]
        here = lane8 == m
        found = lane8 == jnp.where(cell >= 0, m, -1)
        numbers = jnp.where(here[:2], cell.astype(F32), accs[STEPS])
        cell = jnp.maximum(cell, 0)
        out = []
        for t in range(STEPS):
            start = (t + 1) * 8 * span + W * size_y + (cell >> 7)
            v = st_ref[pl.ds(start, rows, stride=span), :]
            out.append(jnp.where(found, roll(v, (m - cell) & 127, 1), accs[t]))
        return tuple(out) + (numbers,)

    zero2 = jnp.zeros((2, LANES), F32)
    accs = lax.fori_loop(0, LANES, slot, (zero8,) * STEPS + (zero2,), unroll=32)
    for t in range(STEPS):
        so_ref[t * 8 : t * 8 + 6] = accs[t][:6]
        so_ref[t * 8 + 6 : t * 8 + 8] = accs[STEPS] if t == 0 else zero2
    for copy in copies[0] + copies[1]:
        copy.wait()


SIN_C = (3.1415926401307077, -5.167710083507896, 2.550077523214726, -0.5982912856213906, 0.07765766030763246)
COS_C = (0.9999999532476085, -4.934792830619649, 4.058411352862754, -1.3318765680819573, 0.21968961109991972)
ROUND = 12582912.0


def horner(coefs, u):
    v = u * coefs[-1] + coefs[-2]
    for k in coefs[-3::-1]:
        v = v * u + k
    return v


def sincos4(turns):
    r = turns - ((turns + ROUND) - ROUND)
    u = r * r
    half_s = horner(SIN_C, u) * r
    half_c = horner(COS_C, u)
    twice = half_s + half_s
    s = twice * half_c
    c = 1.0 - twice * half_s
    s_2, c_2 = s + s, c + c
    s2 = s_2 * c
    c2 = 1.0 - s_2 * s
    s3 = c_2 * s2 - s
    c3 = c_2 * c2 - c
    s2_2 = s2 + s2
    return (s, c), (s2, c2), (s3, c3), (s2_2 * c2, 1.0 - s2_2 * s2)


def sincos(turns):
    return sincos4(turns)[0]


def split(v):
    hi = v.astype(BF16)
    return hi, (v - hi.astype(F32)).astype(BF16)


def project_kernel(
    first, size_x, size_y, size_z, tiles_x, tiles_z, own_ref, r1_ref, r2_ref, r3_ref, owner_ref, out_ref,
    inv_ref, smp_ref, pos_ref, th_ref, tl_ref, a_ref, acc_ref,
):
    gx, gz = lax.axis_index("gx"), lax.axis_index("gz")
    tiles = tiles_x * tiles_z
    base = 0.4 / (2.0 * math.pi)
    polars = ANGLES // NPHI

    def put(b, _):
        inv_ref[owner_ref[b]] = b
        return 0

    lax.fori_loop(0, tiles, put, 0, unroll=8)
    blocks = [inv_ref[(gx ^ (4 * d)) * tiles_z + gz] for d in (first, first + 1)]

    for i, ref in enumerate((own_ref, r1_ref, r2_ref, r3_ref)):
        for core in range(2):
            smp_ref[2 * i + core] = ref[core]
    row16 = iota((16, LANES), 0)
    lane16 = iota((16, LANES), 1)
    row8 = iota((8, LANES), 0)
    lane8 = iota((8, LANES), 1)

    def split3(v):
        a = v.astype(BF16).astype(F32)
        b = (v - a).astype(BF16).astype(F32)
        return a, b, v - a - b

    block = jnp.where(lane16 < 64, blocks[0], blocks[1])
    polar = 2 * block + (lane16 % 64) // 32
    st, _ = sincos((polar.astype(F32) + 0.5) * (0.5 / polars))
    sp, cp = sincos((lane16 % 32).astype(F32) * (1.0 / NPHI))
    ux = split3(base * st * cp)
    uy = split3(base * st * sp)
    mat = jnp.zeros((16, LANES), F32)
    for k in range(9):
        src = ux[k % 3] if k < 6 else uy[k % 3]
        mat = jnp.where(row16 == k, src, mat)
    dirs = mat.astype(BF16)
    combo = 2 * jnp.where(row8 % 4 < 2, blocks[0], blocks[1]) + row8 % 2
    _, uz = sincos((combo.astype(F32) + 0.5) * (0.5 / polars))
    uz = uz * base

    def wave(f, t):
        angle = 0.4 * (f + 1) * DT * (t + 1)
        return math.cos(angle), math.sin(angle)

    def gather(pair, _):
        pos = []
        for core in range(2):
            n = 2 * pair + core
            tile_x = gx ^ (2 * (pair % 2) + core)
            tile_z = gz ^ (pair // 2)
            rows = [smp_ref[n, t * 8 : t * 8 + 8] for t in range(STEPS)]
            cell = jnp.maximum(rows[0][6:7], 0.0).astype(jnp.int32)
            pz = (cell % size_z + tile_z * size_z).astype(F32) + (0.5 - size_z * tiles_z / 2)
            zs = sincos4(uz * pz)
            lanes = slice(core * LANES, (core + 1) * LANES)
            for f in range(FREQS):
                re = sum(wave(f, t)[0] * rows[t] for t in range(STEPS))
                im = sum(wave(f, t)[1] * rows[t] for t in range(STEPS))
                zsin, zcos = zs[f]
                for k in range(4):
                    sk, ck = zsin[k : k + 1], zcos[k : k + 1]
                    both = jnp.concatenate([re * ck - im * sk, re * sk + im * ck], axis=0)
                    hi, lo = split(both)
                    a_ref[pair, f, k * 16 : k * 16 + 16, lanes] = hi
                    a_ref[pair, f, 64 + k * 16 : 80 + k * 16, lanes] = lo
            gxi = cell // (size_y * size_z) + tile_x * size_x - size_x * tiles_x // 2
            high = ((gxi >> 4) << 4).astype(F32)
            low = (gxi & 15).astype(F32) + 0.5
            py = ((cell // size_z) % size_y).astype(F32) + (0.5 - size_y / 2)
            pos.append(
                jnp.where(row16 < 3, high, jnp.where(row16 < 6, low, jnp.where(row16 < 9, py, 0.0)))
            )
        pos_ref[pair] = jnp.concatenate(pos, axis=1).astype(BF16)
        return 0

    lax.fori_loop(0, 4, gather, 0)

    def table(i, b):
        phase = lax.dot_general(
            pos_ref[i], dirs, (((0,), (0,)), ((), ())), preferred_element_type=F32
        )
        for j in range(8):
            dst = slice(j * 32, j * 32 + 32)
            values = sincos4(phase[dst])
            for f in range(FREQS):
                for part in range(2):
                    hi, lo = split(values[f][1 - part])
                    th_ref[b * 4 + f, dst, part * LANES : (part + 1) * LANES] = hi
                    tl_ref[b * 4 + f, dst, part * LANES : (part + 1) * LANES] = lo

    def multiply(i, b):
        for f in range(FREQS):
            a = a_ref[i, f]
            o = jnp.dot(a, th_ref[b * 4 + f], preferred_element_type=F32)
            o = o[:64] + o[64:] + jnp.dot(a[:64], tl_ref[b * 4 + f], preferred_element_type=F32)
            if i == 0:
                acc_ref[f] = o
            else:
                acc_ref[f] += o

    table(0, 0)
    for k in range(4):
        if k < 3:
            table(k + 1, (k + 1) % 2)
        multiply(k, k % 2)

    near = lane8 % 64 < 32
    sign = jnp.where(near, 1.0, -1.0)

    def finish(f, _):
        for d in range(2):
            res = []
            for pol in range(2):
                r = (d * 2 + pol) * 16
                src = d * 64 + pol * 32
                pq = []
                for part in range(2):
                    for comp in range(2):
                        v = acc_ref[
                            f, r + comp * 8 : r + comp * 8 + 8, part * LANES : (part + 1) * LANES
                        ]
                        lo_v = roll(v, (pol * 64 - src) % LANES, 1)
                        hi_v = roll(v, (pol * 64 + 32 - src) % LANES, 1)
                        pq.append(jnp.where(near, lo_v, hi_v))
                pr, pi, qr, qi = pq
                res.append((pr - sign * qi, pi + sign * qr))
            out_ref[d, f, 0:8] = jnp.where(lane8 < 64, res[0][0], res[1][0])
            out_ref[d, f, 8:16] = jnp.where(lane8 < 64, res[0][1], res[1][1])
        return 0

    lax.fori_loop(0, FREQS, finish, 0, unroll=2)


def directions(angle):
    theta = math.pi * ((angle // NPHI).astype(F32) + 0.5) / (ANGLES // NPHI)
    phi = 2.0 * math.pi * (angle % NPHI).astype(F32) / NPHI
    return (jnp.sin(theta) * jnp.cos(phi), jnp.sin(theta) * jnp.sin(phi), jnp.cos(theta))


def project(acc_re, acc_im, pos_x, pos_y, pos_z, angle, omegas):
    dir_x, dir_y, dir_z = directions(angle)
    geometry = (
        dir_x[:, None] * pos_x[None] + dir_y[:, None] * pos_y[None] + dir_z[:, None] * pos_z[None]
    )
    phase = omegas[:, None, None] * geometry[None]
    cosine = jnp.cos(phase)
    sine = jnp.sin(phase)
    high = lax.Precision.HIGHEST
    real = jnp.einsum("fas,fcs->fca", cosine, acc_re, precision=high) - jnp.einsum(
        "fas,fcs->fca", sine, acc_im, precision=high
    )
    imag = jnp.einsum("fas,fcs->fca", sine, acc_re, precision=high) + jnp.einsum(
        "fas,fcs->fca", cosine, acc_im, precision=high
    )
    return jnp.concatenate([real, imag], axis=1)


def far_general(samples, cells, owner_table, sizes, tiles_x, tiles_z, scale):
    size_x, size_y, size_z = sizes
    tiles = tiles_x * tiles_z
    sample = samples.reshape(STEPS, 8, LANES)[:, :6]
    omegas = 0.4 * (jnp.arange(FREQS, dtype=F32) + 1.0)
    phase = omegas[:, None] * (DT * (jnp.arange(STEPS, dtype=F32) + 1.0))[None]
    acc_re = jnp.sum(jnp.cos(phase)[:, :, None, None] * sample[None], axis=1)
    acc_im = jnp.sum(jnp.sin(phase)[:, :, None, None] * sample[None], axis=1)
    local = jnp.maximum(cells, 0)
    glob_x = lax.axis_index("gx") * size_x + local // (size_y * size_z)
    glob_y = local // size_z % size_y
    glob_z = lax.axis_index("gz") * size_z + local % size_z
    pos_x = glob_x.astype(F32) + (0.5 - size_x * tiles_x / 2)
    pos_y = glob_y.astype(F32) + (0.5 - size_y / 2)
    pos_z = glob_z.astype(F32) + (0.5 - size_z * tiles_z / 2)
    block_len = ANGLES // tiles
    owners = jnp.arange(tiles, dtype=jnp.int32)
    blocks = jnp.sum(jnp.where(owner_table[None, :] == owners[:, None], owners[None, :], 0), axis=1)
    angle = (blocks[:, None] * block_len + jnp.arange(block_len, dtype=jnp.int32)[None]).reshape(-1)
    pattern = project(acc_re, acc_im, pos_x, pos_y, pos_z, angle, omegas)
    pattern = jnp.transpose(pattern.reshape(FREQS, 12, tiles, block_len), (2, 0, 1, 3))
    return lax.psum_scatter(pattern, ("gx", "gz"), scatter_dimension=0, tiled=True) * scale


VMEM = pl.BlockSpec(memory_space=pltpu.VMEM)
SMEM = pl.BlockSpec(memory_space=pltpu.SMEM)
ANY = pl.BlockSpec(memory_space=pl.ANY)
HBM = pl.BlockSpec(memory_space=pltpu.HBM)


def in_hbm(v):
    return pltpu.with_memory_space_constraint(v, pltpu.HBM)


def shards(nx, nz, e_init, h_init, material, eps_table, sigma_table, face_cells, owner_table):
    size_x, size_y, size_z = material.shape
    ns = 1 if nz == 2 else 2
    plane = (size_y, size_z)
    both = ("gx", "gz")

    def pair_a(i):
        return i ^ 1

    def pair_b(i):
        return i + 1 if i % 2 else i - 1

    def pair_z(k, s):
        return k + 1 if (k + s) % 2 == 0 else k - 1

    xa, xb, zp, zd = pl.pallas_call(
        functools.partial(pack_kernel, ns),
        out_shape=(
            jax.ShapeDtypeStruct((7 * W + 4 * ns,) + plane, F32),
            jax.ShapeDtypeStruct((7 * W,) + plane, F32),
            jax.ShapeDtypeStruct((ns, 8) + plane, F32),
            jax.ShapeDtypeStruct((ns, 4) + plane, F32),
        ),
        in_specs=[ANY] * 3,
        out_specs=(VMEM,) * 4,
        scratch_shapes=[
            pltpu.VMEM((6, size_x) + plane, F32),
            pltpu.VMEM((size_x,) + plane, jnp.int32),
            pltpu.SemaphoreType.DMA((7,)),
        ],
        compiler_params=pltpu.CompilerParams(vmem_limit_bytes=16 * 1024 * 1024),
        name="pack",
    )(in_hbm(e_init), in_hbm(h_init), in_hbm(material))
    xb_in = lax.ppermute(
        xb, "gx", [(i, pair_b(i)) for i in range(nx) if 0 <= pair_b(i) < nx]
    )

    swap = [(i, pair_a(i)) for i in range(nx)]
    xa_in = lax.ppermute(xa, "gx", swap)

    def turned(v, s, pair_x):
        links = [
            (i * nz + k, pair_x(i) * nz + pair_z(k, s))
            for i in range(nx)
            for k in range(nz)
            if 0 <= pair_x(i) < nx and 0 <= pair_z(k, s) < nz
        ]
        return lax.ppermute(v, both, links)

    z_in = []
    for s in range(ns):
        links = [(k, pair_z(k, s)) for k in range(nz) if 0 <= pair_z(k, s) < nz]
        z_in.append(lax.ppermute(zp[s], "gz", links))
    z_in = jnp.stack(z_in)
    za_in = jnp.stack([turned(zd[s], s, pair_a) for s in range(ns)])
    zb_in = jnp.stack([turned(zd[s], s, pair_b) for s in range(ns)])

    wide = size_x + 2 * W
    e_field, h_field, samples = pl.pallas_call(
        functools.partial(field_kernel, ns, nx, nz),
        out_shape=(
            jax.ShapeDtypeStruct((3, size_x * size_y, size_z), F32),
            jax.ShapeDtypeStruct((3, size_x * size_y, size_z), F32),
            jax.ShapeDtypeStruct((8 * STEPS, LANES), F32),
        ),
        in_specs=[VMEM] * 9 + [HBM] * 3,
        out_specs=(ANY, ANY, VMEM),
        scratch_shapes=[
            pltpu.VMEM(((STEPS + 1) * 8 * wide * size_y, LANES), F32),
            pltpu.VMEM((2 * wide * size_y, LANES), F32),
            pltpu.VMEM((STEPS * 2 * 3 * size_y, LANES), F32),
            pltpu.VMEM((8 * 3 * size_y, LANES), F32),
            pltpu.VMEM((2 * 3 * size_y, LANES), F32),
            pltpu.VMEM((4,) + plane, F32),
            pltpu.SMEM((1, eps_table.shape[0]), F32),
            pltpu.SMEM((1, eps_table.shape[0]), F32),
            pltpu.SMEM((1, LANES), jnp.int32),
            pltpu.SemaphoreType.DMA((12,)),
            pltpu.SemaphoreType.DMA((3,)),
        ],
        compiler_params=pltpu.CompilerParams(vmem_limit_bytes=48 * 1024 * 1024),
        name="fields",
    )(
        e_init, h_init, material, xa_in, xb_in, z_in, za_in, zb_in, zp,
        in_hbm(eps_table.reshape(1, -1)), in_hbm(sigma_table.reshape(1, -1)), in_hbm(face_cells),
    )
    e_field = e_field.reshape(e_init.shape)
    h_field = h_field.reshape(h_init.shape)

    tiles = nx * nz
    scale = 1.0 / math.sqrt(tiles * face_cells.shape[1] * STEPS)
    if not (nx == 16 and nz == 2):
        far = far_general(
            samples, face_cells[0], owner_table, material.shape, nx, nz, scale
        )
        return e_field, h_field, far

    def swap_all(v, mx, mz):
        links = [(i * nz + k, (i ^ mx) * nz + (k ^ mz)) for i in range(nx) for k in range(nz)]
        return lax.ppermute(v, both, links)

    mine = jnp.stack([samples, swap_all(samples, 1, 0)])
    by_y = swap_all(mine, 2, 0)
    by_x = swap_all(mine, 0, 1)
    by_xy = swap_all(mine, 2, 1)
    far_two, near_two = (
        pl.pallas_call(
            functools.partial(project_kernel, first, size_x, size_y, size_z, nx, nz),
            out_shape=jax.ShapeDtypeStruct((2, FREQS, 16, LANES), F32),
            in_specs=[VMEM] * 4 + [SMEM],
            out_specs=VMEM,
            scratch_shapes=[
                pltpu.SMEM((tiles,), jnp.int32),
                pltpu.VMEM((8, 8 * STEPS, LANES), F32),
                pltpu.VMEM((4, 16, 2 * LANES), BF16),
                pltpu.VMEM((2 * FREQS, 2 * LANES, 2 * LANES), BF16),
                pltpu.VMEM((2 * FREQS, 2 * LANES, 2 * LANES), BF16),
                pltpu.VMEM((4, FREQS, 128, 2 * LANES), BF16),
                pltpu.VMEM((FREQS, 64, 2 * LANES), F32),
            ],
            compiler_params=pltpu.CompilerParams(vmem_limit_bytes=32 * 1024 * 1024),
            cost_estimate=pl.CostEstimate(
                flops=1_000_000_000, bytes_accessed=8_000_000, transcendentals=0
            ),
            name="project",
        )(mine, by_y, by_x, by_xy, owner_table)
        for first in (2, 0)
    )
    near_two = near_two + swap_all(far_two, 8, 0)
    total = near_two[0] + swap_all(near_two[1], 4, 0)
    far = jnp.concatenate([total[:, 0:6], total[:, 8:14]], axis=1) * scale
    return e_field, h_field, far[None]


def solution(mesh):
    nx, nz = mesh.shape["gx"], mesh.shape["gz"]
    return jax.shard_map(
        functools.partial(shards, nx, nz),
        mesh=mesh,
        in_specs=(
            P(None, "gx", None, "gz"),
            P(None, "gx", None, "gz"),
            P("gx", None, "gz"),
            P(),
            P(),
            P(("gx", "gz"), None),
            P(),
        ),
        out_specs=(
            P(None, "gx", None, "gz"),
            P(None, "gx", None, "gz"),
            P(("gx", "gz"), None, None, None),
        ),
        check_vma=False,
    )
```

```python
import functools
import math

import jax
import jax.numpy as jnp
from jax import lax
from jax.experimental import pallas as pl
from jax.experimental.pallas import tpu as pltpu
from jax.sharding import PartitionSpec as P

STEPS = 4
ANGLES = 4096
NPHI = 64
FREQS = 4
DT = 0.5

W = 4
BLOCK = 40
LANES = 128
F32 = jnp.float32
BF16 = jnp.bfloat16


def roll(v, shift, axis):
    return pltpu.roll(v, shift, axis)


def iota(shape, axis):
    return lax.broadcasted_iota(jnp.int32, shape, axis)


def fold_pair(a, b, up, lane):
    own = jnp.where(up, lane, 127 - lane) >= 124
    return jnp.where(own, b, roll(a, jnp.where(up, 124, 4), 1))


def pack_kernel(ns, e_hbm, h_hbm, m_hbm, xa_ref, xb_ref, zp_ref, zd_ref, f_ref, m_ref, sem):
    size_x, size_y = m_ref.shape[0], m_ref.shape[1]
    gx, gz = lax.axis_index("gx"), lax.axis_index("gz")
    copies = [
        pltpu.make_async_copy((e_hbm if c < 3 else h_hbm).at[c % 3], f_ref.at[c], sem.at[c])
        for c in range(6)
    ]
    copies.append(pltpu.make_async_copy(m_hbm, m_ref, sem.at[6]))
    for copy in copies:
        copy.start()
    even = gx % 2 == 0
    lane = iota((size_y, LANES), 1)
    group = lane // 8

    def plane(c, x):
        return f_ref[c, x] if c < 6 else m_ref[x].astype(F32)

    for i in range(4):
        comps = (2 * i, 2 * i + 1) if i < 3 else (6, 6)
        for c in sorted(set(comps)):
            copies[c].wait()
            for ref, off in ((xa_ref, size_x - W), (xb_ref, 0)):
                off = jnp.where(even, off, size_x - W - off)
                for j in range(W):
                    ref[c * W + j] = plane(c, off + j)
        for s in range(ns):
            up = (gz + s) % 2 == 0
            base = jnp.where(up, 8, 0)

            def fold(g, acc):
                out = []
                for q in range(2):
                    x = (g + 28) % 32 if q == 0 else g + 12
                    cell = fold_pair(plane(comps[0], x), plane(comps[1], x), up, lane)
                    cell = roll(cell, (base + 8 * g) % LANES, 1)
                    out.append(jnp.where(group == g, cell, acc[q]))
                return tuple(out)

            zero = jnp.zeros((size_y, LANES), F32)
            acc = lax.fori_loop(0, 16, fold, (zero, zero), unroll=8)
            zp_ref[s, i] = acc[0]
            zp_ref[s, 4 + i] = acc[1]
            xa_ref[7 * W + 4 * s + i] = acc[0]
            zd_ref[s, i] = acc[0]


def coef_tables(eps_ref, sigma_ref, shape):
    lane = iota(shape, 1)
    eps = jnp.ones(shape, F32)
    sigma = jnp.zeros(shape, F32)
    for i in range(eps_ref.shape[1]):
        eps = jnp.where(lane == i, eps_ref[0, i], eps)
        sigma = jnp.where(lane == i, sigma_ref[0, i], sigma)
    loss = sigma * DT / (2.0 * eps)
    return (1.0 - loss) / (1.0 + loss), DT / (eps * (1.0 + loss))


def pick(table, index):
    return jnp.take_along_axis(table, index, axis=1, mode="promise_in_bounds")


def field_kernel(
    ns,
    nx,
    nz,
    e_ref,
    h_ref,
    m_ref,
    xa_ref,
    xb_ref,
    zr_ref,
    za_ref,
    zb_ref,
    zp_ref,
    eps_hbm,
    sigma_hbm,
    cells_hbm,
    eo_ref,
    ho_ref,
    so_ref,
    st_ref,
    co_ref,
    in_ref,
    sp_ref,
    sc_ref,
    qb_ref,
    eps_ref,
    sigma_ref,
    cells_ref,
    sem,
    in_sem,
):
    size_x, size_y = m_ref.shape[0], m_ref.shape[1]
    wide = size_x + 2 * W
    span = wide * size_y
    shape = (size_y, LANES)
    gx, gz = lax.axis_index("gx"), lax.axis_index("gz")
    even = gx % 2 == 0
    lower = gx > 0
    upper = gx < nx - 1
    lane = iota(shape, 1)
    row = iota(shape, 0)
    small = [
        pltpu.make_async_copy(src, dst, in_sem.at[i])
        for i, (src, dst) in enumerate(
            (
                (eps_hbm, eps_ref),
                (sigma_hbm, sigma_ref),
                (cells_hbm, cells_ref),
            )
        )
    ]
    for copy in small:
        copy.start()

    def at(t, c, x):
        return pl.ds(((t * 8 + c) * wide + x) * size_y, size_y)

    def coef_at(c, x):
        return pl.ds((c * wide + x) * size_y, size_y)

    def block(i):
        return pl.ds(i * size_y, size_y)

    pos_a = jnp.where(even, size_x + W, 0)
    pos_b = jnp.where(even, 0, size_x + W)
    ok_b = jnp.where(even, lower, upper).astype(F32)
    sides = ((xa_ref, pos_a, None), (xb_ref, pos_b, ok_b))

    def halo_plane(j, _):
        for ref, pos, _ in sides:
            for c in range(6):
                st_ref[at(0, c, pos + j)] = ref[c * W + j]
        return 0

    lax.fori_loop(0, W, halo_plane, 0, unroll=2)

    group = lane // 8
    first_half = lane % 8 < 4
    fy_keep = row < size_y - 1
    by_keep = row > 0

    def fwd_y(v):
        return jnp.where(fy_keep, roll(v, size_y - 1, 0), 0.0)

    def bwd_y(v):
        return jnp.where(by_keep, roll(v, 1, 0), 0.0)

    def fwd_z(v):
        return roll(v, 127, 1)

    def bwd_z(v):
        return roll(v, 1, 1)

    inside = [
        jnp.where(jnp.logical_and(group < W, jnp.logical_not(lower)), 0.0, 1.0),
        jnp.ones(shape, F32),
        jnp.where(jnp.logical_and(group >= W, jnp.logical_not(upper)), 0.0, 1.0),
    ]
    for s in range(ns):
        up = (gz + s) % 2 == 0
        partner = jnp.where(up, gz + 1, gz - 1)
        ok = jnp.logical_and(partner >= 0, partner < nz)
        give_e = jnp.where(jnp.logical_and(up, ok), 1.0, 0.0)
        give_h = jnp.where(jnp.logical_and(jnp.logical_not(up), ok), 1.0, 0.0)
        base = jnp.where(up, 8, 0)

        def corner(j, acc):
            g = j + jnp.where(even, 0, W)
            comps = [xb_ref[c * W + j] for c in range(7)]
            comps.append(comps[6])
            out = []
            for i in range(4):
                cell = fold_pair(comps[2 * i], comps[2 * i + 1], up, lane)
                cell = roll(cell, (base + 8 * g) % LANES, 1)
                out.append(jnp.where(group == g, cell, acc[i]))
            return tuple(out)

        zero = jnp.zeros(shape, F32)
        acc = lax.fori_loop(0, W, corner, (zero,) * 4, unroll=4)
        for i in range(4):
            qb_ref[i] = acc[i]

        def unfold(i, _):
            def whole(mine, other):
                lo = jnp.where(up, mine, other)
                hi = jnp.where(up, other, mine)
                return (
                    jnp.where(first_half, lo, hi),
                    jnp.where(first_half, roll(lo, 124, 1), roll(hi, 4, 1)),
                )

            q0 = whole(zp_ref[s, i], zr_ref[s, i])
            q1 = whole(zp_ref[s, 4 + i], zr_ref[s, 4 + i])
            qa = whole(xa_ref[7 * W + 4 * s + i], za_ref[s, i])
            qb = whole(qb_ref[i], zb_ref[s, i])
            for k in range(2):
                below = jnp.where(even, qb[k], qa[k])
                above = jnp.where(even, qa[k], qb[k])
                c = (2 * i + k) * 3
                sp_ref[block(c)] = jnp.where(group < W, below, q0[k])
                sp_ref[block(c + 1)] = q1[k]
                sp_ref[block(c + 2)] = jnp.where(group < W, q0[k], above)
            return 0

        lax.fori_loop(0, 4, unfold, 0, unroll=4)
        if s == 0:
            for copy in small:
                copy.wait()
            ca_t, cb_t = coef_tables(eps_ref, sigma_ref, shape)

            def halo_coef(j, _):
                for ref, pos, ok_side in sides:
                    index = ref[6 * W + j].astype(jnp.int32)
                    ca, cb = pick(ca_t, index), pick(cb_t, index)
                    if ok_side is not None:
                        ca, cb = ca * ok_side, cb * ok_side
                    co_ref[coef_at(0, pos + j)] = ca
                    co_ref[coef_at(1, pos + j)] = cb
                return 0

            lax.fori_loop(0, W, halo_coef, 0, unroll=4)
        for q in range(3):
            index = sp_ref[block(18 + q)].astype(jnp.int32)
            sc_ref[block(q)] = pick(ca_t, index) * inside[q]
            sc_ref[block(3 + q)] = pick(cb_t, index) * inside[q]

        def fwd_x(v):
            r = [roll(u, 120, 1) for u in v]
            return [jnp.where(lane < 120, r[0], r[1]), jnp.where(lane < 120, r[1], r[2]), r[2]]

        def bwd_x(v):
            r = [roll(u, 8, 1) for u in v]
            return [r[0], jnp.where(lane >= 8, r[1], r[0]), jnp.where(lane >= 8, r[2], r[1])]

        def each(f, *vs):
            return [f(*u) for u in zip(*vs)]

        def own_planes(t):
            for j in range(size_x // STEPS):
                x = t * (size_x // STEPS) + j
                for c in range(3):
                    st_ref[at(0, c, x + W)] = e_ref[c, x]
                    st_ref[at(0, 3 + c, x + W)] = h_ref[c, x]
                index = m_ref[x]
                co_ref[coef_at(0, x + W)] = pick(ca_t, index)
                co_ref[coef_at(1, x + W)] = pick(cb_t, index)

        def strip_step(t, _):
            ex, ey, ez, hx, hy, hz = (
                [sp_ref[block(c * 3 + q)] for q in range(3)] for c in range(6)
            )
            ca_s = [sc_ref[block(q)] for q in range(3)]
            cb_s = [sc_ref[block(3 + q)] for q in range(3)]
            dt_s = [DT * k for k in inside]
            side_e = [[v * give_e for v in ex], [v * give_e for v in ey]]
            ez_x, ey_x = fwd_x(ez), fwd_x(ey)
            hx = each(
                lambda h, z, y, d: h - d * ((fwd_y(z) - z) - (fwd_z(y) - y)), hx, ez, ey, dt_s
            )
            hy = each(
                lambda h, x, z, zx, d: h - d * ((fwd_z(x) - x) - (zx - z)), hy, ex, ez, ez_x, dt_s
            )
            hz = each(
                lambda h, y, yx, x, d: h - d * ((yx - y) - (fwd_y(x) - x)), hz, ey, ey_x, ex, dt_s
            )
            if s == 0:
                own_planes(t)
            hz_x, hy_x = bwd_x(hz), bwd_x(hy)
            ex = each(
                lambda e, z, y, a, b: a * e + b * ((z - bwd_y(z)) - (y - bwd_z(y))),
                ex, hz, hy, ca_s, cb_s,
            )
            ey = each(
                lambda e, x, z, zx, a, b: a * e + b * ((x - bwd_z(x)) - (z - zx)),
                ey, hx, hz, hz_x, ca_s, cb_s,
            )
            ez = each(
                lambda e, y, yx, x, a, b: a * e + b * ((y - yx) - (x - bwd_y(x))),
                ez, hy, hy_x, hx, ca_s, cb_s,
            )
            for c, v in enumerate((ex, ey, ez, hx, hy, hz)):
                for q in range(3):
                    sp_ref[block(c * 3 + q)] = v[q]
            for j, v in enumerate((hx, hy)):
                for q in range(3):
                    dst = block((t * 2 + j) * 3 + q)
                    add = jnp.where(lane % 8 == 4, side_e[j][q], roll(v[q] * give_h, 2, 1))
                    in_ref[dst] = add if s == 0 else in_ref[dst] + add
            return 0

        lax.fori_loop(0, STEPS, strip_step, 0)

    dt_lo = jnp.where(lower, DT, 0.0)
    dt_hi = jnp.where(upper, DT, 0.0)

    planes = range(BLOCK)

    def advance(t, x, carry):
        hy_p, hz_p = carry
        old = [[st_ref[at(t - 1, c, x + i)] for i in range(BLOCK + (c < 3))] for c in range(6)]
        ca = [co_ref[coef_at(0, x + i)] for i in planes]
        cb = [co_ref[coef_at(1, x + i)] for i in planes]
        ex, ey, ez, hx, hy, hz = old
        side_x, side_y = [], []
        for i in planes:
            shift = (123 - 8 * ((x + i) % 16)) % LANES
            side_x.append(roll(in_ref[block((t - 1) * 6 + (x + i) // 16)], shift, 1))
            side_y.append(roll(in_ref[block((t - 1) * 6 + 3 + (x + i) // 16)], shift, 1))
        ex_z = [jnp.where(last, side_x[i], fwd_z(ex[i])) for i in planes]
        ey_z = [jnp.where(last, side_y[i], fwd_z(ey[i])) for i in planes]
        ez_y = [fwd_y(ez[i]) for i in planes]
        ex_y = [fwd_y(ex[i]) for i in planes]
        dt = [
            jnp.where(x + i < W, dt_lo, jnp.where(x + i >= size_x + W, dt_hi, DT)) for i in planes
        ]
        hx = [hx[i] - dt[i] * ((ez_y[i] - ez[i]) - (ey_z[i] - ey[i])) for i in planes]
        hy = [hy[i] - dt[i] * ((ex_z[i] - ex[i]) - (ez[i + 1] - ez[i])) for i in planes]
        hz = [hz[i] - dt[i] * ((ey[i + 1] - ey[i]) - (ex_y[i] - ex[i])) for i in planes]
        hx_z = [jnp.where(first, side_x[i], bwd_z(hx[i])) for i in planes]
        hy_z = [jnp.where(first, side_y[i], bwd_z(hy[i])) for i in planes]
        hy_x, hz_x = [hy_p] + hy, [hz_p] + hz
        new = [
            [ca[i] * ex[i] + cb[i] * ((hz[i] - bwd_y(hz[i])) - (hy[i] - hy_z[i])) for i in planes],
            [ca[i] * ey[i] + cb[i] * ((hx[i] - hx_z[i]) - (hz[i] - hz_x[i])) for i in planes],
            [ca[i] * ez[i] + cb[i] * ((hy[i] - hy_x[i]) - (hx[i] - bwd_y(hx[i]))) for i in planes],
            hx, hy, hz,
        ]
        for c in range(6):
            for i in planes:
                st_ref[at(t, c, x + i)] = new[c][i]
        return hy[-1], hz[-1]

    last, first = lane == 127, lane == 0

    half = size_x // 2
    copies = []
    for part in range(2):
        copies.append([])
        for c in range(3):
            for ref, cc in ((eo_ref, c), (ho_ref, 3 + c)):
                src = ((STEPS * 8 + cc) * wide + W + part * half) * size_y
                copies[part].append(
                    pltpu.make_async_copy(
                        st_ref.at[pl.ds(src, half * size_y)],
                        ref.at[c, pl.ds(part * half * size_y, half * size_y)],
                        sem.at[part * 6 + cc],
                    )
                )
    blocks = wide // BLOCK
    def step(t, _):
        zero = jnp.zeros(shape, F32)

        def planes_from(i, c):
            c = advance(t, i * BLOCK, c)

            @pl.when(jnp.logical_and(t == STEPS, i == blocks // 2 - 1 + blocks % 2))
            def _():
                for copy in copies[0]:
                    copy.start()

            return c

        lax.fori_loop(0, blocks, planes_from, (zero, zero))
        return 0

    lax.fori_loop(1, STEPS + 1, step, 0)
    for copy in copies[1]:
        copy.start()

    rows = 6
    lane8 = iota((rows, LANES), 1)
    zero8 = jnp.zeros((rows, LANES), F32)

    def slot(m, accs):
        cell = cells_ref[0, m]
        here = lane8 == m
        found = lane8 == jnp.where(cell >= 0, m, -1)
        numbers = jnp.where(here[:2], cell.astype(F32), accs[STEPS])
        cell = jnp.maximum(cell, 0)
        out = []
        for t in range(STEPS):
            start = (t + 1) * 8 * span + W * size_y + (cell >> 7)
            v = st_ref[pl.ds(start, rows, stride=span), :]
            out.append(jnp.where(found, roll(v, (m - cell) & 127, 1), accs[t]))
        return tuple(out) + (numbers,)

    zero2 = jnp.zeros((2, LANES), F32)
    accs = lax.fori_loop(0, LANES, slot, (zero8,) * STEPS + (zero2,), unroll=32)
    for t in range(STEPS):
        so_ref[t * 8 : t * 8 + 6] = accs[t][:6]
        so_ref[t * 8 + 6 : t * 8 + 8] = accs[STEPS] if t == 0 else zero2
    for copy in copies[0] + copies[1]:
        copy.wait()


SIN_C = (3.1415926401307077, -5.167710083507896, 2.550077523214726, -0.5982912856213906, 0.07765766030763246)
COS_C = (0.9999999532476085, -4.934792830619649, 4.058411352862754, -1.3318765680819573, 0.21968961109991972)
ROUND = 12582912.0


def horner(coefs, u):
    v = u * coefs[-1] + coefs[-2]
    for k in coefs[-3::-1]:
        v = v * u + k
    return v


def sincos4(turns):
    r = turns - ((turns + ROUND) - ROUND)
    u = r * r
    half_s = horner(SIN_C, u) * r
    half_c = horner(COS_C, u)
    twice = half_s + half_s
    s = twice * half_c
    c = 1.0 - twice * half_s
    s_2, c_2 = s + s, c + c
    s2 = s_2 * c
    c2 = 1.0 - s_2 * s
    s3 = c_2 * s2 - s
    c3 = c_2 * c2 - c
    s2_2 = s2 + s2
    return (s, c), (s2, c2), (s3, c3), (s2_2 * c2, 1.0 - s2_2 * s2)


def sincos(turns):
    return sincos4(turns)[0]


def split(v):
    hi = v.astype(BF16)
    return hi, (v - hi.astype(F32)).astype(BF16)


def project_kernel(
    first, size_x, size_y, size_z, tiles_x, tiles_z, own_ref, r1_ref, r2_ref, r3_ref, owner_ref, out_ref,
    inv_ref, smp_ref, pos_ref, th_ref, tl_ref, a_ref, acc_ref,
):
    gx, gz = lax.axis_index("gx"), lax.axis_index("gz")
    tiles = tiles_x * tiles_z
    base = 0.4 / (2.0 * math.pi)
    polars = ANGLES // NPHI

    def put(b, _):
        inv_ref[owner_ref[b]] = b
        return 0

    lax.fori_loop(0, tiles, put, 0, unroll=8)
    blocks = [inv_ref[(gx ^ (4 * d)) * tiles_z + gz] for d in (first, first + 1)]

    for i, ref in enumerate((own_ref, r1_ref, r2_ref, r3_ref)):
        for core in range(2):
            smp_ref[2 * i + core] = ref[core]
    row16 = iota((16, LANES), 0)
    lane16 = iota((16, LANES), 1)
    row8 = iota((8, LANES), 0)
    lane8 = iota((8, LANES), 1)

    def split3(v):
        a = v.astype(BF16).astype(F32)
        b = (v - a).astype(BF16).astype(F32)
        return a, b, v - a - b

    block = jnp.where(lane16 < 64, blocks[0], blocks[1])
    polar = 2 * block + (lane16 % 64) // 32
    st, _ = sincos((polar.astype(F32) + 0.5) * (0.5 / polars))
    sp, cp = sincos((lane16 % 32).astype(F32) * (1.0 / NPHI))
    ux = split3(base * st * cp)
    uy = split3(base * st * sp)
    mat = jnp.zeros((16, LANES), F32)
    for k in range(9):
        src = ux[k % 3] if k < 6 else uy[k % 3]
        mat = jnp.where(row16 == k, src, mat)
    dirs = mat.astype(BF16)
    combo = 2 * jnp.where(row8 % 4 < 2, blocks[0], blocks[1]) + row8 % 2
    _, uz = sincos((combo.astype(F32) + 0.5) * (0.5 / polars))
    uz = uz * base

    def wave(f, t):
        angle = 0.4 * (f + 1) * DT * (t + 1)
        return math.cos(angle), math.sin(angle)

    def gather(pair, _):
        pos = []
        for core in range(2):
            n = 2 * pair + core
            tile_x = gx ^ (2 * (pair % 2) + core)
            tile_z = gz ^ (pair // 2)
            rows = [smp_ref[n, t * 8 : t * 8 + 8] for t in range(STEPS)]
            cell = jnp.maximum(rows[0][6:7], 0.0).astype(jnp.int32)
            pz = (cell % size_z + tile_z * size_z).astype(F32) + (0.5 - size_z * tiles_z / 2)
            zs = sincos4(uz * pz)
            lanes = slice(core * LANES, (core + 1) * LANES)
            for f in range(FREQS):
                re = sum(wave(f, t)[0] * rows[t] for t in range(STEPS))
                im = sum(wave(f, t)[1] * rows[t] for t in range(STEPS))
                zsin, zcos = zs[f]
                for k in range(4):
                    sk, ck = zsin[k : k + 1], zcos[k : k + 1]
                    both = jnp.concatenate([re * ck - im * sk, re * sk + im * ck], axis=0)
                    hi, lo = split(both)
                    a_ref[pair, f, k * 16 : k * 16 + 16, lanes] = hi
                    a_ref[pair, f, 64 + k * 16 : 80 + k * 16, lanes] = lo
            gxi = cell // (size_y * size_z) + tile_x * size_x - size_x * tiles_x // 2
            high = ((gxi >> 4) << 4).astype(F32)
            low = (gxi & 15).astype(F32) + 0.5
            py = ((cell // size_z) % size_y).astype(F32) + (0.5 - size_y / 2)
            pos.append(
                jnp.where(row16 < 3, high, jnp.where(row16 < 6, low, jnp.where(row16 < 9, py, 0.0)))
            )
        pos_ref[pair] = jnp.concatenate(pos, axis=1).astype(BF16)
        return 0

    lax.fori_loop(0, 4, gather, 0)

    def table(i, b):
        phase = lax.dot_general(
            pos_ref[i], dirs, (((0,), (0,)), ((), ())), preferred_element_type=F32
        )
        for j in range(8):
            dst = slice(j * 32, j * 32 + 32)
            values = sincos4(phase[dst])
            for f in range(FREQS):
                for part in range(2):
                    hi, lo = split(values[f][1 - part])
                    th_ref[b * 4 + f, dst, part * LANES : (part + 1) * LANES] = hi
                    tl_ref[b * 4 + f, dst, part * LANES : (part + 1) * LANES] = lo

    def multiply(i, b):
        for f in range(FREQS):
            a = a_ref[i, f]
            o = jnp.dot(a, th_ref[b * 4 + f], preferred_element_type=F32)
            o = o[:64] + o[64:] + jnp.dot(a[:64], tl_ref[b * 4 + f], preferred_element_type=F32)
            if i == 0:
                acc_ref[f] = o
            else:
                acc_ref[f] += o

    table(0, 0)
    for k in range(4):
        if k < 3:
            table(k + 1, (k + 1) % 2)
        multiply(k, k % 2)

    near = lane8 % 64 < 32
    sign = jnp.where(near, 1.0, -1.0)

    def finish(f, _):
        for d in range(2):
            res = []
            for pol in range(2):
                r = (d * 2 + pol) * 16
                src = d * 64 + pol * 32
                pq = []
                for part in range(2):
                    for comp in range(2):
                        v = acc_ref[
                            f, r + comp * 8 : r + comp * 8 + 8, part * LANES : (part + 1) * LANES
                        ]
                        lo_v = roll(v, (pol * 64 - src) % LANES, 1)
                        hi_v = roll(v, (pol * 64 + 32 - src) % LANES, 1)
                        pq.append(jnp.where(near, lo_v, hi_v))
                pr, pi, qr, qi = pq
                res.append((pr - sign * qi, pi + sign * qr))
            out_ref[d, 0:6, f] = jnp.where(lane8 < 64, res[0][0], res[1][0])[:6]
            out_ref[d, 6:12, f] = jnp.where(lane8 < 64, res[0][1], res[1][1])[:6]
        return 0

    lax.fori_loop(0, FREQS, finish, 0, unroll=2)


def directions(angle):
    theta = math.pi * ((angle // NPHI).astype(F32) + 0.5) / (ANGLES // NPHI)
    phi = 2.0 * math.pi * (angle % NPHI).astype(F32) / NPHI
    return (jnp.sin(theta) * jnp.cos(phi), jnp.sin(theta) * jnp.sin(phi), jnp.cos(theta))


def project(acc_re, acc_im, pos_x, pos_y, pos_z, angle, omegas):
    dir_x, dir_y, dir_z = directions(angle)
    geometry = (
        dir_x[:, None] * pos_x[None] + dir_y[:, None] * pos_y[None] + dir_z[:, None] * pos_z[None]
    )
    phase = omegas[:, None, None] * geometry[None]
    cosine = jnp.cos(phase)
    sine = jnp.sin(phase)
    high = lax.Precision.HIGHEST
    real = jnp.einsum("fas,fcs->fca", cosine, acc_re, precision=high) - jnp.einsum(
        "fas,fcs->fca", sine, acc_im, precision=high
    )
    imag = jnp.einsum("fas,fcs->fca", sine, acc_re, precision=high) + jnp.einsum(
        "fas,fcs->fca", cosine, acc_im, precision=high
    )
    return jnp.concatenate([real, imag], axis=1)


def far_general(samples, cells, owner_table, sizes, tiles_x, tiles_z, scale):
    size_x, size_y, size_z = sizes
    tiles = tiles_x * tiles_z
    sample = samples.reshape(STEPS, 8, LANES)[:, :6]
    omegas = 0.4 * (jnp.arange(FREQS, dtype=F32) + 1.0)
    phase = omegas[:, None] * (DT * (jnp.arange(STEPS, dtype=F32) + 1.0))[None]
    acc_re = jnp.sum(jnp.cos(phase)[:, :, None, None] * sample[None], axis=1)
    acc_im = jnp.sum(jnp.sin(phase)[:, :, None, None] * sample[None], axis=1)
    local = jnp.maximum(cells, 0)
    glob_x = lax.axis_index("gx") * size_x + local // (size_y * size_z)
    glob_y = local // size_z % size_y
    glob_z = lax.axis_index("gz") * size_z + local % size_z
    pos_x = glob_x.astype(F32) + (0.5 - size_x * tiles_x / 2)
    pos_y = glob_y.astype(F32) + (0.5 - size_y / 2)
    pos_z = glob_z.astype(F32) + (0.5 - size_z * tiles_z / 2)
    block_len = ANGLES // tiles
    owners = jnp.arange(tiles, dtype=jnp.int32)
    blocks = jnp.sum(jnp.where(owner_table[None, :] == owners[:, None], owners[None, :], 0), axis=1)
    angle = (blocks[:, None] * block_len + jnp.arange(block_len, dtype=jnp.int32)[None]).reshape(-1)
    pattern = project(acc_re, acc_im, pos_x, pos_y, pos_z, angle, omegas)
    pattern = jnp.transpose(pattern.reshape(FREQS, 12, tiles, block_len), (2, 0, 1, 3))
    return lax.psum_scatter(pattern, ("gx", "gz"), scatter_dimension=0, tiled=True) * scale


VMEM = pl.BlockSpec(memory_space=pltpu.VMEM)
SMEM = pl.BlockSpec(memory_space=pltpu.SMEM)
ANY = pl.BlockSpec(memory_space=pl.ANY)
HBM = pl.BlockSpec(memory_space=pltpu.HBM)


def in_hbm(v):
    return pltpu.with_memory_space_constraint(v, pltpu.HBM)


def shards(nx, nz, e_init, h_init, material, eps_table, sigma_table, face_cells, owner_table):
    size_x, size_y, size_z = material.shape
    ns = 1 if nz == 2 else 2
    plane = (size_y, size_z)
    both = ("gx", "gz")

    def pair_a(i):
        return i ^ 1

    def pair_b(i):
        return i + 1 if i % 2 else i - 1

    def pair_z(k, s):
        return k + 1 if (k + s) % 2 == 0 else k - 1

    xa, xb, zp, zd = pl.pallas_call(
        functools.partial(pack_kernel, ns),
        out_shape=(
            jax.ShapeDtypeStruct((7 * W + 4 * ns,) + plane, F32),
            jax.ShapeDtypeStruct((7 * W,) + plane, F32),
            jax.ShapeDtypeStruct((ns, 8) + plane, F32),
            jax.ShapeDtypeStruct((ns, 4) + plane, F32),
        ),
        in_specs=[ANY] * 3,
        out_specs=(VMEM,) * 4,
        scratch_shapes=[
            pltpu.VMEM((6, size_x) + plane, F32),
            pltpu.VMEM((size_x,) + plane, jnp.int32),
            pltpu.SemaphoreType.DMA((7,)),
        ],
        compiler_params=pltpu.CompilerParams(vmem_limit_bytes=16 * 1024 * 1024),
        name="pack",
    )(in_hbm(e_init), in_hbm(h_init), in_hbm(material))
    xb_in = lax.ppermute(
        xb, "gx", [(i, pair_b(i)) for i in range(nx) if 0 <= pair_b(i) < nx]
    )

    swap = [(i, pair_a(i)) for i in range(nx)]
    xa_in = lax.ppermute(xa, "gx", swap)

    def turned(v, s, pair_x):
        links = [
            (i * nz + k, pair_x(i) * nz + pair_z(k, s))
            for i in range(nx)
            for k in range(nz)
            if 0 <= pair_x(i) < nx and 0 <= pair_z(k, s) < nz
        ]
        return lax.ppermute(v, both, links)

    z_in = []
    for s in range(ns):
        links = [(k, pair_z(k, s)) for k in range(nz) if 0 <= pair_z(k, s) < nz]
        z_in.append(lax.ppermute(zp[s], "gz", links))
    z_in = jnp.stack(z_in)
    za_in = jnp.stack([turned(zd[s], s, pair_a) for s in range(ns)])
    zb_in = jnp.stack([turned(zd[s], s, pair_b) for s in range(ns)])

    wide = size_x + 2 * W
    e_field, h_field, samples = pl.pallas_call(
        functools.partial(field_kernel, ns, nx, nz),
        out_shape=(
            jax.ShapeDtypeStruct((3, size_x * size_y, size_z), F32),
            jax.ShapeDtypeStruct((3, size_x * size_y, size_z), F32),
            jax.ShapeDtypeStruct((8 * STEPS, LANES), F32),
        ),
        in_specs=[VMEM] * 9 + [HBM] * 3,
        out_specs=(ANY, ANY, VMEM),
        scratch_shapes=[
            pltpu.VMEM(((STEPS + 1) * 8 * wide * size_y, LANES), F32),
            pltpu.VMEM((2 * wide * size_y, LANES), F32),
            pltpu.VMEM((STEPS * 2 * 3 * size_y, LANES), F32),
            pltpu.VMEM((8 * 3 * size_y, LANES), F32),
            pltpu.VMEM((2 * 3 * size_y, LANES), F32),
            pltpu.VMEM((4,) + plane, F32),
            pltpu.SMEM((1, eps_table.shape[0]), F32),
            pltpu.SMEM((1, eps_table.shape[0]), F32),
            pltpu.SMEM((1, LANES), jnp.int32),
            pltpu.SemaphoreType.DMA((12,)),
            pltpu.SemaphoreType.DMA((3,)),
        ],
        compiler_params=pltpu.CompilerParams(vmem_limit_bytes=48 * 1024 * 1024),
        name="fields",
    )(
        e_init, h_init, material, xa_in, xb_in, z_in, za_in, zb_in, zp,
        in_hbm(eps_table.reshape(1, -1)), in_hbm(sigma_table.reshape(1, -1)), in_hbm(face_cells),
    )
    e_field = e_field.reshape(e_init.shape)
    h_field = h_field.reshape(h_init.shape)

    tiles = nx * nz
    scale = 1.0 / math.sqrt(tiles * face_cells.shape[1] * STEPS)
    if not (nx == 16 and nz == 2):
        far = far_general(
            samples, face_cells[0], owner_table, material.shape, nx, nz, scale
        )
        return e_field, h_field, far

    def swap_all(v, mx, mz):
        links = [(i * nz + k, (i ^ mx) * nz + (k ^ mz)) for i in range(nx) for k in range(nz)]
        return lax.ppermute(v, both, links)

    mine = jnp.stack([samples, swap_all(samples, 1, 0)])
    by_y = swap_all(mine, 2, 0)
    by_x = swap_all(mine, 0, 1)
    by_xy = swap_all(mine, 2, 1)
    far_two, near_two = (
        pl.pallas_call(
            functools.partial(project_kernel, first, size_x, size_y, size_z, nx, nz),
            out_shape=jax.ShapeDtypeStruct((2, 12, FREQS, LANES), F32),
            in_specs=[VMEM] * 4 + [SMEM],
            out_specs=VMEM,
            scratch_shapes=[
                pltpu.SMEM((tiles,), jnp.int32),
                pltpu.VMEM((8, 8 * STEPS, LANES), F32),
                pltpu.VMEM((4, 16, 2 * LANES), BF16),
                pltpu.VMEM((2 * FREQS, 2 * LANES, 2 * LANES), BF16),
                pltpu.VMEM((2 * FREQS, 2 * LANES, 2 * LANES), BF16),
                pltpu.VMEM((4, FREQS, 128, 2 * LANES), BF16),
                pltpu.VMEM((FREQS, 64, 2 * LANES), F32),
            ],
            compiler_params=pltpu.CompilerParams(vmem_limit_bytes=32 * 1024 * 1024),
            cost_estimate=pl.CostEstimate(
                flops=1_000_000_000, bytes_accessed=8_000_000, transcendentals=0
            ),
            name="project",
        )(mine, by_y, by_x, by_xy, owner_table)
        for first in (2, 0)
    )
    near_two = near_two + swap_all(far_two, 8, 0)
    total = near_two[0] + swap_all(near_two[1], 4, 0)
    far = jnp.transpose(total * scale, (1, 0, 2))
    return e_field, h_field, far[None]


def solution(mesh):
    nx, nz = mesh.shape["gx"], mesh.shape["gz"]
    return jax.shard_map(
        functools.partial(shards, nx, nz),
        mesh=mesh,
        in_specs=(
            P(None, "gx", None, "gz"),
            P(None, "gx", None, "gz"),
            P("gx", None, "gz"),
            P(),
            P(),
            P(("gx", "gz"), None),
            P(),
        ),
        out_specs=(
            P(None, "gx", None, "gz"),
            P(None, "gx", None, "gz"),
            P(("gx", "gz"), None, None, None),
        ),
        check_vma=False,
    )
```

```python
import functools
import math

import jax
import jax.numpy as jnp
from jax import lax
from jax.experimental import pallas as pl
from jax.experimental.pallas import tpu as pltpu
from jax.sharding import PartitionSpec as P

STEPS = 4
ANGLES = 4096
NPHI = 64
FREQS = 4
DT = 0.5

W = 4
BLOCK = 40
LANES = 128
F32 = jnp.float32
BF16 = jnp.bfloat16


def roll(v, shift, axis):
    return pltpu.roll(v, shift, axis)


def iota(shape, axis):
    return lax.broadcasted_iota(jnp.int32, shape, axis)


def fold_pair(a, b, up, lane):
    own = jnp.where(up, lane, 127 - lane) >= 124
    return jnp.where(own, b, roll(a, jnp.where(up, 124, 4), 1))


def pack_kernel(ns, e_hbm, h_hbm, m_hbm, xa_ref, xb_ref, zp_ref, zd_ref, f_ref, m_ref, sem):
    size_x, size_y = m_ref.shape[0], m_ref.shape[1]
    gx, gz = lax.axis_index("gx"), lax.axis_index("gz")
    copies = [
        pltpu.make_async_copy((e_hbm if c < 3 else h_hbm).at[c % 3], f_ref.at[c], sem.at[c])
        for c in range(6)
    ]
    copies.append(pltpu.make_async_copy(m_hbm, m_ref, sem.at[6]))
    for copy in copies:
        copy.start()
    even = gx % 2 == 0
    lane = iota((size_y, LANES), 1)
    group = lane // 8

    def plane(c, x):
        return f_ref[c, x] if c < 6 else m_ref[x].astype(F32)

    for i in range(4):
        comps = (2 * i, 2 * i + 1) if i < 3 else (6, 6)
        for c in sorted(set(comps)):
            copies[c].wait()
            for ref, off in ((xa_ref, size_x - W), (xb_ref, 0)):
                off = jnp.where(even, off, size_x - W - off)
                for j in range(W):
                    ref[c * W + j] = plane(c, off + j)
        for s in range(ns):
            up = (gz + s) % 2 == 0
            base = jnp.where(up, 8, 0)

            def fold(g, acc):
                out = []
                for q in range(2):
                    x = (g + 28) % 32 if q == 0 else g + 12
                    cell = fold_pair(plane(comps[0], x), plane(comps[1], x), up, lane)
                    cell = roll(cell, (base + 8 * g) % LANES, 1)
                    out.append(jnp.where(group == g, cell, acc[q]))
                return tuple(out)

            zero = jnp.zeros((size_y, LANES), F32)
            acc = lax.fori_loop(0, 16, fold, (zero, zero), unroll=16)
            zp_ref[s, i] = acc[0]
            zp_ref[s, 4 + i] = acc[1]
            xa_ref[7 * W + 4 * s + i] = acc[0]
            zd_ref[s, i] = acc[0]


def coef_tables(eps_ref, sigma_ref, shape):
    lane = iota(shape, 1)
    eps = jnp.ones(shape, F32)
    sigma = jnp.zeros(shape, F32)
    for i in range(eps_ref.shape[1]):
        eps = jnp.where(lane == i, eps_ref[0, i], eps)
        sigma = jnp.where(lane == i, sigma_ref[0, i], sigma)
    loss = sigma * DT / (2.0 * eps)
    return (1.0 - loss) / (1.0 + loss), DT / (eps * (1.0 + loss))


def pick(table, index):
    return jnp.take_along_axis(table, index, axis=1, mode="promise_in_bounds")


def field_kernel(
    ns,
    nx,
    nz,
    e_ref,
    h_ref,
    m_ref,
    xa_ref,
    xb_ref,
    zr_ref,
    za_ref,
    zb_ref,
    zp_ref,
    eps_hbm,
    sigma_hbm,
    cells_hbm,
    eo_ref,
    ho_ref,
    so_ref,
    st_ref,
    co_ref,
    in_ref,
    sp_ref,
    sc_ref,
    qb_ref,
    eps_ref,
    sigma_ref,
    cells_ref,
    sem,
    in_sem,
):
    size_x, size_y = m_ref.shape[0], m_ref.shape[1]
    wide = size_x + 2 * W
    span = wide * size_y
    shape = (size_y, LANES)
    gx, gz = lax.axis_index("gx"), lax.axis_index("gz")
    even = gx % 2 == 0
    lower = gx > 0
    upper = gx < nx - 1
    lane = iota(shape, 1)
    row = iota(shape, 0)
    small = [
        pltpu.make_async_copy(src, dst, in_sem.at[i])
        for i, (src, dst) in enumerate(
            (
                (eps_hbm, eps_ref),
                (sigma_hbm, sigma_ref),
                (cells_hbm, cells_ref),
            )
        )
    ]
    for copy in small:
        copy.start()

    def at(t, c, x):
        return pl.ds(((t * 8 + c) * wide + x) * size_y, size_y)

    def coef_at(c, x):
        return pl.ds((c * wide + x) * size_y, size_y)

    def block(i):
        return pl.ds(i * size_y, size_y)

    pos_a = jnp.where(even, size_x + W, 0)
    pos_b = jnp.where(even, 0, size_x + W)
    ok_b = jnp.where(even, lower, upper).astype(F32)
    sides = ((xa_ref, pos_a, None), (xb_ref, pos_b, ok_b))

    def halo_plane(j, _):
        for ref, pos, _ in sides:
            for c in range(6):
                st_ref[at(0, c, pos + j)] = ref[c * W + j]
        return 0

    lax.fori_loop(0, W, halo_plane, 0, unroll=2)

    group = lane // 8
    first_half = lane % 8 < 4
    fy_keep = row < size_y - 1
    by_keep = row > 0

    def fwd_y(v):
        return jnp.where(fy_keep, roll(v, size_y - 1, 0), 0.0)

    def bwd_y(v):
        return jnp.where(by_keep, roll(v, 1, 0), 0.0)

    def fwd_z(v):
        return roll(v, 127, 1)

    def bwd_z(v):
        return roll(v, 1, 1)

    inside = [
        jnp.where(jnp.logical_and(group < W, jnp.logical_not(lower)), 0.0, 1.0),
        jnp.ones(shape, F32),
        jnp.where(jnp.logical_and(group >= W, jnp.logical_not(upper)), 0.0, 1.0),
    ]
    for s in range(ns):
        up = (gz + s) % 2 == 0
        partner = jnp.where(up, gz + 1, gz - 1)
        ok = jnp.logical_and(partner >= 0, partner < nz)
        give_e = jnp.where(jnp.logical_and(up, ok), 1.0, 0.0)
        give_h = jnp.where(jnp.logical_and(jnp.logical_not(up), ok), 1.0, 0.0)
        base = jnp.where(up, 8, 0)

        def corner(j, acc):
            g = j + jnp.where(even, 0, W)
            comps = [xb_ref[c * W + j] for c in range(7)]
            comps.append(comps[6])
            out = []
            for i in range(4):
                cell = fold_pair(comps[2 * i], comps[2 * i + 1], up, lane)
                cell = roll(cell, (base + 8 * g) % LANES, 1)
                out.append(jnp.where(group == g, cell, acc[i]))
            return tuple(out)

        zero = jnp.zeros(shape, F32)
        acc = lax.fori_loop(0, W, corner, (zero,) * 4, unroll=4)
        for i in range(4):
            qb_ref[i] = acc[i]

        def unfold(i, _):
            def whole(mine, other):
                lo = jnp.where(up, mine, other)
                hi = jnp.where(up, other, mine)
                return (
                    jnp.where(first_half, lo, hi),
                    jnp.where(first_half, roll(lo, 124, 1), roll(hi, 4, 1)),
                )

            q0 = whole(zp_ref[s, i], zr_ref[s, i])
            q1 = whole(zp_ref[s, 4 + i], zr_ref[s, 4 + i])
            qa = whole(xa_ref[7 * W + 4 * s + i], za_ref[s, i])
            qb = whole(qb_ref[i], zb_ref[s, i])
            for k in range(2):
                below = jnp.where(even, qb[k], qa[k])
                above = jnp.where(even, qa[k], qb[k])
                c = (2 * i + k) * 3
                sp_ref[block(c)] = jnp.where(group < W, below, q0[k])
                sp_ref[block(c + 1)] = q1[k]
                sp_ref[block(c + 2)] = jnp.where(group < W, q0[k], above)
            return 0

        lax.fori_loop(0, 4, unfold, 0, unroll=4)
        if s == 0:
            for copy in small:
                copy.wait()
            ca_t, cb_t = coef_tables(eps_ref, sigma_ref, shape)

            def halo_coef(j, _):
                for ref, pos, ok_side in sides:
                    index = ref[6 * W + j].astype(jnp.int32)
                    ca, cb = pick(ca_t, index), pick(cb_t, index)
                    if ok_side is not None:
                        ca, cb = ca * ok_side, cb * ok_side
                    co_ref[coef_at(0, pos + j)] = ca
                    co_ref[coef_at(1, pos + j)] = cb
                return 0

            lax.fori_loop(0, W, halo_coef, 0, unroll=4)
        for q in range(3):
            index = sp_ref[block(18 + q)].astype(jnp.int32)
            sc_ref[block(q)] = pick(ca_t, index) * inside[q]
            sc_ref[block(3 + q)] = pick(cb_t, index) * inside[q]

        def fwd_x(v):
            r = [roll(u, 120, 1) for u in v]
            return [jnp.where(lane < 120, r[0], r[1]), jnp.where(lane < 120, r[1], r[2]), r[2]]

        def bwd_x(v):
            r = [roll(u, 8, 1) for u in v]
            return [r[0], jnp.where(lane >= 8, r[1], r[0]), jnp.where(lane >= 8, r[2], r[1])]

        def each(f, *vs):
            return [f(*u) for u in zip(*vs)]

        def own_planes(t):
            for j in range(size_x // STEPS):
                x = t * (size_x // STEPS) + j
                for c in range(3):
                    st_ref[at(0, c, x + W)] = e_ref[c, x]
                    st_ref[at(0, 3 + c, x + W)] = h_ref[c, x]
                index = m_ref[x]
                co_ref[coef_at(0, x + W)] = pick(ca_t, index)
                co_ref[coef_at(1, x + W)] = pick(cb_t, index)

        def strip_step(t, _):
            ex, ey, ez, hx, hy, hz = (
                [sp_ref[block(c * 3 + q)] for q in range(3)] for c in range(6)
            )
            ca_s = [sc_ref[block(q)] for q in range(3)]
            cb_s = [sc_ref[block(3 + q)] for q in range(3)]
            dt_s = [DT * k for k in inside]
            side_e = [[v * give_e for v in ex], [v * give_e for v in ey]]
            ez_x, ey_x = fwd_x(ez), fwd_x(ey)
            hx = each(
                lambda h, z, y, d: h - d * ((fwd_y(z) - z) - (fwd_z(y) - y)), hx, ez, ey, dt_s
            )
            hy = each(
                lambda h, x, z, zx, d: h - d * ((fwd_z(x) - x) - (zx - z)), hy, ex, ez, ez_x, dt_s
            )
            hz = each(
                lambda h, y, yx, x, d: h - d * ((yx - y) - (fwd_y(x) - x)), hz, ey, ey_x, ex, dt_s
            )
            if s == 0:
                own_planes(t)
            hz_x, hy_x = bwd_x(hz), bwd_x(hy)
            ex = each(
                lambda e, z, y, a, b: a * e + b * ((z - bwd_y(z)) - (y - bwd_z(y))),
                ex, hz, hy, ca_s, cb_s,
            )
            ey = each(
                lambda e, x, z, zx, a, b: a * e + b * ((x - bwd_z(x)) - (z - zx)),
                ey, hx, hz, hz_x, ca_s, cb_s,
            )
            ez = each(
                lambda e, y, yx, x, a, b: a * e + b * ((y - yx) - (x - bwd_y(x))),
                ez, hy, hy_x, hx, ca_s, cb_s,
            )
            for c, v in enumerate((ex, ey, ez, hx, hy, hz)):
                for q in range(3):
                    sp_ref[block(c * 3 + q)] = v[q]
            for j, v in enumerate((hx, hy)):
                for q in range(3):
                    dst = block((t * 2 + j) * 3 + q)
                    add = jnp.where(lane % 8 == 4, side_e[j][q], roll(v[q] * give_h, 2, 1))
                    in_ref[dst] = add if s == 0 else in_ref[dst] + add
            return 0

        lax.fori_loop(0, STEPS, strip_step, 0)

    dt_lo = jnp.where(lower, DT, 0.0)
    dt_hi = jnp.where(upper, DT, 0.0)

    planes = range(BLOCK)

    def advance(t, x, carry):
        hy_p, hz_p = carry
        old = [[st_ref[at(t - 1, c, x + i)] for i in range(BLOCK + (c < 3))] for c in range(6)]
        ca = [co_ref[coef_at(0, x + i)] for i in planes]
        cb = [co_ref[coef_at(1, x + i)] for i in planes]
        ex, ey, ez, hx, hy, hz = old
        side_x, side_y = [], []
        for i in planes:
            shift = (123 - 8 * ((x + i) % 16)) % LANES
            side_x.append(roll(in_ref[block((t - 1) * 6 + (x + i) // 16)], shift, 1))
            side_y.append(roll(in_ref[block((t - 1) * 6 + 3 + (x + i) // 16)], shift, 1))
        ex_z = [jnp.where(last, side_x[i], fwd_z(ex[i])) for i in planes]
        ey_z = [jnp.where(last, side_y[i], fwd_z(ey[i])) for i in planes]
        ez_y = [fwd_y(ez[i]) for i in planes]
        ex_y = [fwd_y(ex[i]) for i in planes]
        dt = [
            jnp.where(x + i < W, dt_lo, jnp.where(x + i >= size_x + W, dt_hi, DT)) for i in planes
        ]
        hx = [hx[i] - dt[i] * ((ez_y[i] - ez[i]) - (ey_z[i] - ey[i])) for i in planes]
        hy = [hy[i] - dt[i] * ((ex_z[i] - ex[i]) - (ez[i + 1] - ez[i])) for i in planes]
        hz = [hz[i] - dt[i] * ((ey[i + 1] - ey[i]) - (ex_y[i] - ex[i])) for i in planes]
        hx_z = [jnp.where(first, side_x[i], bwd_z(hx[i])) for i in planes]
        hy_z = [jnp.where(first, side_y[i], bwd_z(hy[i])) for i in planes]
        hy_x, hz_x = [hy_p] + hy, [hz_p] + hz
        new = [
            [ca[i] * ex[i] + cb[i] * ((hz[i] - bwd_y(hz[i])) - (hy[i] - hy_z[i])) for i in planes],
            [ca[i] * ey[i] + cb[i] * ((hx[i] - hx_z[i]) - (hz[i] - hz_x[i])) for i in planes],
            [ca[i] * ez[i] + cb[i] * ((hy[i] - hy_x[i]) - (hx[i] - bwd_y(hx[i]))) for i in planes],
            hx, hy, hz,
        ]
        for c in range(6):
            for i in planes:
                st_ref[at(t, c, x + i)] = new[c][i]
        return hy[-1], hz[-1]

    last, first = lane == 127, lane == 0

    half = size_x // 2
    copies = []
    for part in range(2):
        copies.append([])
        for c in range(3):
            for ref, cc in ((eo_ref, c), (ho_ref, 3 + c)):
                src = ((STEPS * 8 + cc) * wide + W + part * half) * size_y
                copies[part].append(
                    pltpu.make_async_copy(
                        st_ref.at[pl.ds(src, half * size_y)],
                        ref.at[c, pl.ds(part * half * size_y, half * size_y)],
                        sem.at[part * 6 + cc],
                    )
                )
    blocks = wide // BLOCK
    def step(t, _):
        zero = jnp.zeros(shape, F32)

        def planes_from(i, c):
            c = advance(t, i * BLOCK, c)

            @pl.when(jnp.logical_and(t == STEPS, i == blocks // 2 - 1 + blocks % 2))
            def _():
                for copy in copies[0]:
                    copy.start()

            return c

        lax.fori_loop(0, blocks, planes_from, (zero, zero))
        return 0

    lax.fori_loop(1, STEPS + 1, step, 0)
    for copy in copies[1]:
        copy.start()

    rows = 6
    lane8 = iota((rows, LANES), 1)
    zero8 = jnp.zeros((rows, LANES), F32)

    def slot(m, accs):
        cell = cells_ref[0, m]
        here = lane8 == m
        found = lane8 == jnp.where(cell >= 0, m, -1)
        numbers = jnp.where(here[:2], cell.astype(F32), accs[STEPS])
        cell = jnp.maximum(cell, 0)
        out = []
        for t in range(STEPS):
            start = (t + 1) * 8 * span + W * size_y + (cell >> 7)
            v = st_ref[pl.ds(start, rows, stride=span), :]
            out.append(jnp.where(found, roll(v, (m - cell) & 127, 1), accs[t]))
        return tuple(out) + (numbers,)

    zero2 = jnp.zeros((2, LANES), F32)
    accs = lax.fori_loop(0, LANES, slot, (zero8,) * STEPS + (zero2,), unroll=64)
    for t in range(STEPS):
        so_ref[t * 8 : t * 8 + 6] = accs[t][:6]
        so_ref[t * 8 + 6 : t * 8 + 8] = accs[STEPS] if t == 0 else zero2
    for copy in copies[0] + copies[1]:
        copy.wait()


SIN_C = (3.1415926401307077, -5.167710083507896, 2.550077523214726, -0.5982912856213906, 0.07765766030763246)
COS_C = (0.9999999532476085, -4.934792830619649, 4.058411352862754, -1.3318765680819573, 0.21968961109991972)
ROUND = 12582912.0


def horner(coefs, u):
    v = u * coefs[-1] + coefs[-2]
    for k in coefs[-3::-1]:
        v = v * u + k
    return v


def sincos4(turns):
    r = turns - ((turns + ROUND) - ROUND)
    u = r * r
    half_s = horner(SIN_C, u) * r
    half_c = horner(COS_C, u)
    twice = half_s + half_s
    s = twice * half_c
    c = 1.0 - twice * half_s
    s_2, c_2 = s + s, c + c
    s2 = s_2 * c
    c2 = 1.0 - s_2 * s
    s3 = c_2 * s2 - s
    c3 = c_2 * c2 - c
    s2_2 = s2 + s2
    return (s, c), (s2, c2), (s3, c3), (s2_2 * c2, 1.0 - s2_2 * s2)


def sincos(turns):
    return sincos4(turns)[0]


def split(v):
    hi = v.astype(BF16)
    return hi, (v - hi.astype(F32)).astype(BF16)


def project_kernel(
    first, size_x, size_y, size_z, tiles_x, tiles_z, own_ref, r1_ref, r2_ref, r3_ref, owner_ref, out_ref,
    inv_ref, smp_ref, pos_ref, th_ref, tl_ref, a_ref, acc_ref,
):
    gx, gz = lax.axis_index("gx"), lax.axis_index("gz")
    tiles = tiles_x * tiles_z
    base = 0.4 / (2.0 * math.pi)
    polars = ANGLES // NPHI

    def put(b, _):
        inv_ref[owner_ref[b]] = b
        return 0

    lax.fori_loop(0, tiles, put, 0, unroll=8)
    blocks = [inv_ref[(gx ^ (4 * d)) * tiles_z + gz] for d in (first, first + 1)]

    for i, ref in enumerate((own_ref, r1_ref, r2_ref, r3_ref)):
        for core in range(2):
            smp_ref[2 * i + core] = ref[core]
    row16 = iota((16, LANES), 0)
    lane16 = iota((16, LANES), 1)
    row8 = iota((8, LANES), 0)
    lane8 = iota((8, LANES), 1)

    def split3(v):
        a = v.astype(BF16).astype(F32)
        b = (v - a).astype(BF16).astype(F32)
        return a, b, v - a - b

    block = jnp.where(lane16 < 64, blocks[0], blocks[1])
    polar = 2 * block + (lane16 % 64) // 32
    st, _ = sincos((polar.astype(F32) + 0.5) * (0.5 / polars))
    sp, cp = sincos((lane16 % 32).astype(F32) * (1.0 / NPHI))
    ux = split3(base * st * cp)
    uy = split3(base * st * sp)
    mat = jnp.zeros((16, LANES), F32)
    for k in range(9):
        src = ux[k % 3] if k < 6 else uy[k % 3]
        mat = jnp.where(row16 == k, src, mat)
    dirs = mat.astype(BF16)
    combo = 2 * jnp.where(row8 % 4 < 2, blocks[0], blocks[1]) + row8 % 2
    _, uz = sincos((combo.astype(F32) + 0.5) * (0.5 / polars))
    uz = uz * base

    def wave(f, t):
        angle = 0.4 * (f + 1) * DT * (t + 1)
        return math.cos(angle), math.sin(angle)

    def gather(pair, _):
        pos = []
        for core in range(2):
            n = 2 * pair + core
            tile_x = gx ^ (2 * (pair % 2) + core)
            tile_z = gz ^ (pair // 2)
            rows = [smp_ref[n, t * 8 : t * 8 + 8] for t in range(STEPS)]
            cell = jnp.maximum(rows[0][6:7], 0.0).astype(jnp.int32)
            pz = (cell % size_z + tile_z * size_z).astype(F32) + (0.5 - size_z * tiles_z / 2)
            zs = sincos4(uz * pz)
            lanes = slice(core * LANES, (core + 1) * LANES)
            for f in range(FREQS):
                re = sum(wave(f, t)[0] * rows[t] for t in range(STEPS))
                im = sum(wave(f, t)[1] * rows[t] for t in range(STEPS))
                zsin, zcos = zs[f]
                for k in range(4):
                    sk, ck = zsin[k : k + 1], zcos[k : k + 1]
                    both = jnp.concatenate([re * ck - im * sk, re * sk + im * ck], axis=0)
                    hi, lo = split(both)
                    a_ref[pair, f, k * 16 : k * 16 + 16, lanes] = hi
                    a_ref[pair, f, 64 + k * 16 : 80 + k * 16, lanes] = lo
            gxi = cell // (size_y * size_z) + tile_x * size_x - size_x * tiles_x // 2
            high = ((gxi >> 4) << 4).astype(F32)
            low = (gxi & 15).astype(F32) + 0.5
            py = ((cell // size_z) % size_y).astype(F32) + (0.5 - size_y / 2)
            pos.append(
                jnp.where(row16 < 3, high, jnp.where(row16 < 6, low, jnp.where(row16 < 9, py, 0.0)))
            )
        pos_ref[pair] = jnp.concatenate(pos, axis=1).astype(BF16)
        return 0

    lax.fori_loop(0, 4, gather, 0, unroll=4)

    def table(i, b):
        phase = lax.dot_general(
            pos_ref[i], dirs, (((0,), (0,)), ((), ())), preferred_element_type=F32
        )
        for j in range(8):
            dst = slice(j * 32, j * 32 + 32)
            values = sincos4(phase[dst])
            for f in range(FREQS):
                for part in range(2):
                    hi, lo = split(values[f][1 - part])
                    th_ref[b * 4 + f, dst, part * LANES : (part + 1) * LANES] = hi
                    tl_ref[b * 4 + f, dst, part * LANES : (part + 1) * LANES] = lo

    def multiply(i, b):
        for f in range(FREQS):
            a = a_ref[i, f]
            o = jnp.dot(a, th_ref[b * 4 + f], preferred_element_type=F32)
            o = o[:64] + o[64:] + jnp.dot(a[:64], tl_ref[b * 4 + f], preferred_element_type=F32)
            if i == 0:
                acc_ref[f] = o
            else:
                acc_ref[f] += o

    table(0, 0)
    for k in range(4):
        if k < 3:
            table(k + 1, (k + 1) % 2)
        multiply(k, k % 2)

    near = lane8 % 64 < 32
    sign = jnp.where(near, 1.0, -1.0)

    def finish(f, _):
        for d in range(2):
            res = []
            for pol in range(2):
                r = (d * 2 + pol) * 16
                src = d * 64 + pol * 32
                pq = []
                for part in range(2):
                    for comp in range(2):
                        v = acc_ref[
                            f, r + comp * 8 : r + comp * 8 + 8, part * LANES : (part + 1) * LANES
                        ]
                        lo_v = roll(v, (pol * 64 - src) % LANES, 1)
                        hi_v = roll(v, (pol * 64 + 32 - src) % LANES, 1)
                        pq.append(jnp.where(near, lo_v, hi_v))
                pr, pi, qr, qi = pq
                res.append((pr - sign * qi, pi + sign * qr))
            out_ref[d, 0:6, f] = jnp.where(lane8 < 64, res[0][0], res[1][0])[:6]
            out_ref[d, 6:12, f] = jnp.where(lane8 < 64, res[0][1], res[1][1])[:6]
        return 0

    lax.fori_loop(0, FREQS, finish, 0, unroll=4)


def directions(angle):
    theta = math.pi * ((angle // NPHI).astype(F32) + 0.5) / (ANGLES // NPHI)
    phi = 2.0 * math.pi * (angle % NPHI).astype(F32) / NPHI
    return (jnp.sin(theta) * jnp.cos(phi), jnp.sin(theta) * jnp.sin(phi), jnp.cos(theta))


def project(acc_re, acc_im, pos_x, pos_y, pos_z, angle, omegas):
    dir_x, dir_y, dir_z = directions(angle)
    geometry = (
        dir_x[:, None] * pos_x[None] + dir_y[:, None] * pos_y[None] + dir_z[:, None] * pos_z[None]
    )
    phase = omegas[:, None, None] * geometry[None]
    cosine = jnp.cos(phase)
    sine = jnp.sin(phase)
    high = lax.Precision.HIGHEST
    real = jnp.einsum("fas,fcs->fca", cosine, acc_re, precision=high) - jnp.einsum(
        "fas,fcs->fca", sine, acc_im, precision=high
    )
    imag = jnp.einsum("fas,fcs->fca", sine, acc_re, precision=high) + jnp.einsum(
        "fas,fcs->fca", cosine, acc_im, precision=high
    )
    return jnp.concatenate([real, imag], axis=1)


def far_general(samples, cells, owner_table, sizes, tiles_x, tiles_z, scale):
    size_x, size_y, size_z = sizes
    tiles = tiles_x * tiles_z
    sample = samples.reshape(STEPS, 8, LANES)[:, :6]
    omegas = 0.4 * (jnp.arange(FREQS, dtype=F32) + 1.0)
    phase = omegas[:, None] * (DT * (jnp.arange(STEPS, dtype=F32) + 1.0))[None]
    acc_re = jnp.sum(jnp.cos(phase)[:, :, None, None] * sample[None], axis=1)
    acc_im = jnp.sum(jnp.sin(phase)[:, :, None, None] * sample[None], axis=1)
    local = jnp.maximum(cells, 0)
    glob_x = lax.axis_index("gx") * size_x + local // (size_y * size_z)
    glob_y = local // size_z % size_y
    glob_z = lax.axis_index("gz") * size_z + local % size_z
    pos_x = glob_x.astype(F32) + (0.5 - size_x * tiles_x / 2)
    pos_y = glob_y.astype(F32) + (0.5 - size_y / 2)
    pos_z = glob_z.astype(F32) + (0.5 - size_z * tiles_z / 2)
    block_len = ANGLES // tiles
    owners = jnp.arange(tiles, dtype=jnp.int32)
    blocks = jnp.sum(jnp.where(owner_table[None, :] == owners[:, None], owners[None, :], 0), axis=1)
    angle = (blocks[:, None] * block_len + jnp.arange(block_len, dtype=jnp.int32)[None]).reshape(-1)
    pattern = project(acc_re, acc_im, pos_x, pos_y, pos_z, angle, omegas)
    pattern = jnp.transpose(pattern.reshape(FREQS, 12, tiles, block_len), (2, 0, 1, 3))
    return lax.psum_scatter(pattern, ("gx", "gz"), scatter_dimension=0, tiled=True) * scale


VMEM = pl.BlockSpec(memory_space=pltpu.VMEM)
SMEM = pl.BlockSpec(memory_space=pltpu.SMEM)
ANY = pl.BlockSpec(memory_space=pl.ANY)
HBM = pl.BlockSpec(memory_space=pltpu.HBM)


def in_hbm(v):
    return pltpu.with_memory_space_constraint(v, pltpu.HBM)


def shards(nx, nz, e_init, h_init, material, eps_table, sigma_table, face_cells, owner_table):
    size_x, size_y, size_z = material.shape
    ns = 1 if nz == 2 else 2
    plane = (size_y, size_z)
    both = ("gx", "gz")

    def pair_a(i):
        return i ^ 1

    def pair_b(i):
        return i + 1 if i % 2 else i - 1

    def pair_z(k, s):
        return k + 1 if (k + s) % 2 == 0 else k - 1

    xa, xb, zp, zd = pl.pallas_call(
        functools.partial(pack_kernel, ns),
        out_shape=(
            jax.ShapeDtypeStruct((7 * W + 4 * ns,) + plane, F32),
            jax.ShapeDtypeStruct((7 * W,) + plane, F32),
            jax.ShapeDtypeStruct((ns, 8) + plane, F32),
            jax.ShapeDtypeStruct((ns, 4) + plane, F32),
        ),
        in_specs=[ANY] * 3,
        out_specs=(VMEM,) * 4,
        scratch_shapes=[
            pltpu.VMEM((6, size_x) + plane, F32),
            pltpu.VMEM((size_x,) + plane, jnp.int32),
            pltpu.SemaphoreType.DMA((7,)),
        ],
        compiler_params=pltpu.CompilerParams(vmem_limit_bytes=16 * 1024 * 1024),
        name="pack",
    )(in_hbm(e_init), in_hbm(h_init), in_hbm(material))
    xb_in = lax.ppermute(
        xb, "gx", [(i, pair_b(i)) for i in range(nx) if 0 <= pair_b(i) < nx]
    )

    swap = [(i, pair_a(i)) for i in range(nx)]
    xa_in = lax.ppermute(xa, "gx", swap)

    def turned(v, s, pair_x):
        links = [
            (i * nz + k, pair_x(i) * nz + pair_z(k, s))
            for i in range(nx)
            for k in range(nz)
            if 0 <= pair_x(i) < nx and 0 <= pair_z(k, s) < nz
        ]
        return lax.ppermute(v, both, links)

    z_in = []
    for s in range(ns):
        links = [(k, pair_z(k, s)) for k in range(nz) if 0 <= pair_z(k, s) < nz]
        z_in.append(lax.ppermute(zp[s], "gz", links))
    z_in = jnp.stack(z_in)
    za_in = jnp.stack([turned(zd[s], s, pair_a) for s in range(ns)])
    zb_in = jnp.stack([turned(zd[s], s, pair_b) for s in range(ns)])

    wide = size_x + 2 * W
    e_field, h_field, samples = pl.pallas_call(
        functools.partial(field_kernel, ns, nx, nz),
        out_shape=(
            jax.ShapeDtypeStruct((3, size_x * size_y, size_z), F32),
            jax.ShapeDtypeStruct((3, size_x * size_y, size_z), F32),
            jax.ShapeDtypeStruct((8 * STEPS, LANES), F32),
        ),
        in_specs=[VMEM] * 9 + [HBM] * 3,
        out_specs=(ANY, ANY, VMEM),
        scratch_shapes=[
            pltpu.VMEM(((STEPS + 1) * 8 * wide * size_y, LANES), F32),
            pltpu.VMEM((2 * wide * size_y, LANES), F32),
            pltpu.VMEM((STEPS * 2 * 3 * size_y, LANES), F32),
            pltpu.VMEM((8 * 3 * size_y, LANES), F32),
            pltpu.VMEM((2 * 3 * size_y, LANES), F32),
            pltpu.VMEM((4,) + plane, F32),
            pltpu.SMEM((1, eps_table.shape[0]), F32),
            pltpu.SMEM((1, eps_table.shape[0]), F32),
            pltpu.SMEM((1, LANES), jnp.int32),
            pltpu.SemaphoreType.DMA((12,)),
            pltpu.SemaphoreType.DMA((3,)),
        ],
        compiler_params=pltpu.CompilerParams(vmem_limit_bytes=48 * 1024 * 1024),
        name="fields",
    )(
        e_init, h_init, material, xa_in, xb_in, z_in, za_in, zb_in, zp,
        in_hbm(eps_table.reshape(1, -1)), in_hbm(sigma_table.reshape(1, -1)), in_hbm(face_cells),
    )
    e_field = e_field.reshape(e_init.shape)
    h_field = h_field.reshape(h_init.shape)

    tiles = nx * nz
    scale = 1.0 / math.sqrt(tiles * face_cells.shape[1] * STEPS)
    if not (nx == 16 and nz == 2):
        far = far_general(
            samples, face_cells[0], owner_table, material.shape, nx, nz, scale
        )
        return e_field, h_field, far

    def swap_all(v, mx, mz):
        links = [(i * nz + k, (i ^ mx) * nz + (k ^ mz)) for i in range(nx) for k in range(nz)]
        return lax.ppermute(v, both, links)

    mine = jnp.stack([samples, swap_all(samples, 1, 0)])
    by_y = swap_all(mine, 2, 0)
    by_x = swap_all(mine, 0, 1)
    by_xy = swap_all(mine, 2, 1)
    far_two, near_two = (
        pl.pallas_call(
            functools.partial(project_kernel, first, size_x, size_y, size_z, nx, nz),
            out_shape=jax.ShapeDtypeStruct((2, 12, FREQS, LANES), F32),
            in_specs=[VMEM] * 4 + [SMEM],
            out_specs=VMEM,
            scratch_shapes=[
                pltpu.SMEM((tiles,), jnp.int32),
                pltpu.VMEM((8, 8 * STEPS, LANES), F32),
                pltpu.VMEM((4, 16, 2 * LANES), BF16),
                pltpu.VMEM((2 * FREQS, 2 * LANES, 2 * LANES), BF16),
                pltpu.VMEM((2 * FREQS, 2 * LANES, 2 * LANES), BF16),
                pltpu.VMEM((4, FREQS, 128, 2 * LANES), BF16),
                pltpu.VMEM((FREQS, 64, 2 * LANES), F32),
            ],
            compiler_params=pltpu.CompilerParams(vmem_limit_bytes=32 * 1024 * 1024),
            cost_estimate=pl.CostEstimate(
                flops=1_000_000_000, bytes_accessed=8_000_000, transcendentals=0
            ),
            name="project",
        )(mine, by_y, by_x, by_xy, owner_table)
        for first in (2, 0)
    )
    near_two = near_two + swap_all(far_two, 8, 0)
    total = near_two[0] + swap_all(near_two[1], 4, 0)
    far = jnp.transpose(total * scale, (1, 0, 2))
    return e_field, h_field, far[None]


def solution(mesh):
    nx, nz = mesh.shape["gx"], mesh.shape["gz"]
    return jax.shard_map(
        functools.partial(shards, nx, nz),
        mesh=mesh,
        in_specs=(
            P(None, "gx", None, "gz"),
            P(None, "gx", None, "gz"),
            P("gx", None, "gz"),
            P(),
            P(),
            P(("gx", "gz"), None),
            P(),
        ),
        out_specs=(
            P(None, "gx", None, "gz"),
            P(None, "gx", None, "gz"),
            P(("gx", "gz"), None, None, None),
        ),
        check_vma=False,
    )
```

```python
import functools
import math

import jax
import jax.numpy as jnp
from jax import lax
from jax.experimental import pallas as pl
from jax.experimental.pallas import tpu as pltpu
from jax.sharding import PartitionSpec as P

STEPS = 4
ANGLES = 4096
NPHI = 64
FREQS = 4
DT = 0.5

W = 4
BLOCK = 40
LANES = 128
F32 = jnp.float32
BF16 = jnp.bfloat16


def roll(v, shift, axis):
    return pltpu.roll(v, shift, axis)


def iota(shape, axis):
    return lax.broadcasted_iota(jnp.int32, shape, axis)


def fold_pair(a, b, up, lane):
    own = jnp.where(up, lane, 127 - lane) >= 124
    return jnp.where(own, b, roll(a, jnp.where(up, 124, 4), 1))


def pack_kernel(ns, e_hbm, h_hbm, m_hbm, xa_ref, xb_ref, zp_ref, zd_ref, f_ref, m_ref, sem):
    size_x, size_y = m_ref.shape[0], m_ref.shape[1]
    gx, gz = lax.axis_index("gx"), lax.axis_index("gz")
    copies = [
        pltpu.make_async_copy((e_hbm if c < 3 else h_hbm).at[c % 3], f_ref.at[c], sem.at[c])
        for c in range(6)
    ]
    copies.append(pltpu.make_async_copy(m_hbm, m_ref, sem.at[6]))
    for copy in copies:
        copy.start()
    even = gx % 2 == 0
    lane = iota((size_y, LANES), 1)
    group = lane // 8

    def plane(c, x):
        return f_ref[c, x] if c < 6 else m_ref[x].astype(F32)

    for i in range(4):
        comps = (2 * i, 2 * i + 1) if i < 3 else (6, 6)
        for c in sorted(set(comps)):
            copies[c].wait()
            for ref, off in ((xa_ref, size_x - W), (xb_ref, 0)):
                off = jnp.where(even, off, size_x - W - off)
                for j in range(W):
                    ref[c * W + j] = plane(c, off + j)
        for s in range(ns):
            up = (gz + s) % 2 == 0
            base = jnp.where(up, 8, 0)

            def fold(g, acc):
                out = []
                for q in range(2):
                    x = (g + 28) % 32 if q == 0 else g + 12
                    cell = fold_pair(plane(comps[0], x), plane(comps[1], x), up, lane)
                    cell = roll(cell, (base + 8 * g) % LANES, 1)
                    out.append(jnp.where(group == g, cell, acc[q]))
                return tuple(out)

            zero = jnp.zeros((size_y, LANES), F32)
            acc = lax.fori_loop(0, 16, fold, (zero, zero), unroll=16)
            zp_ref[s, i] = acc[0]
            zp_ref[s, 4 + i] = acc[1]
            xa_ref[7 * W + 4 * s + i] = acc[0]
            zd_ref[s, i] = acc[0]


def coef_tables(eps_ref, sigma_ref, shape):
    lane = iota(shape, 1)
    eps = jnp.ones(shape, F32)
    sigma = jnp.zeros(shape, F32)
    for i in range(eps_ref.shape[1]):
        eps = jnp.where(lane == i, eps_ref[0, i], eps)
        sigma = jnp.where(lane == i, sigma_ref[0, i], sigma)
    loss = sigma * DT / (2.0 * eps)
    return (1.0 - loss) / (1.0 + loss), DT / (eps * (1.0 + loss))


def pick(table, index):
    return jnp.take_along_axis(table, index, axis=1, mode="promise_in_bounds")


def field_kernel(
    ns,
    nx,
    nz,
    e_ref,
    h_ref,
    m_ref,
    xa_ref,
    xb_ref,
    zr_ref,
    za_ref,
    zb_ref,
    zp_ref,
    eps_hbm,
    sigma_hbm,
    cells_hbm,
    eo_ref,
    ho_ref,
    so_ref,
    st_ref,
    co_ref,
    in_ref,
    sp_ref,
    sc_ref,
    qb_ref,
    eps_ref,
    sigma_ref,
    cells_ref,
    sem,
    in_sem,
):
    size_x, size_y = m_ref.shape[0], m_ref.shape[1]
    wide = size_x + 2 * W
    span = wide * size_y
    shape = (size_y, LANES)
    gx, gz = lax.axis_index("gx"), lax.axis_index("gz")
    even = gx % 2 == 0
    lower = gx > 0
    upper = gx < nx - 1
    lane = iota(shape, 1)
    row = iota(shape, 0)
    small = [
        pltpu.make_async_copy(src, dst, in_sem.at[i])
        for i, (src, dst) in enumerate(
            (
                (eps_hbm, eps_ref),
                (sigma_hbm, sigma_ref),
                (cells_hbm, cells_ref),
            )
        )
    ]
    for copy in small:
        copy.start()

    def at(t, c, x):
        return pl.ds(((t * 8 + c) * wide + x) * size_y, size_y)

    def coef_at(c, x):
        return pl.ds((c * wide + x) * size_y, size_y)

    def block(i):
        return pl.ds(i * size_y, size_y)

    pos_a = jnp.where(even, size_x + W, 0)
    pos_b = jnp.where(even, 0, size_x + W)
    ok_b = jnp.where(even, lower, upper).astype(F32)
    sides = ((xa_ref, pos_a, None), (xb_ref, pos_b, ok_b))

    def halo_plane(j, _):
        for ref, pos, _ in sides:
            for c in range(6):
                st_ref[at(0, c, pos + j)] = ref[c * W + j]
        return 0

    lax.fori_loop(0, W, halo_plane, 0, unroll=2)

    group = lane // 8
    first_half = lane % 8 < 4
    fy_keep = row < size_y - 1
    by_keep = row > 0

    def fwd_y(v):
        return jnp.where(fy_keep, roll(v, size_y - 1, 0), 0.0)

    def bwd_y(v):
        return jnp.where(by_keep, roll(v, 1, 0), 0.0)

    def fwd_z(v):
        return roll(v, 127, 1)

    def bwd_z(v):
        return roll(v, 1, 1)

    inside = [
        jnp.where(jnp.logical_and(group < W, jnp.logical_not(lower)), 0.0, 1.0),
        jnp.ones(shape, F32),
        jnp.where(jnp.logical_and(group >= W, jnp.logical_not(upper)), 0.0, 1.0),
    ]
    for s in range(ns):
        up = (gz + s) % 2 == 0
        partner = jnp.where(up, gz + 1, gz - 1)
        ok = jnp.logical_and(partner >= 0, partner < nz)
        give_e = jnp.where(jnp.logical_and(up, ok), 1.0, 0.0)
        give_h = jnp.where(jnp.logical_and(jnp.logical_not(up), ok), 1.0, 0.0)
        base = jnp.where(up, 8, 0)

        def corner(j, acc):
            g = j + jnp.where(even, 0, W)
            comps = [xb_ref[c * W + j] for c in range(7)]
            comps.append(comps[6])
            out = []
            for i in range(4):
                cell = fold_pair(comps[2 * i], comps[2 * i + 1], up, lane)
                cell = roll(cell, (base + 8 * g) % LANES, 1)
                out.append(jnp.where(group == g, cell, acc[i]))
            return tuple(out)

        zero = jnp.zeros(shape, F32)
        acc = lax.fori_loop(0, W, corner, (zero,) * 4, unroll=4)
        for i in range(4):
            qb_ref[i] = acc[i]

        def unfold(i, _):
            def whole(mine, other):
                lo = jnp.where(up, mine, other)
                hi = jnp.where(up, other, mine)
                return (
                    jnp.where(first_half, lo, hi),
                    jnp.where(first_half, roll(lo, 124, 1), roll(hi, 4, 1)),
                )

            q0 = whole(zp_ref[s, i], zr_ref[s, i])
            q1 = whole(zp_ref[s, 4 + i], zr_ref[s, 4 + i])
            qa = whole(xa_ref[7 * W + 4 * s + i], za_ref[s, i])
            qb = whole(qb_ref[i], zb_ref[s, i])
            for k in range(2):
                below = jnp.where(even, qb[k], qa[k])
                above = jnp.where(even, qa[k], qb[k])
                c = (2 * i + k) * 3
                sp_ref[block(c)] = jnp.where(group < W, below, q0[k])
                sp_ref[block(c + 1)] = q1[k]
                sp_ref[block(c + 2)] = jnp.where(group < W, q0[k], above)
            return 0

        lax.fori_loop(0, 4, unfold, 0, unroll=4)
        if s == 0:
            for copy in small:
                copy.wait()
            ca_t, cb_t = coef_tables(eps_ref, sigma_ref, shape)

            def halo_coef(j, _):
                for ref, pos, ok_side in sides:
                    index = ref[6 * W + j].astype(jnp.int32)
                    ca, cb = pick(ca_t, index), pick(cb_t, index)
                    if ok_side is not None:
                        ca, cb = ca * ok_side, cb * ok_side
                    co_ref[coef_at(0, pos + j)] = ca
                    co_ref[coef_at(1, pos + j)] = cb
                return 0

            lax.fori_loop(0, W, halo_coef, 0, unroll=4)
        for q in range(3):
            index = sp_ref[block(18 + q)].astype(jnp.int32)
            sc_ref[block(q)] = pick(ca_t, index) * inside[q]
            sc_ref[block(3 + q)] = pick(cb_t, index) * inside[q]

        def fwd_x(v):
            r = [roll(u, 120, 1) for u in v]
            return [jnp.where(lane < 120, r[0], r[1]), jnp.where(lane < 120, r[1], r[2]), r[2]]

        def bwd_x(v):
            r = [roll(u, 8, 1) for u in v]
            return [r[0], jnp.where(lane >= 8, r[1], r[0]), jnp.where(lane >= 8, r[2], r[1])]

        def each(f, *vs):
            return [f(*u) for u in zip(*vs)]

        def own_planes(t):
            for j in range(size_x // STEPS):
                x = t * (size_x // STEPS) + j
                for c in range(3):
                    st_ref[at(0, c, x + W)] = e_ref[c, x]
                    st_ref[at(0, 3 + c, x + W)] = h_ref[c, x]
                index = m_ref[x]
                co_ref[coef_at(0, x + W)] = pick(ca_t, index)
                co_ref[coef_at(1, x + W)] = pick(cb_t, index)

        def strip_step(t, _):
            ex, ey, ez, hx, hy, hz = (
                [sp_ref[block(c * 3 + q)] for q in range(3)] for c in range(6)
            )
            ca_s = [sc_ref[block(q)] for q in range(3)]
            cb_s = [sc_ref[block(3 + q)] for q in range(3)]
            dt_s = [DT * k for k in inside]
            side_e = [[v * give_e for v in ex], [v * give_e for v in ey]]
            ez_x, ey_x = fwd_x(ez), fwd_x(ey)
            hx = each(
                lambda h, z, y, d: h - d * ((fwd_y(z) - z) - (fwd_z(y) - y)), hx, ez, ey, dt_s
            )
            hy = each(
                lambda h, x, z, zx, d: h - d * ((fwd_z(x) - x) - (zx - z)), hy, ex, ez, ez_x, dt_s
            )
            hz = each(
                lambda h, y, yx, x, d: h - d * ((yx - y) - (fwd_y(x) - x)), hz, ey, ey_x, ex, dt_s
            )
            if s == 0:
                own_planes(t)
            hz_x, hy_x = bwd_x(hz), bwd_x(hy)
            ex = each(
                lambda e, z, y, a, b: a * e + b * ((z - bwd_y(z)) - (y - bwd_z(y))),
                ex, hz, hy, ca_s, cb_s,
            )
            ey = each(
                lambda e, x, z, zx, a, b: a * e + b * ((x - bwd_z(x)) - (z - zx)),
                ey, hx, hz, hz_x, ca_s, cb_s,
            )
            ez = each(
                lambda e, y, yx, x, a, b: a * e + b * ((y - yx) - (x - bwd_y(x))),
                ez, hy, hy_x, hx, ca_s, cb_s,
            )
            for c, v in enumerate((ex, ey, ez, hx, hy, hz)):
                for q in range(3):
                    sp_ref[block(c * 3 + q)] = v[q]
            for j, v in enumerate((hx, hy)):
                for q in range(3):
                    dst = block((t * 2 + j) * 3 + q)
                    add = jnp.where(lane % 8 == 4, side_e[j][q], roll(v[q] * give_h, 2, 1))
                    in_ref[dst] = add if s == 0 else in_ref[dst] + add
            return 0

        lax.fori_loop(0, STEPS, strip_step, 0, unroll=4)

    dt_lo = jnp.where(lower, DT, 0.0)
    dt_hi = jnp.where(upper, DT, 0.0)

    planes = range(BLOCK)

    def advance(t, x, carry):
        hy_p, hz_p = carry
        old = [[st_ref[at(t - 1, c, x + i)] for i in range(BLOCK + (c < 3))] for c in range(6)]
        ca = [co_ref[coef_at(0, x + i)] for i in planes]
        cb = [co_ref[coef_at(1, x + i)] for i in planes]
        ex, ey, ez, hx, hy, hz = old
        side_x, side_y = [], []
        for i in planes:
            shift = (123 - 8 * ((x + i) % 16)) % LANES
            side_x.append(roll(in_ref[block((t - 1) * 6 + (x + i) // 16)], shift, 1))
            side_y.append(roll(in_ref[block((t - 1) * 6 + 3 + (x + i) // 16)], shift, 1))
        ex_z = [jnp.where(last, side_x[i], fwd_z(ex[i])) for i in planes]
        ey_z = [jnp.where(last, side_y[i], fwd_z(ey[i])) for i in planes]
        ez_y = [fwd_y(ez[i]) for i in planes]
        ex_y = [fwd_y(ex[i]) for i in planes]
        dt = [
            jnp.where(x + i < W, dt_lo, jnp.where(x + i >= size_x + W, dt_hi, DT)) for i in planes
        ]
        hx = [hx[i] - dt[i] * ((ez_y[i] - ez[i]) - (ey_z[i] - ey[i])) for i in planes]
        hy = [hy[i] - dt[i] * ((ex_z[i] - ex[i]) - (ez[i + 1] - ez[i])) for i in planes]
        hz = [hz[i] - dt[i] * ((ey[i + 1] - ey[i]) - (ex_y[i] - ex[i])) for i in planes]
        hx_z = [jnp.where(first, side_x[i], bwd_z(hx[i])) for i in planes]
        hy_z = [jnp.where(first, side_y[i], bwd_z(hy[i])) for i in planes]
        hy_x, hz_x = [hy_p] + hy, [hz_p] + hz
        new = [
            [ca[i] * ex[i] + cb[i] * ((hz[i] - bwd_y(hz[i])) - (hy[i] - hy_z[i])) for i in planes],
            [ca[i] * ey[i] + cb[i] * ((hx[i] - hx_z[i]) - (hz[i] - hz_x[i])) for i in planes],
            [ca[i] * ez[i] + cb[i] * ((hy[i] - hy_x[i]) - (hx[i] - bwd_y(hx[i]))) for i in planes],
            hx, hy, hz,
        ]
        for c in range(6):
            for i in planes:
                st_ref[at(t, c, x + i)] = new[c][i]
        return hy[-1], hz[-1]

    last, first = lane == 127, lane == 0

    half = size_x // 2
    copies = []
    for part in range(2):
        copies.append([])
        for c in range(3):
            for ref, cc in ((eo_ref, c), (ho_ref, 3 + c)):
                src = ((STEPS * 8 + cc) * wide + W + part * half) * size_y
                copies[part].append(
                    pltpu.make_async_copy(
                        st_ref.at[pl.ds(src, half * size_y)],
                        ref.at[c, pl.ds(part * half * size_y, half * size_y)],
                        sem.at[part * 6 + cc],
                    )
                )
    blocks = wide // BLOCK
    def step(t, _):
        zero = jnp.zeros(shape, F32)

        def planes_from(i, c):
            c = advance(t, i * BLOCK, c)

            @pl.when(jnp.logical_and(t == STEPS, i == blocks // 2 - 1 + blocks % 2))
            def _():
                for copy in copies[0]:
                    copy.start()

            return c

        lax.fori_loop(0, blocks, planes_from, (zero, zero))
        return 0

    lax.fori_loop(1, STEPS + 1, step, 0, unroll=2)
    for copy in copies[1]:
        copy.start()

    rows = 6
    lane8 = iota((rows, LANES), 1)
    zero8 = jnp.zeros((rows, LANES), F32)

    def slot(m, accs):
        cell = cells_ref[0, m]
        here = lane8 == m
        found = lane8 == jnp.where(cell >= 0, m, -1)
        numbers = jnp.where(here[:2], cell.astype(F32), accs[STEPS])
        cell = jnp.maximum(cell, 0)
        out = []
        for t in range(STEPS):
            start = (t + 1) * 8 * span + W * size_y + (cell >> 7)
            v = st_ref[pl.ds(start, rows, stride=span), :]
            out.append(jnp.where(found, roll(v, (m - cell) & 127, 1), accs[t]))
        return tuple(out) + (numbers,)

    zero2 = jnp.zeros((2, LANES), F32)
    accs = lax.fori_loop(0, LANES, slot, (zero8,) * STEPS + (zero2,), unroll=64)
    for t in range(STEPS):
        so_ref[t * 8 : t * 8 + 6] = accs[t][:6]
        so_ref[t * 8 + 6 : t * 8 + 8] = accs[STEPS] if t == 0 else zero2
    for copy in copies[0] + copies[1]:
        copy.wait()


SIN_C = (3.1415926401307077, -5.167710083507896, 2.550077523214726, -0.5982912856213906, 0.07765766030763246)
COS_C = (0.9999999532476085, -4.934792830619649, 4.058411352862754, -1.3318765680819573, 0.21968961109991972)
ROUND = 12582912.0


def horner(coefs, u):
    v = u * coefs[-1] + coefs[-2]
    for k in coefs[-3::-1]:
        v = v * u + k
    return v


def sincos4(turns):
    r = turns - ((turns + ROUND) - ROUND)
    u = r * r
    half_s = horner(SIN_C, u) * r
    half_c = horner(COS_C, u)
    twice = half_s + half_s
    s = twice * half_c
    c = 1.0 - twice * half_s
    s_2, c_2 = s + s, c + c
    s2 = s_2 * c
    c2 = 1.0 - s_2 * s
    s3 = c_2 * s2 - s
    c3 = c_2 * c2 - c
    s2_2 = s2 + s2
    return (s, c), (s2, c2), (s3, c3), (s2_2 * c2, 1.0 - s2_2 * s2)


def sincos(turns):
    return sincos4(turns)[0]


def split(v):
    hi = v.astype(BF16)
    return hi, (v - hi.astype(F32)).astype(BF16)


def project_kernel(
    first, size_x, size_y, size_z, tiles_x, tiles_z, own_ref, r1_ref, r2_ref, r3_ref, owner_ref, out_ref,
    inv_ref, smp_ref, pos_ref, th_ref, tl_ref, a_ref, acc_ref,
):
    gx, gz = lax.axis_index("gx"), lax.axis_index("gz")
    tiles = tiles_x * tiles_z
    base = 0.4 / (2.0 * math.pi)
    polars = ANGLES // NPHI

    def put(b, _):
        inv_ref[owner_ref[b]] = b
        return 0

    lax.fori_loop(0, tiles, put, 0, unroll=8)
    blocks = [inv_ref[(gx ^ (4 * d)) * tiles_z + gz] for d in (first, first + 1)]

    for i, ref in enumerate((own_ref, r1_ref, r2_ref, r3_ref)):
        for core in range(2):
            smp_ref[2 * i + core] = ref[core]
    row16 = iota((16, LANES), 0)
    lane16 = iota((16, LANES), 1)
    row8 = iota((8, LANES), 0)
    lane8 = iota((8, LANES), 1)

    def split3(v):
        a = v.astype(BF16).astype(F32)
        b = (v - a).astype(BF16).astype(F32)
        return a, b, v - a - b

    block = jnp.where(lane16 < 64, blocks[0], blocks[1])
    polar = 2 * block + (lane16 % 64) // 32
    st, _ = sincos((polar.astype(F32) + 0.5) * (0.5 / polars))
    sp, cp = sincos((lane16 % 32).astype(F32) * (1.0 / NPHI))
    ux = split3(base * st * cp)
    uy = split3(base * st * sp)
    mat = jnp.zeros((16, LANES), F32)
    for k in range(9):
        src = ux[k % 3] if k < 6 else uy[k % 3]
        mat = jnp.where(row16 == k, src, mat)
    dirs = mat.astype(BF16)
    combo = 2 * jnp.where(row8 % 4 < 2, blocks[0], blocks[1]) + row8 % 2
    _, uz = sincos((combo.astype(F32) + 0.5) * (0.5 / polars))
    uz = uz * base

    def wave(f, t):
        angle = 0.4 * (f + 1) * DT * (t + 1)
        return math.cos(angle), math.sin(angle)

    def gather(pair, _):
        pos = []
        for core in range(2):
            n = 2 * pair + core
            tile_x = gx ^ (2 * (pair % 2) + core)
            tile_z = gz ^ (pair // 2)
            rows = [smp_ref[n, t * 8 : t * 8 + 8] for t in range(STEPS)]
            cell = jnp.maximum(rows[0][6:7], 0.0).astype(jnp.int32)
            pz = (cell % size_z + tile_z * size_z).astype(F32) + (0.5 - size_z * tiles_z / 2)
            zs = sincos4(uz * pz)
            lanes = slice(core * LANES, (core + 1) * LANES)
            for f in range(FREQS):
                re = sum(wave(f, t)[0] * rows[t] for t in range(STEPS))
                im = sum(wave(f, t)[1] * rows[t] for t in range(STEPS))
                zsin, zcos = zs[f]
                for k in range(4):
                    sk, ck = zsin[k : k + 1], zcos[k : k + 1]
                    both = jnp.concatenate([re * ck - im * sk, re * sk + im * ck], axis=0)
                    hi, lo = split(both)
                    a_ref[pair, f, k * 16 : k * 16 + 16, lanes] = hi
                    a_ref[pair, f, 64 + k * 16 : 80 + k * 16, lanes] = lo
            gxi = cell // (size_y * size_z) + tile_x * size_x - size_x * tiles_x // 2
            high = ((gxi >> 4) << 4).astype(F32)
            low = (gxi & 15).astype(F32) + 0.5
            py = ((cell // size_z) % size_y).astype(F32) + (0.5 - size_y / 2)
            pos.append(
                jnp.where(row16 < 3, high, jnp.where(row16 < 6, low, jnp.where(row16 < 9, py, 0.0)))
            )
        pos_ref[pair] = jnp.concatenate(pos, axis=1).astype(BF16)
        return 0

    lax.fori_loop(0, 4, gather, 0, unroll=4)

    def table(i, b):
        phase = lax.dot_general(
            pos_ref[i], dirs, (((0,), (0,)), ((), ())), preferred_element_type=F32
        )
        for j in range(8):
            dst = slice(j * 32, j * 32 + 32)
            values = sincos4(phase[dst])
            for f in range(FREQS):
                for part in range(2):
                    hi, lo = split(values[f][1 - part])
                    th_ref[b * 4 + f, dst, part * LANES : (part + 1) * LANES] = hi
                    tl_ref[b * 4 + f, dst, part * LANES : (part + 1) * LANES] = lo

    def multiply(i, b):
        for f in range(FREQS):
            a = a_ref[i, f]
            o = jnp.dot(a, th_ref[b * 4 + f], preferred_element_type=F32)
            o = o[:64] + o[64:] + jnp.dot(a[:64], tl_ref[b * 4 + f], preferred_element_type=F32)
            if i == 0:
                acc_ref[f] = o
            else:
                acc_ref[f] += o

    table(0, 0)
    for k in range(4):
        if k < 3:
            table(k + 1, (k + 1) % 2)
        multiply(k, k % 2)

    near = lane8 % 64 < 32
    sign = jnp.where(near, 1.0, -1.0)

    def finish(f, _):
        for d in range(2):
            res = []
            for pol in range(2):
                r = (d * 2 + pol) * 16
                src = d * 64 + pol * 32
                pq = []
                for part in range(2):
                    for comp in range(2):
                        v = acc_ref[
                            f, r + comp * 8 : r + comp * 8 + 8, part * LANES : (part + 1) * LANES
                        ]
                        lo_v = roll(v, (pol * 64 - src) % LANES, 1)
                        hi_v = roll(v, (pol * 64 + 32 - src) % LANES, 1)
                        pq.append(jnp.where(near, lo_v, hi_v))
                pr, pi, qr, qi = pq
                res.append((pr - sign * qi, pi + sign * qr))
            out_ref[d, 0:6, f] = jnp.where(lane8 < 64, res[0][0], res[1][0])[:6]
            out_ref[d, 6:12, f] = jnp.where(lane8 < 64, res[0][1], res[1][1])[:6]
        return 0

    lax.fori_loop(0, FREQS, finish, 0, unroll=4)


def directions(angle):
    theta = math.pi * ((angle // NPHI).astype(F32) + 0.5) / (ANGLES // NPHI)
    phi = 2.0 * math.pi * (angle % NPHI).astype(F32) / NPHI
    return (jnp.sin(theta) * jnp.cos(phi), jnp.sin(theta) * jnp.sin(phi), jnp.cos(theta))


def project(acc_re, acc_im, pos_x, pos_y, pos_z, angle, omegas):
    dir_x, dir_y, dir_z = directions(angle)
    geometry = (
        dir_x[:, None] * pos_x[None] + dir_y[:, None] * pos_y[None] + dir_z[:, None] * pos_z[None]
    )
    phase = omegas[:, None, None] * geometry[None]
    cosine = jnp.cos(phase)
    sine = jnp.sin(phase)
    high = lax.Precision.HIGHEST
    real = jnp.einsum("fas,fcs->fca", cosine, acc_re, precision=high) - jnp.einsum(
        "fas,fcs->fca", sine, acc_im, precision=high
    )
    imag = jnp.einsum("fas,fcs->fca", sine, acc_re, precision=high) + jnp.einsum(
        "fas,fcs->fca", cosine, acc_im, precision=high
    )
    return jnp.concatenate([real, imag], axis=1)


def far_general(samples, cells, owner_table, sizes, tiles_x, tiles_z, scale):
    size_x, size_y, size_z = sizes
    tiles = tiles_x * tiles_z
    sample = samples.reshape(STEPS, 8, LANES)[:, :6]
    omegas = 0.4 * (jnp.arange(FREQS, dtype=F32) + 1.0)
    phase = omegas[:, None] * (DT * (jnp.arange(STEPS, dtype=F32) + 1.0))[None]
    acc_re = jnp.sum(jnp.cos(phase)[:, :, None, None] * sample[None], axis=1)
    acc_im = jnp.sum(jnp.sin(phase)[:, :, None, None] * sample[None], axis=1)
    local = jnp.maximum(cells, 0)
    glob_x = lax.axis_index("gx") * size_x + local // (size_y * size_z)
    glob_y = local // size_z % size_y
    glob_z = lax.axis_index("gz") * size_z + local % size_z
    pos_x = glob_x.astype(F32) + (0.5 - size_x * tiles_x / 2)
    pos_y = glob_y.astype(F32) + (0.5 - size_y / 2)
    pos_z = glob_z.astype(F32) + (0.5 - size_z * tiles_z / 2)
    block_len = ANGLES // tiles
    owners = jnp.arange(tiles, dtype=jnp.int32)
    blocks = jnp.sum(jnp.where(owner_table[None, :] == owners[:, None], owners[None, :], 0), axis=1)
    angle = (blocks[:, None] * block_len + jnp.arange(block_len, dtype=jnp.int32)[None]).reshape(-1)
    pattern = project(acc_re, acc_im, pos_x, pos_y, pos_z, angle, omegas)
    pattern = jnp.transpose(pattern.reshape(FREQS, 12, tiles, block_len), (2, 0, 1, 3))
    return lax.psum_scatter(pattern, ("gx", "gz"), scatter_dimension=0, tiled=True) * scale


VMEM = pl.BlockSpec(memory_space=pltpu.VMEM)
SMEM = pl.BlockSpec(memory_space=pltpu.SMEM)
ANY = pl.BlockSpec(memory_space=pl.ANY)
HBM = pl.BlockSpec(memory_space=pltpu.HBM)


def in_hbm(v):
    return pltpu.with_memory_space_constraint(v, pltpu.HBM)


def shards(nx, nz, e_init, h_init, material, eps_table, sigma_table, face_cells, owner_table):
    size_x, size_y, size_z = material.shape
    ns = 1 if nz == 2 else 2
    plane = (size_y, size_z)
    both = ("gx", "gz")

    def pair_a(i):
        return i ^ 1

    def pair_b(i):
        return i + 1 if i % 2 else i - 1

    def pair_z(k, s):
        return k + 1 if (k + s) % 2 == 0 else k - 1

    xa, xb, zp, zd = pl.pallas_call(
        functools.partial(pack_kernel, ns),
        out_shape=(
            jax.ShapeDtypeStruct((7 * W + 4 * ns,) + plane, F32),
            jax.ShapeDtypeStruct((7 * W,) + plane, F32),
            jax.ShapeDtypeStruct((ns, 8) + plane, F32),
            jax.ShapeDtypeStruct((ns, 4) + plane, F32),
        ),
        in_specs=[ANY] * 3,
        out_specs=(VMEM,) * 4,
        scratch_shapes=[
            pltpu.VMEM((6, size_x) + plane, F32),
            pltpu.VMEM((size_x,) + plane, jnp.int32),
            pltpu.SemaphoreType.DMA((7,)),
        ],
        compiler_params=pltpu.CompilerParams(vmem_limit_bytes=16 * 1024 * 1024),
        name="pack",
    )(in_hbm(e_init), in_hbm(h_init), in_hbm(material))
    xb_in = lax.ppermute(
        xb, "gx", [(i, pair_b(i)) for i in range(nx) if 0 <= pair_b(i) < nx]
    )

    swap = [(i, pair_a(i)) for i in range(nx)]
    xa_in = lax.ppermute(xa, "gx", swap)

    def turned(v, s, pair_x):
        links = [
            (i * nz + k, pair_x(i) * nz + pair_z(k, s))
            for i in range(nx)
            for k in range(nz)
            if 0 <= pair_x(i) < nx and 0 <= pair_z(k, s) < nz
        ]
        return lax.ppermute(v, both, links)

    z_in = []
    for s in range(ns):
        links = [(k, pair_z(k, s)) for k in range(nz) if 0 <= pair_z(k, s) < nz]
        z_in.append(lax.ppermute(zp[s], "gz", links))
    z_in = jnp.stack(z_in)
    za_in = jnp.stack([turned(zd[s], s, pair_a) for s in range(ns)])
    zb_in = jnp.stack([turned(zd[s], s, pair_b) for s in range(ns)])

    wide = size_x + 2 * W
    e_field, h_field, samples = pl.pallas_call(
        functools.partial(field_kernel, ns, nx, nz),
        out_shape=(
            jax.ShapeDtypeStruct((3, size_x * size_y, size_z), F32),
            jax.ShapeDtypeStruct((3, size_x * size_y, size_z), F32),
            jax.ShapeDtypeStruct((8 * STEPS, LANES), F32),
        ),
        in_specs=[VMEM] * 9 + [HBM] * 3,
        out_specs=(ANY, ANY, VMEM),
        scratch_shapes=[
            pltpu.VMEM(((STEPS + 1) * 8 * wide * size_y, LANES), F32),
            pltpu.VMEM((2 * wide * size_y, LANES), F32),
            pltpu.VMEM((STEPS * 2 * 3 * size_y, LANES), F32),
            pltpu.VMEM((8 * 3 * size_y, LANES), F32),
            pltpu.VMEM((2 * 3 * size_y, LANES), F32),
            pltpu.VMEM((4,) + plane, F32),
            pltpu.SMEM((1, eps_table.shape[0]), F32),
            pltpu.SMEM((1, eps_table.shape[0]), F32),
            pltpu.SMEM((1, LANES), jnp.int32),
            pltpu.SemaphoreType.DMA((12,)),
            pltpu.SemaphoreType.DMA((3,)),
        ],
        compiler_params=pltpu.CompilerParams(vmem_limit_bytes=48 * 1024 * 1024),
        name="fields",
    )(
        e_init, h_init, material, xa_in, xb_in, z_in, za_in, zb_in, zp,
        in_hbm(eps_table.reshape(1, -1)), in_hbm(sigma_table.reshape(1, -1)), in_hbm(face_cells),
    )
    e_field = e_field.reshape(e_init.shape)
    h_field = h_field.reshape(h_init.shape)

    tiles = nx * nz
    scale = 1.0 / math.sqrt(tiles * face_cells.shape[1] * STEPS)
    if not (nx == 16 and nz == 2):
        far = far_general(
            samples, face_cells[0], owner_table, material.shape, nx, nz, scale
        )
        return e_field, h_field, far

    def swap_all(v, mx, mz):
        links = [(i * nz + k, (i ^ mx) * nz + (k ^ mz)) for i in range(nx) for k in range(nz)]
        return lax.ppermute(v, both, links)

    mine = jnp.stack([samples, swap_all(samples, 1, 0)])
    by_y = swap_all(mine, 2, 0)
    by_x = swap_all(mine, 0, 1)
    by_xy = swap_all(mine, 2, 1)
    far_two, near_two = (
        pl.pallas_call(
            functools.partial(project_kernel, first, size_x, size_y, size_z, nx, nz),
            out_shape=jax.ShapeDtypeStruct((2, 12, FREQS, LANES), F32),
            in_specs=[VMEM] * 4 + [SMEM],
            out_specs=VMEM,
            scratch_shapes=[
                pltpu.SMEM((tiles,), jnp.int32),
                pltpu.VMEM((8, 8 * STEPS, LANES), F32),
                pltpu.VMEM((4, 16, 2 * LANES), BF16),
                pltpu.VMEM((2 * FREQS, 2 * LANES, 2 * LANES), BF16),
                pltpu.VMEM((2 * FREQS, 2 * LANES, 2 * LANES), BF16),
                pltpu.VMEM((4, FREQS, 128, 2 * LANES), BF16),
                pltpu.VMEM((FREQS, 64, 2 * LANES), F32),
            ],
            compiler_params=pltpu.CompilerParams(vmem_limit_bytes=32 * 1024 * 1024),
            cost_estimate=pl.CostEstimate(
                flops=1_000_000_000, bytes_accessed=8_000_000, transcendentals=0
            ),
            name="project",
        )(mine, by_y, by_x, by_xy, owner_table)
        for first in (2, 0)
    )
    near_two = near_two + swap_all(far_two, 8, 0)
    total = near_two[0] + swap_all(near_two[1], 4, 0)
    far = jnp.transpose(total * scale, (1, 0, 2))
    return e_field, h_field, far[None]


def solution(mesh):
    nx, nz = mesh.shape["gx"], mesh.shape["gz"]
    return jax.shard_map(
        functools.partial(shards, nx, nz),
        mesh=mesh,
        in_specs=(
            P(None, "gx", None, "gz"),
            P(None, "gx", None, "gz"),
            P("gx", None, "gz"),
            P(),
            P(),
            P(("gx", "gz"), None),
            P(),
        ),
        out_specs=(
            P(None, "gx", None, "gz"),
            P(None, "gx", None, "gz"),
            P(("gx", "gz"), None, None, None),
        ),
        check_vma=False,
    )
```

```python
import functools
import math

import jax
import jax.numpy as jnp
from jax import lax
from jax.experimental import pallas as pl
from jax.experimental.pallas import tpu as pltpu
from jax.sharding import PartitionSpec as P

STEPS = 4
ANGLES = 4096
NPHI = 64
FREQS = 4
DT = 0.5

W = 4
BLOCK = 40
LANES = 128
F32 = jnp.float32
BF16 = jnp.bfloat16


def roll(v, shift, axis):
    return pltpu.roll(v, shift, axis)


def iota(shape, axis):
    return lax.broadcasted_iota(jnp.int32, shape, axis)


def fold_pair(a, b, up, lane):
    own = jnp.where(up, lane, 127 - lane) >= 124
    return jnp.where(own, b, roll(a, jnp.where(up, 124, 4), 1))


def pack_kernel(ns, e_hbm, h_hbm, m_hbm, xa_ref, xb_ref, zp_ref, zd_ref, f_ref, m_ref, sem):
    size_x, size_y = m_ref.shape[0], m_ref.shape[1]
    gx, gz = lax.axis_index("gx"), lax.axis_index("gz")
    copies = [
        pltpu.make_async_copy((e_hbm if c < 3 else h_hbm).at[c % 3], f_ref.at[c], sem.at[c])
        for c in range(6)
    ]
    copies.append(pltpu.make_async_copy(m_hbm, m_ref, sem.at[6]))
    for copy in copies:
        copy.start()
    even = gx % 2 == 0
    lane = iota((size_y, LANES), 1)
    group = lane // 8

    def plane(c, x):
        return f_ref[c, x] if c < 6 else m_ref[x].astype(F32)

    for i in range(4):
        comps = (2 * i, 2 * i + 1) if i < 3 else (6, 6)
        for c in sorted(set(comps)):
            copies[c].wait()
            for ref, off in ((xa_ref, size_x - W), (xb_ref, 0)):
                off = jnp.where(even, off, size_x - W - off)
                for j in range(W):
                    ref[c * W + j] = plane(c, off + j)
        for s in range(ns):
            up = (gz + s) % 2 == 0
            base = jnp.where(up, 8, 0)

            def fold(g, acc):
                out = []
                for q in range(2):
                    x = (g + 28) % 32 if q == 0 else g + 12
                    cell = fold_pair(plane(comps[0], x), plane(comps[1], x), up, lane)
                    cell = roll(cell, (base + 8 * g) % LANES, 1)
                    out.append(jnp.where(group == g, cell, acc[q]))
                return tuple(out)

            zero = jnp.zeros((size_y, LANES), F32)
            acc = lax.fori_loop(0, 16, fold, (zero, zero), unroll=16)
            zp_ref[s, i] = acc[0]
            zp_ref[s, 4 + i] = acc[1]
            xa_ref[7 * W + 4 * s + i] = acc[0]
            zd_ref[s, i] = acc[0]


def coef_tables(eps_ref, sigma_ref, shape):
    lane = iota(shape, 1)
    eps = jnp.ones(shape, F32)
    sigma = jnp.zeros(shape, F32)
    for i in range(eps_ref.shape[1]):
        eps = jnp.where(lane == i, eps_ref[0, i], eps)
        sigma = jnp.where(lane == i, sigma_ref[0, i], sigma)
    loss = sigma * DT / (2.0 * eps)
    return (1.0 - loss) / (1.0 + loss), DT / (eps * (1.0 + loss))


def pick(table, index):
    return jnp.take_along_axis(table, index, axis=1, mode="promise_in_bounds")


def field_kernel(
    ns,
    nx,
    nz,
    e_ref,
    h_ref,
    m_ref,
    xa_ref,
    xb_ref,
    zr_ref,
    za_ref,
    zb_ref,
    zp_ref,
    eps_hbm,
    sigma_hbm,
    cells_hbm,
    eo_ref,
    ho_ref,
    so_ref,
    st_ref,
    co_ref,
    in_ref,
    sp_ref,
    sc_ref,
    qb_ref,
    eps_ref,
    sigma_ref,
    cells_ref,
    sem,
    in_sem,
):
    size_x, size_y = m_ref.shape[0], m_ref.shape[1]
    wide = size_x + 2 * W
    span = wide * size_y
    shape = (size_y, LANES)
    gx, gz = lax.axis_index("gx"), lax.axis_index("gz")
    even = gx % 2 == 0
    lower = gx > 0
    upper = gx < nx - 1
    lane = iota(shape, 1)
    row = iota(shape, 0)
    small = [
        pltpu.make_async_copy(src, dst, in_sem.at[i])
        for i, (src, dst) in enumerate(
            (
                (eps_hbm, eps_ref),
                (sigma_hbm, sigma_ref),
                (cells_hbm, cells_ref),
            )
        )
    ]
    for copy in small:
        copy.start()

    def at(t, c, x):
        return pl.ds(((t * 8 + c) * wide + x) * size_y, size_y)

    def coef_at(c, x):
        return pl.ds((c * wide + x) * size_y, size_y)

    def block(i):
        return pl.ds(i * size_y, size_y)

    pos_a = jnp.where(even, size_x + W, 0)
    pos_b = jnp.where(even, 0, size_x + W)
    ok_b = jnp.where(even, lower, upper).astype(F32)
    sides = ((xa_ref, pos_a, None), (xb_ref, pos_b, ok_b))

    def halo_plane(j, _):
        for ref, pos, _ in sides:
            for c in range(6):
                st_ref[at(0, c, pos + j)] = ref[c * W + j]
        return 0

    lax.fori_loop(0, W, halo_plane, 0, unroll=2)

    group = lane // 8
    first_half = lane % 8 < 4
    fy_keep = row < size_y - 1
    by_keep = row > 0

    def fwd_y(v):
        return jnp.where(fy_keep, roll(v, size_y - 1, 0), 0.0)

    def bwd_y(v):
        return jnp.where(by_keep, roll(v, 1, 0), 0.0)

    def fwd_z(v):
        return roll(v, 127, 1)

    def bwd_z(v):
        return roll(v, 1, 1)

    inside = [
        jnp.where(jnp.logical_and(group < W, jnp.logical_not(lower)), 0.0, 1.0),
        jnp.ones(shape, F32),
        jnp.where(jnp.logical_and(group >= W, jnp.logical_not(upper)), 0.0, 1.0),
    ]
    for s in range(ns):
        up = (gz + s) % 2 == 0
        partner = jnp.where(up, gz + 1, gz - 1)
        ok = jnp.logical_and(partner >= 0, partner < nz)
        give_e = jnp.where(jnp.logical_and(up, ok), 1.0, 0.0)
        give_h = jnp.where(jnp.logical_and(jnp.logical_not(up), ok), 1.0, 0.0)
        base = jnp.where(up, 8, 0)

        def corner(j, acc):
            g = j + jnp.where(even, 0, W)
            comps = [xb_ref[c * W + j] for c in range(7)]
            comps.append(comps[6])
            out = []
            for i in range(4):
                cell = fold_pair(comps[2 * i], comps[2 * i + 1], up, lane)
                cell = roll(cell, (base + 8 * g) % LANES, 1)
                out.append(jnp.where(group == g, cell, acc[i]))
            return tuple(out)

        zero = jnp.zeros(shape, F32)
        acc = lax.fori_loop(0, W, corner, (zero,) * 4, unroll=4)
        for i in range(4):
            qb_ref[i] = acc[i]

        def unfold(i, _):
            def whole(mine, other):
                lo = jnp.where(up, mine, other)
                hi = jnp.where(up, other, mine)
                return (
                    jnp.where(first_half, lo, hi),
                    jnp.where(first_half, roll(lo, 124, 1), roll(hi, 4, 1)),
                )

            q0 = whole(zp_ref[s, i], zr_ref[s, i])
            q1 = whole(zp_ref[s, 4 + i], zr_ref[s, 4 + i])
            qa = whole(xa_ref[7 * W + 4 * s + i], za_ref[s, i])
            qb = whole(qb_ref[i], zb_ref[s, i])
            for k in range(2):
                below = jnp.where(even, qb[k], qa[k])
                above = jnp.where(even, qa[k], qb[k])
                c = (2 * i + k) * 3
                sp_ref[block(c)] = jnp.where(group < W, below, q0[k])
                sp_ref[block(c + 1)] = q1[k]
                sp_ref[block(c + 2)] = jnp.where(group < W, q0[k], above)
            return 0

        lax.fori_loop(0, 4, unfold, 0, unroll=4)
        if s == 0:
            for copy in small:
                copy.wait()
            ca_t, cb_t = coef_tables(eps_ref, sigma_ref, shape)

            def halo_coef(j, _):
                for ref, pos, ok_side in sides:
                    index = ref[6 * W + j].astype(jnp.int32)
                    ca, cb = pick(ca_t, index), pick(cb_t, index)
                    if ok_side is not None:
                        ca, cb = ca * ok_side, cb * ok_side
                    co_ref[coef_at(0, pos + j)] = ca
                    co_ref[coef_at(1, pos + j)] = cb
                return 0

            lax.fori_loop(0, W, halo_coef, 0, unroll=4)
        for q in range(3):
            index = sp_ref[block(18 + q)].astype(jnp.int32)
            sc_ref[block(q)] = pick(ca_t, index) * inside[q]
            sc_ref[block(3 + q)] = pick(cb_t, index) * inside[q]

        def fwd_x(v):
            r = [roll(u, 120, 1) for u in v]
            return [jnp.where(lane < 120, r[0], r[1]), jnp.where(lane < 120, r[1], r[2]), r[2]]

        def bwd_x(v):
            r = [roll(u, 8, 1) for u in v]
            return [r[0], jnp.where(lane >= 8, r[1], r[0]), jnp.where(lane >= 8, r[2], r[1])]

        def each(f, *vs):
            return [f(*u) for u in zip(*vs)]

        def own_planes(t):
            for j in range(size_x // STEPS):
                x = t * (size_x // STEPS) + j
                for c in range(3):
                    st_ref[at(0, c, x + W)] = e_ref[c, x]
                    st_ref[at(0, 3 + c, x + W)] = h_ref[c, x]
                index = m_ref[x]
                co_ref[coef_at(0, x + W)] = pick(ca_t, index)
                co_ref[coef_at(1, x + W)] = pick(cb_t, index)

        def strip_step(t, _):
            ex, ey, ez, hx, hy, hz = (
                [sp_ref[block(c * 3 + q)] for q in range(3)] for c in range(6)
            )
            ca_s = [sc_ref[block(q)] for q in range(3)]
            cb_s = [sc_ref[block(3 + q)] for q in range(3)]
            dt_s = [DT * k for k in inside]
            side_e = [[v * give_e for v in ex], [v * give_e for v in ey]]
            ez_x, ey_x = fwd_x(ez), fwd_x(ey)
            hx = each(
                lambda h, z, y, d: h - d * ((fwd_y(z) - z) - (fwd_z(y) - y)), hx, ez, ey, dt_s
            )
            hy = each(
                lambda h, x, z, zx, d: h - d * ((fwd_z(x) - x) - (zx - z)), hy, ex, ez, ez_x, dt_s
            )
            hz = each(
                lambda h, y, yx, x, d: h - d * ((yx - y) - (fwd_y(x) - x)), hz, ey, ey_x, ex, dt_s
            )
            if s == 0:
                own_planes(t)
            hz_x, hy_x = bwd_x(hz), bwd_x(hy)
            ex = each(
                lambda e, z, y, a, b: a * e + b * ((z - bwd_y(z)) - (y - bwd_z(y))),
                ex, hz, hy, ca_s, cb_s,
            )
            ey = each(
                lambda e, x, z, zx, a, b: a * e + b * ((x - bwd_z(x)) - (z - zx)),
                ey, hx, hz, hz_x, ca_s, cb_s,
            )
            ez = each(
                lambda e, y, yx, x, a, b: a * e + b * ((y - yx) - (x - bwd_y(x))),
                ez, hy, hy_x, hx, ca_s, cb_s,
            )
            for c, v in enumerate((ex, ey, ez, hx, hy, hz)):
                for q in range(3):
                    sp_ref[block(c * 3 + q)] = v[q]
            for j, v in enumerate((hx, hy)):
                for q in range(3):
                    dst = block((t * 2 + j) * 3 + q)
                    add = jnp.where(lane % 8 == 4, side_e[j][q], roll(v[q] * give_h, 2, 1))
                    in_ref[dst] = add if s == 0 else in_ref[dst] + add
            return 0

        lax.fori_loop(0, STEPS, strip_step, 0, unroll=4)

    dt_lo = jnp.where(lower, DT, 0.0)
    dt_hi = jnp.where(upper, DT, 0.0)

    planes = range(BLOCK)

    def advance(t, x, carry):
        hy_p, hz_p = carry
        old = [[st_ref[at(t - 1, c, x + i)] for i in range(BLOCK + (c < 3))] for c in range(6)]
        ca = [co_ref[coef_at(0, x + i)] for i in planes]
        cb = [co_ref[coef_at(1, x + i)] for i in planes]
        ex, ey, ez, hx, hy, hz = old
        side_x, side_y = [], []
        for i in planes:
            shift = (123 - 8 * ((x + i) % 16)) % LANES
            side_x.append(roll(in_ref[block((t - 1) * 6 + (x + i) // 16)], shift, 1))
            side_y.append(roll(in_ref[block((t - 1) * 6 + 3 + (x + i) // 16)], shift, 1))
        ex_z = [jnp.where(last, side_x[i], fwd_z(ex[i])) for i in planes]
        ey_z = [jnp.where(last, side_y[i], fwd_z(ey[i])) for i in planes]
        ez_y = [fwd_y(ez[i]) for i in planes]
        ex_y = [fwd_y(ex[i]) for i in planes]
        dt = [
            jnp.where(x + i < W, dt_lo, jnp.where(x + i >= size_x + W, dt_hi, DT)) for i in planes
        ]
        hx = [hx[i] - dt[i] * ((ez_y[i] - ez[i]) - (ey_z[i] - ey[i])) for i in planes]
        hy = [hy[i] - dt[i] * ((ex_z[i] - ex[i]) - (ez[i + 1] - ez[i])) for i in planes]
        hz = [hz[i] - dt[i] * ((ey[i + 1] - ey[i]) - (ex_y[i] - ex[i])) for i in planes]
        hx_z = [jnp.where(first, side_x[i], bwd_z(hx[i])) for i in planes]
        hy_z = [jnp.where(first, side_y[i], bwd_z(hy[i])) for i in planes]
        hy_x, hz_x = [hy_p] + hy, [hz_p] + hz
        new = [
            [ca[i] * ex[i] + cb[i] * ((hz[i] - bwd_y(hz[i])) - (hy[i] - hy_z[i])) for i in planes],
            [ca[i] * ey[i] + cb[i] * ((hx[i] - hx_z[i]) - (hz[i] - hz_x[i])) for i in planes],
            [ca[i] * ez[i] + cb[i] * ((hy[i] - hy_x[i]) - (hx[i] - bwd_y(hx[i]))) for i in planes],
            hx, hy, hz,
        ]
        for c in range(6):
            for i in planes:
                st_ref[at(t, c, x + i)] = new[c][i]
        return hy[-1], hz[-1]

    last, first = lane == 127, lane == 0

    half = size_x // 2
    copies = []
    for part in range(2):
        copies.append([])
        for c in range(3):
            for ref, cc in ((eo_ref, c), (ho_ref, 3 + c)):
                src = ((STEPS * 8 + cc) * wide + W + part * half) * size_y
                copies[part].append(
                    pltpu.make_async_copy(
                        st_ref.at[pl.ds(src, half * size_y)],
                        ref.at[c, pl.ds(part * half * size_y, half * size_y)],
                        sem.at[part * 6 + cc],
                    )
                )
    blocks = wide // BLOCK
    def step(t, _):
        zero = jnp.zeros(shape, F32)

        def planes_from(i, c):
            c = advance(t, i * BLOCK, c)

            @pl.when(jnp.logical_and(t == STEPS, i == blocks // 2 - 1 + blocks % 2))
            def _():
                for copy in copies[0]:
                    copy.start()

            return c

        lax.fori_loop(0, blocks, planes_from, (zero, zero))
        return 0

    lax.fori_loop(1, STEPS + 1, step, 0, unroll=4)
    for copy in copies[1]:
        copy.start()

    rows = 6
    lane8 = iota((rows, LANES), 1)
    zero8 = jnp.zeros((rows, LANES), F32)

    def slot(m, accs):
        cell = cells_ref[0, m]
        here = lane8 == m
        found = lane8 == jnp.where(cell >= 0, m, -1)
        numbers = jnp.where(here[:2], cell.astype(F32), accs[STEPS])
        cell = jnp.maximum(cell, 0)
        out = []
        for t in range(STEPS):
            start = (t + 1) * 8 * span + W * size_y + (cell >> 7)
            v = st_ref[pl.ds(start, rows, stride=span), :]
            out.append(jnp.where(found, roll(v, (m - cell) & 127, 1), accs[t]))
        return tuple(out) + (numbers,)

    zero2 = jnp.zeros((2, LANES), F32)
    accs = lax.fori_loop(0, LANES, slot, (zero8,) * STEPS + (zero2,), unroll=64)
    for t in range(STEPS):
        so_ref[t * 8 : t * 8 + 6] = accs[t][:6]
        so_ref[t * 8 + 6 : t * 8 + 8] = accs[STEPS] if t == 0 else zero2
    for copy in copies[0] + copies[1]:
        copy.wait()


SIN_C = (3.1415926401307077, -5.167710083507896, 2.550077523214726, -0.5982912856213906, 0.07765766030763246)
COS_C = (0.9999999532476085, -4.934792830619649, 4.058411352862754, -1.3318765680819573, 0.21968961109991972)
ROUND = 12582912.0


def horner(coefs, u):
    v = u * coefs[-1] + coefs[-2]
    for k in coefs[-3::-1]:
        v = v * u + k
    return v


def sincos4(turns):
    r = turns - ((turns + ROUND) - ROUND)
    u = r * r
    half_s = horner(SIN_C, u) * r
    half_c = horner(COS_C, u)
    twice = half_s + half_s
    s = twice * half_c
    c = 1.0 - twice * half_s
    s_2, c_2 = s + s, c + c
    s2 = s_2 * c
    c2 = 1.0 - s_2 * s
    s3 = c_2 * s2 - s
    c3 = c_2 * c2 - c
    s2_2 = s2 + s2
    return (s, c), (s2, c2), (s3, c3), (s2_2 * c2, 1.0 - s2_2 * s2)


def sincos(turns):
    return sincos4(turns)[0]


def split(v):
    hi = v.astype(BF16)
    return hi, (v - hi.astype(F32)).astype(BF16)


def project_kernel(
    first, size_x, size_y, size_z, tiles_x, tiles_z, own_ref, r1_ref, r2_ref, r3_ref, owner_ref, out_ref,
    inv_ref, smp_ref, pos_ref, th_ref, tl_ref, a_ref, acc_ref,
):
    gx, gz = lax.axis_index("gx"), lax.axis_index("gz")
    tiles = tiles_x * tiles_z
    base = 0.4 / (2.0 * math.pi)
    polars = ANGLES // NPHI

    def put(b, _):
        inv_ref[owner_ref[b]] = b
        return 0

    lax.fori_loop(0, tiles, put, 0, unroll=8)
    blocks = [inv_ref[(gx ^ (4 * d)) * tiles_z + gz] for d in (first, first + 1)]

    for i, ref in enumerate((own_ref, r1_ref, r2_ref, r3_ref)):
        for core in range(2):
            smp_ref[2 * i + core] = ref[core]
    row16 = iota((16, LANES), 0)
    lane16 = iota((16, LANES), 1)
    row8 = iota((8, LANES), 0)
    lane8 = iota((8, LANES), 1)

    def split3(v):
        a = v.astype(BF16).astype(F32)
        b = (v - a).astype(BF16).astype(F32)
        return a, b, v - a - b

    block = jnp.where(lane16 < 64, blocks[0], blocks[1])
    polar = 2 * block + (lane16 % 64) // 32
    st, _ = sincos((polar.astype(F32) + 0.5) * (0.5 / polars))
    sp, cp = sincos((lane16 % 32).astype(F32) * (1.0 / NPHI))
    ux = split3(base * st * cp)
    uy = split3(base * st * sp)
    mat = jnp.zeros((16, LANES), F32)
    for k in range(9):
        src = ux[k % 3] if k < 6 else uy[k % 3]
        mat = jnp.where(row16 == k, src, mat)
    dirs = mat.astype(BF16)
    combo = 2 * jnp.where(row8 % 4 < 2, blocks[0], blocks[1]) + row8 % 2
    _, uz = sincos((combo.astype(F32) + 0.5) * (0.5 / polars))
    uz = uz * base

    def wave(f, t):
        angle = 0.4 * (f + 1) * DT * (t + 1)
        return math.cos(angle), math.sin(angle)

    def gather(pair, _):
        pos = []
        for core in range(2):
            n = 2 * pair + core
            tile_x = gx ^ (2 * (pair % 2) + core)
            tile_z = gz ^ (pair // 2)
            rows = [smp_ref[n, t * 8 : t * 8 + 8] for t in range(STEPS)]
            cell = jnp.maximum(rows[0][6:7], 0.0).astype(jnp.int32)
            pz = (cell % size_z + tile_z * size_z).astype(F32) + (0.5 - size_z * tiles_z / 2)
            zs = sincos4(uz * pz)
            lanes = slice(core * LANES, (core + 1) * LANES)
            for f in range(FREQS):
                re = sum(wave(f, t)[0] * rows[t] for t in range(STEPS))
                im = sum(wave(f, t)[1] * rows[t] for t in range(STEPS))
                zsin, zcos = zs[f]
                for k in range(4):
                    sk, ck = zsin[k : k + 1], zcos[k : k + 1]
                    both = jnp.concatenate([re * ck - im * sk, re * sk + im * ck], axis=0)
                    hi, lo = split(both)
                    a_ref[pair, f, k * 16 : k * 16 + 16, lanes] = hi
                    a_ref[pair, f, 64 + k * 16 : 80 + k * 16, lanes] = lo
            gxi = cell // (size_y * size_z) + tile_x * size_x - size_x * tiles_x // 2
            high = ((gxi >> 4) << 4).astype(F32)
            low = (gxi & 15).astype(F32) + 0.5
            py = ((cell // size_z) % size_y).astype(F32) + (0.5 - size_y / 2)
            pos.append(
                jnp.where(row16 < 3, high, jnp.where(row16 < 6, low, jnp.where(row16 < 9, py, 0.0)))
            )
        pos_ref[pair] = jnp.concatenate(pos, axis=1).astype(BF16)
        return 0

    lax.fori_loop(0, 4, gather, 0, unroll=4)

    def table(i, b):
        phase = lax.dot_general(
            pos_ref[i], dirs, (((0,), (0,)), ((), ())), preferred_element_type=F32
        )
        for j in range(8):
            dst = slice(j * 32, j * 32 + 32)
            values = sincos4(phase[dst])
            for f in range(FREQS):
                for part in range(2):
                    hi, lo = split(values[f][1 - part])
                    th_ref[b * 4 + f, dst, part * LANES : (part + 1) * LANES] = hi
                    tl_ref[b * 4 + f, dst, part * LANES : (part + 1) * LANES] = lo

    def multiply(i, b):
        for f in range(FREQS):
            a = a_ref[i, f]
            o = jnp.dot(a, th_ref[b * 4 + f], preferred_element_type=F32)
            o = o[:64] + o[64:] + jnp.dot(a[:64], tl_ref[b * 4 + f], preferred_element_type=F32)
            if i == 0:
                acc_ref[f] = o
            else:
                acc_ref[f] += o

    table(0, 0)
    for k in range(4):
        if k < 3:
            table(k + 1, (k + 1) % 2)
        multiply(k, k % 2)

    near = lane8 % 64 < 32
    sign = jnp.where(near, 1.0, -1.0)

    def finish(f, _):
        for d in range(2):
            res = []
            for pol in range(2):
                r = (d * 2 + pol) * 16
                src = d * 64 + pol * 32
                pq = []
                for part in range(2):
                    for comp in range(2):
                        v = acc_ref[
                            f, r + comp * 8 : r + comp * 8 + 8, part * LANES : (part + 1) * LANES
                        ]
                        lo_v = roll(v, (pol * 64 - src) % LANES, 1)
                        hi_v = roll(v, (pol * 64 + 32 - src) % LANES, 1)
                        pq.append(jnp.where(near, lo_v, hi_v))
                pr, pi, qr, qi = pq
                res.append((pr - sign * qi, pi + sign * qr))
            out_ref[d, 0:6, f] = jnp.where(lane8 < 64, res[0][0], res[1][0])[:6]
            out_ref[d, 6:12, f] = jnp.where(lane8 < 64, res[0][1], res[1][1])[:6]
        return 0

    lax.fori_loop(0, FREQS, finish, 0, unroll=4)


def directions(angle):
    theta = math.pi * ((angle // NPHI).astype(F32) + 0.5) / (ANGLES // NPHI)
    phi = 2.0 * math.pi * (angle % NPHI).astype(F32) / NPHI
    return (jnp.sin(theta) * jnp.cos(phi), jnp.sin(theta) * jnp.sin(phi), jnp.cos(theta))


def project(acc_re, acc_im, pos_x, pos_y, pos_z, angle, omegas):
    dir_x, dir_y, dir_z = directions(angle)
    geometry = (
        dir_x[:, None] * pos_x[None] + dir_y[:, None] * pos_y[None] + dir_z[:, None] * pos_z[None]
    )
    phase = omegas[:, None, None] * geometry[None]
    cosine = jnp.cos(phase)
    sine = jnp.sin(phase)
    high = lax.Precision.HIGHEST
    real = jnp.einsum("fas,fcs->fca", cosine, acc_re, precision=high) - jnp.einsum(
        "fas,fcs->fca", sine, acc_im, precision=high
    )
    imag = jnp.einsum("fas,fcs->fca", sine, acc_re, precision=high) + jnp.einsum(
        "fas,fcs->fca", cosine, acc_im, precision=high
    )
    return jnp.concatenate([real, imag], axis=1)


def far_general(samples, cells, owner_table, sizes, tiles_x, tiles_z, scale):
    size_x, size_y, size_z = sizes
    tiles = tiles_x * tiles_z
    sample = samples.reshape(STEPS, 8, LANES)[:, :6]
    omegas = 0.4 * (jnp.arange(FREQS, dtype=F32) + 1.0)
    phase = omegas[:, None] * (DT * (jnp.arange(STEPS, dtype=F32) + 1.0))[None]
    acc_re = jnp.sum(jnp.cos(phase)[:, :, None, None] * sample[None], axis=1)
    acc_im = jnp.sum(jnp.sin(phase)[:, :, None, None] * sample[None], axis=1)
    local = jnp.maximum(cells, 0)
    glob_x = lax.axis_index("gx") * size_x + local // (size_y * size_z)
    glob_y = local // size_z % size_y
    glob_z = lax.axis_index("gz") * size_z + local % size_z
    pos_x = glob_x.astype(F32) + (0.5 - size_x * tiles_x / 2)
    pos_y = glob_y.astype(F32) + (0.5 - size_y / 2)
    pos_z = glob_z.astype(F32) + (0.5 - size_z * tiles_z / 2)
    block_len = ANGLES // tiles
    owners = jnp.arange(tiles, dtype=jnp.int32)
    blocks = jnp.sum(jnp.where(owner_table[None, :] == owners[:, None], owners[None, :], 0), axis=1)
    angle = (blocks[:, None] * block_len + jnp.arange(block_len, dtype=jnp.int32)[None]).reshape(-1)
    pattern = project(acc_re, acc_im, pos_x, pos_y, pos_z, angle, omegas)
    pattern = jnp.transpose(pattern.reshape(FREQS, 12, tiles, block_len), (2, 0, 1, 3))
    return lax.psum_scatter(pattern, ("gx", "gz"), scatter_dimension=0, tiled=True) * scale


VMEM = pl.BlockSpec(memory_space=pltpu.VMEM)
SMEM = pl.BlockSpec(memory_space=pltpu.SMEM)
ANY = pl.BlockSpec(memory_space=pl.ANY)
HBM = pl.BlockSpec(memory_space=pltpu.HBM)


def in_hbm(v):
    return pltpu.with_memory_space_constraint(v, pltpu.HBM)


def shards(nx, nz, e_init, h_init, material, eps_table, sigma_table, face_cells, owner_table):
    size_x, size_y, size_z = material.shape
    ns = 1 if nz == 2 else 2
    plane = (size_y, size_z)
    both = ("gx", "gz")

    def pair_a(i):
        return i ^ 1

    def pair_b(i):
        return i + 1 if i % 2 else i - 1

    def pair_z(k, s):
        return k + 1 if (k + s) % 2 == 0 else k - 1

    xa, xb, zp, zd = pl.pallas_call(
        functools.partial(pack_kernel, ns),
        out_shape=(
            jax.ShapeDtypeStruct((7 * W + 4 * ns,) + plane, F32),
            jax.ShapeDtypeStruct((7 * W,) + plane, F32),
            jax.ShapeDtypeStruct((ns, 8) + plane, F32),
            jax.ShapeDtypeStruct((ns, 4) + plane, F32),
        ),
        in_specs=[ANY] * 3,
        out_specs=(VMEM,) * 4,
        scratch_shapes=[
            pltpu.VMEM((6, size_x) + plane, F32),
            pltpu.VMEM((size_x,) + plane, jnp.int32),
            pltpu.SemaphoreType.DMA((7,)),
        ],
        compiler_params=pltpu.CompilerParams(vmem_limit_bytes=16 * 1024 * 1024),
        name="pack",
    )(in_hbm(e_init), in_hbm(h_init), in_hbm(material))
    xb_in = lax.ppermute(
        xb, "gx", [(i, pair_b(i)) for i in range(nx) if 0 <= pair_b(i) < nx]
    )

    swap = [(i, pair_a(i)) for i in range(nx)]
    xa_in = lax.ppermute(xa, "gx", swap)

    def turned(v, s, pair_x):
        links = [
            (i * nz + k, pair_x(i) * nz + pair_z(k, s))
            for i in range(nx)
            for k in range(nz)
            if 0 <= pair_x(i) < nx and 0 <= pair_z(k, s) < nz
        ]
        return lax.ppermute(v, both, links)

    z_in = []
    for s in range(ns):
        links = [(k, pair_z(k, s)) for k in range(nz) if 0 <= pair_z(k, s) < nz]
        z_in.append(lax.ppermute(zp[s], "gz", links))
    z_in = jnp.stack(z_in)
    za_in = jnp.stack([turned(zd[s], s, pair_a) for s in range(ns)])
    zb_in = jnp.stack([turned(zd[s], s, pair_b) for s in range(ns)])

    wide = size_x + 2 * W
    e_field, h_field, samples = pl.pallas_call(
        functools.partial(field_kernel, ns, nx, nz),
        out_shape=(
            jax.ShapeDtypeStruct((3, size_x * size_y, size_z), F32),
            jax.ShapeDtypeStruct((3, size_x * size_y, size_z), F32),
            jax.ShapeDtypeStruct((8 * STEPS, LANES), F32),
        ),
        in_specs=[VMEM] * 9 + [HBM] * 3,
        out_specs=(ANY, ANY, VMEM),
        scratch_shapes=[
            pltpu.VMEM(((STEPS + 1) * 8 * wide * size_y, LANES), F32),
            pltpu.VMEM((2 * wide * size_y, LANES), F32),
            pltpu.VMEM((STEPS * 2 * 3 * size_y, LANES), F32),
            pltpu.VMEM((8 * 3 * size_y, LANES), F32),
            pltpu.VMEM((2 * 3 * size_y, LANES), F32),
            pltpu.VMEM((4,) + plane, F32),
            pltpu.SMEM((1, eps_table.shape[0]), F32),
            pltpu.SMEM((1, eps_table.shape[0]), F32),
            pltpu.SMEM((1, LANES), jnp.int32),
            pltpu.SemaphoreType.DMA((12,)),
            pltpu.SemaphoreType.DMA((3,)),
        ],
        compiler_params=pltpu.CompilerParams(vmem_limit_bytes=48 * 1024 * 1024),
        name="fields",
    )(
        e_init, h_init, material, xa_in, xb_in, z_in, za_in, zb_in, zp,
        in_hbm(eps_table.reshape(1, -1)), in_hbm(sigma_table.reshape(1, -1)), in_hbm(face_cells),
    )
    e_field = e_field.reshape(e_init.shape)
    h_field = h_field.reshape(h_init.shape)

    tiles = nx * nz
    scale = 1.0 / math.sqrt(tiles * face_cells.shape[1] * STEPS)
    if not (nx == 16 and nz == 2):
        far = far_general(
            samples, face_cells[0], owner_table, material.shape, nx, nz, scale
        )
        return e_field, h_field, far

    def swap_all(v, mx, mz):
        links = [(i * nz + k, (i ^ mx) * nz + (k ^ mz)) for i in range(nx) for k in range(nz)]
        return lax.ppermute(v, both, links)

    mine = jnp.stack([samples, swap_all(samples, 1, 0)])
    by_y = swap_all(mine, 2, 0)
    by_x = swap_all(mine, 0, 1)
    by_xy = swap_all(mine, 2, 1)
    far_two, near_two = (
        pl.pallas_call(
            functools.partial(project_kernel, first, size_x, size_y, size_z, nx, nz),
            out_shape=jax.ShapeDtypeStruct((2, 12, FREQS, LANES), F32),
            in_specs=[VMEM] * 4 + [SMEM],
            out_specs=VMEM,
            scratch_shapes=[
                pltpu.SMEM((tiles,), jnp.int32),
                pltpu.VMEM((8, 8 * STEPS, LANES), F32),
                pltpu.VMEM((4, 16, 2 * LANES), BF16),
                pltpu.VMEM((2 * FREQS, 2 * LANES, 2 * LANES), BF16),
                pltpu.VMEM((2 * FREQS, 2 * LANES, 2 * LANES), BF16),
                pltpu.VMEM((4, FREQS, 128, 2 * LANES), BF16),
                pltpu.VMEM((FREQS, 64, 2 * LANES), F32),
            ],
            compiler_params=pltpu.CompilerParams(vmem_limit_bytes=32 * 1024 * 1024),
            cost_estimate=pl.CostEstimate(
                flops=1_000_000_000, bytes_accessed=8_000_000, transcendentals=0
            ),
            name="project",
        )(mine, by_y, by_x, by_xy, owner_table)
        for first in (2, 0)
    )
    near_two = near_two + swap_all(far_two, 8, 0)
    total = near_two[0] + swap_all(near_two[1], 4, 0)
    far = jnp.transpose(total * scale, (1, 0, 2))
    return e_field, h_field, far[None]


def solution(mesh):
    nx, nz = mesh.shape["gx"], mesh.shape["gz"]
    return jax.shard_map(
        functools.partial(shards, nx, nz),
        mesh=mesh,
        in_specs=(
            P(None, "gx", None, "gz"),
            P(None, "gx", None, "gz"),
            P("gx", None, "gz"),
            P(),
            P(),
            P(("gx", "gz"), None),
            P(),
        ),
        out_specs=(
            P(None, "gx", None, "gz"),
            P(None, "gx", None, "gz"),
            P(("gx", "gz"), None, None, None),
        ),
        check_vma=False,
    )
```
